256 devices in a mesh: seq: 4 (over x), ctx: 64 (over z, y, core).
Axes of the slice: x: 4, y: 4, z: 8, core: 2. Of those that a mesh axis runs over, the one named last changes fastest.
Arguments:
- inputs: bfloat16 [4, 8192, 1024], P('seq', 'ctx'), may hold values from -16 to 16
- w_query: bfloat16 [1024, 1024], replicated, may hold values from -0.1875 to 0.1875
- w_key: bfloat16 [1024, 1024], replicated, as said below
- w_value: bfloat16 [1024, 1024], replicated, may hold values from -0.1875 to 0.1875
- damping: float32 [8, 128], replicated, may hold values from 0.25 to 4
- grad_out: bfloat16 [4, 8192, 1024], P('seq', 'ctx'), may hold values from -6 to 6
Outputs:
- grad_inputs: bfloat16 [4, 8192, 1024], P('seq', 'ctx')
- grad_weights: float32 [1024, 1024], P(('seq', 'ctx'))
The draws below stay inside these ranges and needn't reach their ends.
Inputs may be any that keep to these rules, and one draw needn't show every extreme that they name: `w_key`: entries scaled by a random factor per column.
All inputs are finite; a program needn't handle non-finite values.
Results may differ from the reference program's by a relative error of at most 0.013.
Values sent between devices are 32-bit elements; how exact they have to be, the bound alone decides.
No kernel may reach another device: no remote copies, remote signals or barrier semaphores. Data moves between devices by JAX's collectives and lax.ppermute only.
A program may use at most 256 MiB of HBM per device.

```python
import math
import jax
import jax.numpy as jnp
from jax import lax

D = 1024
HEADS = 8
DK = 128
ITERS = 2
TOK_DEV = 128
HD = 1024
BATCH = 4
SEQLEN = 8192


def draw_w_key(key, part):
    base_key, scale_key = jax.random.split(jax.random.fold_in(key, 17))
    column_scale = jnp.exp(jax.random.uniform(scale_key, (HEADS * DK,), jnp.float32, math.log(0.1), math.log(3.0)))
    entries = jax.random.truncated_normal(base_key, -4.0, 4.0, (D, HEADS * DK), jnp.float32)
    return (entries * column_scale[None, :] / math.sqrt(D)).astype(jnp.bfloat16)


def raised(values, rng, source, target, shards_of, factor):
    def block_of(position):
        return (jnp.arange(values.shape[position]) // (values.shape[position] // shards_of)).reshape((-1,) + (1,) * (values.ndim - 1 - position))

    one_side = jax.random.permutation(rng, shards_of)[block_of(target)]
    other_side = (block_of(target) + shards_of // 2) % shards_of
    return jnp.where((block_of(source) == one_side) | (block_of(source) == other_side), factor * values, values)


def block_scale(own_key, extent, shards, low, largest):
    gain = 1.0
    for dim, blocks in shards:
        heights = jax.random.uniform(jax.random.fold_in(jax.random.fold_in(own_key, 6), dim), (blocks,), jnp.float32, low / len(shards), largest / len(shards))
        gain = gain * jnp.repeat(jnp.exp(heights), extent[dim] // blocks).reshape((-1,) + (1,) * (len(extent) - 1 - dim))
    return gain


def noise(own_key, shape, scale, most, cuts=(), dtype=jnp.bfloat16):
    level = block_scale(own_key, shape, cuts, -0.22, 0.18) if cuts else 1.0
    values = jax.random.normal(own_key, shape, jnp.float32) * scale * level
    return jnp.minimum(jnp.maximum(values, -most), most).astype(dtype)


def gaussian_with(rng, dims, scale, most, cuts, heavy, dtype=jnp.bfloat16):
    values = scale * jax.random.normal(rng, dims, jnp.float32)
    if cuts:
        values = values * block_scale(rng, dims, cuts, -0.22, 0.18)
    return jnp.clip(raised(values, jax.random.fold_in(rng, 3), *heavy), -most, most).astype(dtype)


def setup_inputs(seed: int = 0) -> dict:
    key_of = jax.random.split(jax.random.key(seed), 7)
    return {
        "inputs": gaussian_with(key_of[0], (BATCH, SEQLEN, D), 1.0, 16.0, ((0, 4), (1, 64)), (1, 2, 64, 4.0)),
        "w_query": noise(key_of[1], (D, HD), D ** -0.5, 0.1875),
        "w_key": draw_w_key(jax.random.fold_in(key_of[6], 71), 0),
        "w_value": noise(key_of[3], (D, HD), D ** -0.5, 0.1875),
        "damping": jnp.clip(jnp.exp(jax.random.uniform(key_of[4], (HEADS, DK), jnp.float32, math.log(0.25), math.log(4.0))), 0.25, 4.0),
        "grad_out": noise(key_of[5], (BATCH, SEQLEN, HD), 1.0, 6.0, ((0, 4), (1, 64))),
    }


EPSILON = 1e-06
EXACT_PRECISION = lax.Precision.HIGHEST

def unit_rows(tensor):
    inv_norm = lax.rsqrt(lax.optimization_barrier(jnp.sum(tensor * tensor, axis=-1, keepdims=True)) + EPSILON)
    return (tensor * inv_norm, inv_norm)

def unit_back(normed, inv_norm, upstream_gradient):
    return (upstream_gradient - normed * lax.optimization_barrier(jnp.sum(normed * upstream_gradient, axis=-1, keepdims=True))) * inv_norm

def causal_mask(length):
    rows_idx = lax.broadcasted_iota(jnp.int32, (length, length), 0)
    cols_idx = lax.broadcasted_iota(jnp.int32, (length, length), 1)
    return (rows_idx >= cols_idx).astype(jnp.float32)

def apply_system(vector, key_inputs, prior_state, damping, causal):
    inner = jnp.einsum('htk,hsk->hts', vector, key_inputs, precision=EXACT_PRECISION) * causal
    result = jnp.einsum('hkj,htj->htk', prior_state, vector, precision=EXACT_PRECISION)
    result = result + jnp.einsum('hts,hsk->htk', inner, key_inputs, precision=EXACT_PRECISION)
    return result + damping[:, None, :] * vector

def conjugate(target, key_inputs, prior_state, damping, causal):
    solution = jnp.zeros_like(target)
    residual = target
    direction = target
    norm_now = lax.optimization_barrier(jnp.sum(residual * residual, axis=-1, keepdims=True))
    for sweep in range(ITERS):
        image_vec = apply_system(direction, key_inputs, prior_state, damping, causal)
        step_size = norm_now / (lax.optimization_barrier(jnp.sum(direction * image_vec, axis=-1, keepdims=True)) + EPSILON)
        solution = solution + step_size * direction
        residual = residual - step_size * image_vec
        norm_next = lax.optimization_barrier(jnp.sum(residual * residual, axis=-1, keepdims=True))
        direction = residual + norm_next / (norm_now + EPSILON) * direction
        norm_now = norm_next
    return solution

def key_states(key_inputs, value_inputs):
    gram_local = jnp.einsum('htk,htj->hkj', key_inputs, key_inputs, precision=EXACT_PRECISION)
    cross_term_local = jnp.einsum('htv,htk->hvk', value_inputs, key_inputs, precision=EXACT_PRECISION)
    return (gram_local, cross_term_local)

def value_scores(upstream_gradient, value_inputs, causal):
    return jnp.einsum('htv,hsv->hts', upstream_gradient, value_inputs, precision=EXACT_PRECISION) * causal

def solve_block(normed_q, key_inputs, value_inputs, upstream_gradient, gram_prior, cross_prior, damping, causal):
    query_solution = conjugate(normed_q, key_inputs, gram_prior, damping, causal)
    scores = value_scores(upstream_gradient, value_inputs, causal)
    adjoint_rhs = jnp.einsum('hvk,htv->htk', cross_prior, upstream_gradient, precision=EXACT_PRECISION)
    adjoint_rhs = adjoint_rhs + jnp.einsum('hts,hsk->htk', scores, key_inputs, precision=EXACT_PRECISION)
    adjoint = conjugate(adjoint_rhs, key_inputs, gram_prior, damping, causal)
    return (query_solution, adjoint, scores)

def answer_states(query_solution, adjoint, upstream_gradient):
    cross_term_local = jnp.einsum('sip,sig->spg', query_solution, upstream_gradient, precision=EXACT_PRECISION)
    gram_half = jnp.einsum('htk,htj->hkj', adjoint, query_solution, precision=EXACT_PRECISION)
    return (cross_term_local, gram_half + jnp.swapaxes(gram_half, 1, 2))

def block_grads(query_solution, adjoint, scores, key_inputs, value_inputs, upstream_gradient, cross_term_after, gram_after, causal):
    query_keys = jnp.einsum('htk,hsk->hts', query_solution, key_inputs, precision=EXACT_PRECISION) * causal
    adjoint_keys = jnp.einsum('htk,hsk->hts', adjoint, key_inputs, precision=EXACT_PRECISION) * causal
    key_gradient = jnp.einsum('zrp,zwp->zwr', cross_term_after, value_inputs, precision=EXACT_PRECISION)
    key_gradient = key_gradient + jnp.einsum('hts,htk->hsk', scores, query_solution, precision=EXACT_PRECISION)
    key_gradient = key_gradient - jnp.einsum('hkj,hsj->hsk', gram_after, key_inputs, precision=EXACT_PRECISION)
    key_gradient = key_gradient - jnp.einsum('hts,htk->hsk', query_keys, adjoint, precision=EXACT_PRECISION)
    key_gradient = key_gradient - jnp.einsum('hts,htk->hsk', adjoint_keys, query_solution, precision=EXACT_PRECISION)
    value_gradient = jnp.einsum('zgf,ztg->ztf', cross_term_after, key_inputs, precision=EXACT_PRECISION)
    value_gradient = value_gradient + jnp.einsum('hts,htv->hsv', query_keys, upstream_gradient, precision=EXACT_PRECISION)
    return (key_gradient, value_gradient)

def reference(inputs, w_query, w_key, w_value, damping, grad_out):
    local_rows = inputs.reshape(BATCH * SEQLEN, D)
    query_all = jnp.dot(local_rows, w_query, preferred_element_type=jnp.float32).astype(jnp.bfloat16)
    key_all = jnp.dot(local_rows, w_key, preferred_element_type=jnp.float32).astype(jnp.bfloat16)
    value_all = jnp.dot(local_rows, w_value, preferred_element_type=jnp.float32).astype(jnp.bfloat16)
    block_count = SEQLEN // TOK_DEV
    causal = causal_mask(TOK_DEV)

    def to_blocks(tensor):
        return tensor.astype(jnp.float32).reshape(block_count, TOK_DEV, HEADS, DK).transpose(0, 2, 1, 3)

    def from_blocks(tensor):
        return tensor.transpose(0, 2, 1, 3).reshape(SEQLEN, HEADS * DK)

    def one_sequence(pieces):
        query_blocks = to_blocks(pieces[0])
        key_blocks = to_blocks(pieces[1])
        value_blocks = to_blocks(pieces[2])
        upstream_blocks = to_blocks(pieces[3])

        def forward(carried, members):
            gram_prior, cross_prior = carried
            query_rows, key_rows, value_inputs, upstream_gradient = members
            normed_q, inv_q = unit_rows(query_rows)
            key_inputs, inv_k = unit_rows(key_rows)
            gram_local, cross_term_local = key_states(key_inputs, value_inputs)
            query_solution, adjoint, scores = solve_block(normed_q, key_inputs, value_inputs, upstream_gradient, gram_prior, cross_prior, damping, causal)
            return ((gram_prior + gram_local, cross_prior + cross_term_local), (query_solution, adjoint))
        start_state = (jnp.zeros((HEADS, DK, DK), jnp.float32), jnp.zeros((HEADS, DK, DK), jnp.float32))
        unused, solved = lax.scan(forward, start_state, (query_blocks, key_blocks, value_blocks, upstream_blocks))

        def backward(carried, members):
            cross_term_after, gram_after = carried
            query_rows, key_rows, value_inputs, upstream_gradient, query_solution, adjoint = members
            normed_q, inv_q = unit_rows(query_rows)
            key_inputs, inv_k = unit_rows(key_rows)
            scores = value_scores(upstream_gradient, value_inputs, causal)
            key_gradient, value_gradient = block_grads(query_solution, adjoint, scores, key_inputs, value_inputs, upstream_gradient, cross_term_after, gram_after, causal)
            cross_term_local, gram_local = answer_states(query_solution, adjoint, upstream_gradient)
            outputs = (unit_back(normed_q, inv_q, adjoint), unit_back(key_inputs, inv_k, key_gradient), value_gradient)
            return ((cross_term_after + cross_term_local, gram_after + gram_local), outputs)
        unused_two, grads = lax.scan(backward, start_state, (query_blocks, key_blocks, value_blocks, upstream_blocks, solved[0], solved[1]), reverse=True)
        joined = jnp.concatenate([from_blocks(grads[0]), from_blocks(grads[1]), from_blocks(grads[2])], axis=1)
        return joined.astype(jnp.bfloat16)
    shaped = (query_all.reshape(BATCH, SEQLEN, HEADS * DK), key_all.reshape(BATCH, SEQLEN, HEADS * DK), value_all.reshape(BATCH, SEQLEN, HEADS * DK), grad_out)
    head_grads = lax.map(one_sequence, shaped).reshape(BATCH * SEQLEN, 3 * HEADS * DK)
    width = HEADS * DK
    summed = jnp.dot(head_grads[:, :width], w_query.T, preferred_element_type=jnp.float32)
    summed = summed + jnp.dot(head_grads[:, width:2 * width], w_key.T, preferred_element_type=jnp.float32)
    summed = summed + jnp.dot(head_grads[:, 2 * width:], w_value.T, preferred_element_type=jnp.float32)
    grad_inputs = summed.astype(jnp.bfloat16).reshape(BATCH, SEQLEN, D)
    grad_weights = jnp.dot(local_rows.T, head_grads[:, width:2 * width], preferred_element_type=jnp.float32)
    return (grad_inputs, grad_weights)
```

```python
import functools

import jax
import jax.numpy as jnp
from jax import lax
from jax.experimental import pallas as pl
from jax.experimental.pallas import tpu as pltpu
from jax.sharding import Mesh, PartitionSpec as P


ITERS = 2
EPSILON = 1e-06
F32 = jnp.float32
BF16 = jnp.bfloat16
HEADS = 8
DK = 128
CHUNKS = 8
PLANE = ("y", "core")


def halves(x):
    hi = x.astype(BF16)
    return hi, (x - hi.astype(F32)).astype(BF16)


def nn(a, b):
    return lax.dot_general(a, b, (((1,), (0,)), ((), ())), preferred_element_type=F32)


def nt(a, b):
    return lax.dot_general(a, b, (((1,), (1,)), ((), ())), preferred_element_type=F32)


def tn(a, b):
    return lax.dot_general(a, b, (((0,), (0,)), ((), ())), preferred_element_type=F32)


def wide(x):
    return jnp.concatenate(halves(x), axis=1)


def tall(x):
    return jnp.concatenate(halves(x), axis=0)


def twice_wide(b):
    return jnp.concatenate([b, b], axis=1)


def twice_tall(b):
    return jnp.concatenate([b, b], axis=0)


def fold_cols(m):
    half = m.shape[1] // 2
    return m[:, :half] + m[:, half:]


def fold_rows(m):
    half = m.shape[0] // 2
    return m[:half] + m[half:]


def rowsum(x):
    return jnp.sum(x, axis=-1, keepdims=True)


def causal(size):
    rows = lax.broadcasted_iota(jnp.int32, (size, size), 0)
    cols = lax.broadcasted_iota(jnp.int32, (size, size), 1)
    return rows >= cols


def inv_norm(block):
    wide_block = block.astype(F32)
    return lax.rsqrt(rowsum(wide_block * wide_block) + EPSILON)


def across(column):
    size = column.shape[0]
    return jnp.transpose(jnp.broadcast_to(column, (size, size)))


def apply_all(vectors, keys, grams, scale2, damp):
    splits = [halves(p) for p in vectors]
    cats = [jnp.concatenate(s, axis=1) for s in splits]
    raw = [nt(c, twice_wide(k)) for c, k in zip(cats, keys)]
    prior = []
    for c, s, g in zip(cats, splits, grams):
        g_hi, g_lo = halves(g)
        prior.append(nn(c, twice_tall(g_hi)) + nn(s[0], g_lo))
    inner = [wide(r * m) for r, m in zip(raw, scale2)]
    return [
        o + nn(i, twice_tall(k)) + damp * p
        for o, i, k, p in zip(prior, inner, keys, vectors)
    ]


def conjugate(targets, keys, grams, scale2, damp):
    residual = list(targets)
    direction = list(targets)
    norm_now = [rowsum(r * r) for r in residual]
    solution = None
    for sweep in range(ITERS):
        image = apply_all(direction, keys, grams, scale2, damp)
        step = [n / (rowsum(p * w) + EPSILON) for n, p, w in zip(norm_now, direction, image)]
        moved = [a * p for a, p in zip(step, direction)]
        solution = moved if solution is None else [x + m for x, m in zip(solution, moved)]
        if sweep + 1 < ITERS:
            residual = [r - a * w for r, a, w in zip(residual, step, image)]
            norm_next = [rowsum(r * r) for r in residual]
            direction = [
                r + n / (o + EPSILON) * p
                for r, n, o, p in zip(residual, norm_next, norm_now, direction)
            ]
            norm_now = norm_next
    return solution


def key_kernel(slots, pos_ref, *refs):
    count = len(slots)
    pieces, (wk_ref, xb_ref, k_ref, pre_ref, tot_ref) = refs[:count], refs[count:]
    for n, (slot, start) in enumerate(slots):
        rows = pieces[n].shape[0]
        xb_ref[pos_ref[slot], start : start + rows, :] = pieces[n][...].astype(BF16)
    wk = wk_ref[...]
    running = jnp.zeros((DK, DK), F32)
    for j in range(CHUNKS):
        k = nn(xb_ref[j], wk).astype(BF16)
        k_ref[j] = k
        rk = inv_norm(k)
        pre_ref[j] = running
        running = running + fold_cols(tn(k, wide(k.astype(F32) * (rk * rk))))
    tot_ref[...] = running


def value_kernel(xb_ref, wq_ref, wv_ref, k_ref, q_ref, v_ref, pre_ref, tot_ref):
    wq, wv = wq_ref[...], wv_ref[...]
    running = jnp.zeros((DK, DK), F32)
    for j in range(CHUNKS):
        x = xb_ref[j]
        q_ref[j] = nn(x, wq).astype(BF16)
        v = nn(x, wv).astype(BF16)
        v_ref[j] = v
        k = k_ref[j]
        pre_ref[j] = running
        running = running + fold_cols(tn(v, wide(k.astype(F32) * inv_norm(k))))
    tot_ref[...] = running


def query_solve_kernel(
    q_ref, k_ref, g_ref, pre_ref, prior_ref, damp_ref, z_ref, suf_ref, tot_ref
):
    keep = causal(DK)
    keys = [k_ref[j] for j in range(CHUNKS)]
    grams = [pre_ref[j] + prior_ref[...] for j in range(CHUNKS)]
    scale2 = []
    for k in keys:
        rk = inv_norm(k)
        scale2.append(jnp.where(keep, across(rk * rk), 0.0))
    targets = [q_ref[j].astype(F32) * inv_norm(q_ref[j]) for j in range(CHUNKS)]
    z = conjugate(targets, keys, grams, scale2, damp_ref[...])
    running = jnp.zeros((DK, DK), F32)
    for j in reversed(range(CHUNKS)):
        z_ref[j] = z[j]
        suf_ref[j] = running
        running = running + fold_cols(tn(g_ref[j].astype(BF16), wide(z[j])))
    tot_ref[...] = running


def adjoint_solve_kernel(
    q_ref, k_ref, v_ref, g_ref, z_ref, gpre_ref, gprior_ref, spre_ref, sprior_ref, damp_ref,
    u_ref, dq_ref, suf_ref, tot_ref,
):
    keep = causal(DK)
    keys = [k_ref[j] for j in range(CHUNKS)]
    grams = [gpre_ref[j] + gprior_ref[...] for j in range(CHUNKS)]
    scale2, targets = [], []
    for j, k in enumerate(keys):
        rk = inv_norm(k)
        row = across(rk)
        scale2.append(jnp.where(keep, row * row, 0.0))
        g = g_ref[j].astype(BF16)
        scores = nt(g, v_ref[j]) * jnp.where(keep, row, 0.0)
        state = spre_ref[j] + sprior_ref[...]
        targets.append(nn(twice_wide(g), tall(state)) + nn(wide(scores), twice_tall(k)))
    u = conjugate(targets, keys, grams, scale2, damp_ref[...])
    running = jnp.zeros((DK, DK), F32)
    for j in reversed(range(CHUNKS)):
        u_ref[j] = u[j]
        q = q_ref[j]
        rq = inv_norm(q)
        qn = q.astype(F32) * rq
        dq_ref[j] = ((u[j] - qn * rowsum(qn * u[j])) * rq).astype(BF16).astype(F32)
        z = z_ref[j]
        suf_ref[j] = running
        left = jnp.concatenate([wide(u[j]), wide(z)], axis=0)
        right = jnp.concatenate([wide(z), wide(u[j])], axis=0)
        running = running + fold_rows(fold_cols(tn(left, right)))
    tot_ref[...] = running


def value_grad_kernel(k_ref, z_ref, g_ref, suf_ref, after_ref, dv_ref):
    keep = causal(DK)
    for j in range(CHUNKS):
        k = k_ref[j]
        rk = inv_norm(k)
        g = g_ref[j].astype(BF16)
        scores = nt(wide(z_ref[j]), twice_wide(k)) * jnp.where(keep, across(rk), 0.0)
        state = suf_ref[j] + after_ref[...]
        out = rk * nt(twice_wide(k), wide(state)) + tn(tall(scores), twice_tall(g))
        dv_ref[j] = out.astype(BF16).astype(F32)


def key_grad_kernel(
    k_ref, v_ref, g_ref, z_ref, u_ref, csuf_ref, cafter_ref, asuf_ref, aafter_ref, xb_ref,
    dk_ref, dw_ref,
):
    keep = causal(DK)
    total = jnp.zeros((xb_ref.shape[2], DK), F32)
    for j in range(CHUNKS):
        k, v = k_ref[j], v_ref[j]
        rk = inv_norm(k)
        kn = k.astype(F32) * rk
        row = jnp.where(keep, across(rk), 0.0)
        scores = jnp.where(keep, nt(g_ref[j].astype(BF16), v), 0.0)
        u, z = u_ref[j], z_ref[j]
        both = jnp.concatenate([u, z], axis=0)
        pair = nt(wide(both), twice_wide(k)) * twice_tall(row)
        left = jnp.concatenate([scores - pair[:DK], -pair[DK:]], axis=0)
        right = jnp.concatenate([z, u], axis=0)
        out = fold_rows(fold_cols(tn(wide(left), wide(right))))
        out = out + nn(twice_wide(v), tall(csuf_ref[j] + cafter_ref[...]))
        out = out - rk * nn(twice_wide(k), tall(asuf_ref[j] + aafter_ref[...]))
        dk = ((out - kn * rowsum(kn * out)) * rk).astype(BF16)
        dk_ref[j] = dk.astype(F32)
        total = total + tn(xb_ref[j], dk)
    dw_ref[...] = total


def input_grad_kernel(first_ref, second_ref, w1_ref, w2_ref, out_ref):
    def side(ref):
        return jnp.concatenate([ref[h].astype(BF16) for h in range(HEADS)], axis=1)

    out_ref[...] = nt(side(first_ref), w1_ref[...]) + nt(side(second_ref), w2_ref[...])


def input_grad_last_kernel(third_ref, w_ref, sum_ref, out_ref):
    cat = jnp.concatenate([third_ref[h].astype(BF16) for h in range(HEADS)], axis=1)
    out_ref[...] = (sum_ref[...] + nt(cat, w_ref[...])).astype(BF16)


def shaped(*dims, dtype=F32):
    return jax.ShapeDtypeStruct(dims, dtype)


VMEM = pl.BlockSpec(memory_space=pltpu.VMEM)


def call(body, outs, args, flops, smem=0, name=None):
    moved = sum(a.size * a.dtype.itemsize for a in args) + sum(
        o.size * jnp.dtype(o.dtype).itemsize for o in outs
    )
    return pl.pallas_call(
        body,
        out_shape=tuple(outs),
        in_specs=[pl.BlockSpec(memory_space=pltpu.SMEM)] * smem + [VMEM] * (len(args) - smem),
        out_specs=tuple([VMEM] * len(outs)),
        compiler_params=pltpu.CompilerParams(vmem_limit_bytes=40 << 20),
        cost_estimate=pl.CostEstimate(flops=flops, bytes_accessed=moved, transcendentals=0),
        name=name,
    )(*args)


def shift(x, axis, by, wrap):
    size = lax.axis_size(axis)
    pairs = [(i, (i + by) % size) for i in range(size) if wrap or 0 <= i + by < size]
    return lax.ppermute(x, axis, pairs)


def exclusive(total, sign):
    near = shift(total, "z", sign, False) + shift(total, "z", 2 * sign, False)
    third = total + near
    return near + (shift(third, "z", 3 * sign, False) + shift(third, "z", 6 * sign, False))


def exchange(x, axis):
    return lax.all_to_all(x, axis, 0, 0)


def gather_plane(mine):
    y, core = lax.axis_index("y"), lax.axis_index("core")
    rows = mine.shape[0] // 2
    own = mine.astype(F32)
    low, high = own[:rows], own[rows:]
    prev_low = shift(low, "y", 1, True)
    next_high = shift(high, "y", -1, True)
    prev_high = shift(high, "y", 1, True)
    next_low = shift(low, "y", -1, True)
    far_low = shift(prev_low, "y", 1, True)
    far_high = shift(next_high, "y", -1, True)
    near = [
        (prev_low, 1, 0), (next_high, 2, rows), (prev_high, 1, rows), (next_low, 2, 0),
        (far_low, 3, 0), (far_high, 3, rows),
    ]
    pieces = [(mine, 0, 0), (shift(own, "core", 1, True), 4, 0)]
    for piece, slot, start in near:
        pieces.append((piece, slot, start))
        pieces.append((shift(piece, "core", 1, True), slot + 4, start))
    ysize = lax.axis_size("y")
    places = [
        ((y + step) % ysize) * 2 + c for c in (core, 1 - core) for step in (0, -1, 1, 2)
    ]
    return pieces, jnp.stack(places).astype(jnp.int32)


def on_device(inputs, w_query, w_key, w_value, damping, grad_out):
    mine = inputs[0]
    tokens, width = mine.shape
    head = lax.axis_index("y") * 2 + lax.axis_index("core")
    cols = lambda w: lax.dynamic_slice_in_dim(w, head * DK, DK, axis=1)
    damp = lax.dynamic_slice_in_dim(damping, head, 1, axis=0)
    blocks = (CHUNKS, tokens, DK)
    state = shaped(DK, DK)
    states = shaped(CHUNKS, DK, DK)
    unit = 2 * CHUNKS * tokens * DK * DK

    pieces, places = gather_plane(mine)
    slots = tuple((slot, start) for _, slot, start in pieces)
    xb, k, gram_pre, gram_tot = call(
        functools.partial(key_kernel, slots),
        [shaped(CHUNKS, tokens, width, dtype=BF16), shaped(*blocks, dtype=BF16), states, state],
        [places] + [p for p, _, _ in pieces] + [cols(w_key)],
        unit * 10, smem=1, name="keys",
    )
    gram_prior = exclusive(gram_tot, 1)

    upstream, _ = lax.optimization_barrier((grad_out[0], gram_tot))
    upstream = upstream.astype(F32).reshape(tokens, HEADS, DK).transpose(1, 0, 2)
    g = exchange(upstream, PLANE)

    q, v, cross_pre, cross_tot = call(
        value_kernel,
        [shaped(*blocks, dtype=BF16), shaped(*blocks, dtype=BF16), states, state],
        [xb, cols(w_query), cols(w_value), k],
        unit * 18, name="values",
    )
    cross_prior = exclusive(cross_tot, 1)

    z, cross_suf, after_tot = call(
        query_solve_kernel,
        [shaped(*blocks), states, state],
        [q, k, g, gram_pre, gram_prior, damp],
        unit * 16, name="solve_query",
    )
    cross_after = exclusive(after_tot, -1)

    u, dq, gram_suf, gram_after_tot = call(
        adjoint_solve_kernel,
        [shaped(*blocks), shaped(*blocks), states, state],
        [q, k, v, g, z, gram_pre, gram_prior, cross_pre, cross_prior, damp],
        unit * 20, name="solve_adjoint",
    )
    gram_after = exclusive(gram_after_tot, -1)
    dq_all = exchange(dq, PLANE)

    (dv,) = call(
        value_grad_kernel, [shaped(*blocks)], [k, z, g, cross_suf, cross_after], unit * 6,
        name="value_grad",
    )
    dv_all = exchange(dv, PLANE)

    dk, dw = call(
        key_grad_kernel,
        [shaped(*blocks), shaped(width, DK)],
        [k, v, g, z, u, cross_suf, cross_after, gram_suf, gram_after, xb],
        unit * 20, name="key_grad",
    )
    dk_all = exchange(dk, PLANE)

    seq = lax.axis_size("seq")
    ctx = ("z", "y", "core")
    rows = width // (seq * 64)
    dw = jnp.sum(exchange(dw.reshape(seq, width // seq, DK), "seq"), axis=0)
    dw = exchange(dw.reshape(64, rows, DK), ctx).reshape(8, HEADS, rows, DK)
    grad_weights = jnp.sum(dw, axis=0).transpose(1, 0, 2).reshape(rows, HEADS * DK)

    (partial,) = call(
        input_grad_kernel, [shaped(tokens, width)], [dq_all, dv_all, w_query, w_value],
        unit * 16, name="input_grad",
    )
    (grad_inputs,) = call(
        input_grad_last_kernel, [shaped(tokens, width, dtype=BF16)], [dk_all, w_key, partial],
        unit * 8, name="input_grad_last",
    )
    return (grad_inputs[None], grad_weights)


def solution(mesh):
    grid = Mesh(mesh.devices.reshape(4, 8, 4, 2), ("seq", "z", "y", "core"))
    ctx = ("z", "y", "core")
    in_specs = (P("seq", ctx, None), P(), P(), P(), P(), P("seq", ctx, None))
    out_specs = (P("seq", ctx, None), P(("seq",) + ctx, None))
    return jax.shard_map(
        on_device, mesh=grid, in_specs=in_specs, out_specs=out_specs, check_vma=False
    )
```

```python
import functools

import jax
import jax.numpy as jnp
from jax import lax
from jax.experimental import pallas as pl
from jax.experimental.pallas import tpu as pltpu
from jax.sharding import Mesh, PartitionSpec as P


ITERS = 2
EPSILON = 1e-06
F32 = jnp.float32
BF16 = jnp.bfloat16
HEADS = 8
DK = 128
CHUNKS = 8
PLANE = ("y", "core")


def halves(x):
    hi = x.astype(BF16)
    return hi, (x - hi.astype(F32)).astype(BF16)


def nn(a, b):
    return lax.dot_general(a, b, (((1,), (0,)), ((), ())), preferred_element_type=F32)


def nt(a, b):
    return lax.dot_general(a, b, (((1,), (1,)), ((), ())), preferred_element_type=F32)


def tn(a, b):
    return lax.dot_general(a, b, (((0,), (0,)), ((), ())), preferred_element_type=F32)


def wide(x):
    return jnp.concatenate(halves(x), axis=1)


def tall(x):
    return jnp.concatenate(halves(x), axis=0)


def twice_wide(b):
    return jnp.concatenate([b, b], axis=1)


def twice_tall(b):
    return jnp.concatenate([b, b], axis=0)


def fold_cols(m):
    half = m.shape[1] // 2
    return m[:, :half] + m[:, half:]


def fold_rows(m):
    half = m.shape[0] // 2
    return m[:half] + m[half:]


def rowsum(x):
    return jnp.sum(x, axis=-1, keepdims=True)


def causal(size):
    rows = lax.broadcasted_iota(jnp.int32, (size, size), 0)
    cols = lax.broadcasted_iota(jnp.int32, (size, size), 1)
    return rows >= cols


def inv_norm(block):
    wide_block = block.astype(F32)
    return lax.rsqrt(rowsum(wide_block * wide_block) + EPSILON)


def across(column):
    size = column.shape[0]
    return jnp.transpose(jnp.broadcast_to(column, (size, size)))


def apply_all(vectors, keys, grams, scale2, damp):
    splits = [halves(p) for p in vectors]
    cats = [jnp.concatenate(s, axis=1) for s in splits]
    raw = [nt(c, twice_wide(k)) for c, k in zip(cats, keys)]
    prior = []
    for c, s, g in zip(cats, splits, grams):
        g_hi, g_lo = halves(g)
        prior.append(nn(c, twice_tall(g_hi)) + nn(s[0], g_lo))
    inner = [wide(r * m) for r, m in zip(raw, scale2)]
    return [
        o + nn(i, twice_tall(k)) + damp * p
        for o, i, k, p in zip(prior, inner, keys, vectors)
    ]


def conjugate(targets, keys, grams, scale2, damp):
    residual = list(targets)
    direction = list(targets)
    norm_now = [rowsum(r * r) for r in residual]
    solution = None
    for sweep in range(ITERS):
        image = apply_all(direction, keys, grams, scale2, damp)
        step = [n / (rowsum(p * w) + EPSILON) for n, p, w in zip(norm_now, direction, image)]
        moved = [a * p for a, p in zip(step, direction)]
        solution = moved if solution is None else [x + m for x, m in zip(solution, moved)]
        if sweep + 1 < ITERS:
            residual = [r - a * w for r, a, w in zip(residual, step, image)]
            norm_next = [rowsum(r * r) for r in residual]
            direction = [
                r + n / (o + EPSILON) * p
                for r, n, o, p in zip(residual, norm_next, norm_now, direction)
            ]
            norm_now = norm_next
    return solution


def staged(body, counts, tables, *refs):
    n_in, n_out = counts
    sources, refs = refs[:n_in], refs[n_in:]
    targets, refs = refs[:n_out], refs[n_out:]
    held, refs = refs[:n_in], refs[n_in:]
    made, (in_sems, out_sems, *rest) = refs[:n_out], refs[n_out:]
    loads = [
        pltpu.make_async_copy(s, h, in_sems.at[n]) for n, (s, h) in enumerate(zip(sources, held))
    ]
    stores = [
        pltpu.make_async_copy(m, t, out_sems.at[n]) for n, (m, t) in enumerate(zip(made, targets))
    ]
    for load in loads:
        load.start()
    arrived, sent = set(), set()

    def need(n):
        if n not in arrived:
            arrived.add(n)
            loads[n].wait()
        return held[n]

    def put(n):
        sent.add(n)
        stores[n].start()

    body(tables, need, made, put, *rest)
    for n in range(n_in):
        need(n)
    for n in range(n_out):
        if n not in sent:
            put(n)
    for store in stores:
        store.wait()


def shaped(*dims, dtype=F32):
    return jax.ShapeDtypeStruct(dims, dtype)


def call(body, outs, args, flops, name, tables=(), raw=(), scratch=()):
    def kernel(*refs):
        t, r = len(tables), len(raw)
        operands = refs[t + r :]
        staged(
            functools.partial(body, *refs[t : t + r]), (len(args), len(outs)), refs[:t], *operands
        )

    moved = sum(a.size * a.dtype.itemsize for a in args) + sum(
        o.size * jnp.dtype(o.dtype).itemsize for o in outs
    )
    anywhere = pl.BlockSpec(memory_space=pl.ANY)
    return pl.pallas_call(
        kernel,
        out_shape=tuple(outs),
        in_specs=[pl.BlockSpec(memory_space=pltpu.SMEM)] * len(tables)
        + [anywhere] * (len(raw) + len(args)),
        out_specs=tuple([anywhere] * len(outs)),
        scratch_shapes=[pltpu.VMEM(a.shape, a.dtype) for a in args]
        + [pltpu.VMEM(o.shape, o.dtype) for o in outs]
        + [pltpu.SemaphoreType.DMA((len(args),)), pltpu.SemaphoreType.DMA((len(outs),))]
        + list(scratch),
        compiler_params=pltpu.CompilerParams(vmem_limit_bytes=60 << 20),
        cost_estimate=pl.CostEstimate(flops=flops, bytes_accessed=moved, transcendentals=0),
        name=name,
    )(*tables, *raw, *args)


def prepare_body(tables, need, made, put):
    x, (low, high, upstream) = need(0), made
    rows = low.shape[0]
    low[...] = x[:rows].astype(F32)
    put(0)
    high[...] = x[rows:].astype(F32)
    put(1)
    g = need(1)
    for h in range(HEADS):
        upstream[h] = g[:, h * DK : (h + 1) * DK].astype(F32)


def project_body(slots, wq_hbm, wk_hbm, wv_hbm, tables, need, made, put, w_buf, w_sem):
    (where,) = tables
    xb, q_out, k_out, v_out, gram_out, cross_out, tot = made
    cols = pl.ds(pl.multiple_of(where[len(where) - 1] * DK, DK), DK)
    weights = [
        pltpu.make_async_copy(w.at[:, cols], w_buf.at[n], w_sem.at[n])
        for n, w in enumerate((wq_hbm, wk_hbm, wv_hbm))
    ]
    for copy in weights:
        copy.start()
    for n, (slot, start) in enumerate(slots):
        piece = need(n)
        row = pl.multiple_of(where[slot] * DK + start, DK // 2)
        xb[pl.ds(row, piece.shape[0]), :] = piece[...].astype(BF16)
    put(0)
    for copy in weights:
        copy.wait()
    wq, wk, wv = w_buf[0], w_buf[1], w_buf[2]
    gram = jnp.zeros((DK, DK), F32)
    cross = jnp.zeros((DK, DK), F32)
    for j in range(CHUNKS):
        x = xb[j * DK : (j + 1) * DK, :]
        k = nn(x, wk).astype(BF16)
        v = nn(x, wv).astype(BF16)
        k_out[j] = k
        v_out[j] = v
        rk = inv_norm(k)
        kn = k.astype(F32) * rk
        gram_out[j] = gram
        cross_out[j] = cross
        gram = gram + fold_cols(tn(k, wide(kn * rk)))
        cross = cross + fold_cols(tn(v, wide(kn)))
    tot[0] = gram
    tot[1] = cross
    put(6)
    for n in (2, 3, 4, 5):
        put(n)
    for j in range(CHUNKS):
        q_out[j] = nn(xb[j * DK : (j + 1) * DK, :], wq).astype(BF16)


def total_of(need, first):
    near = [need(first + n) for n in range(4)]
    return [(near[0][i] + near[1][i]) + (near[2][i] + near[3][i]) for i in range(2)]


def solve_body(tables, need, made, put):
    (where,) = tables
    q_in, k_in, v_in, gram_in, cross_in, damp_in, g_in = [need(n) for n in range(7)]
    gram_prior, cross_prior = total_of(need, 7)
    z_out, u_out, dq_out, suf, tot = made
    damp = damp_in[pl.ds(where[len(where) - 1], 1), :]
    keep = causal(DK)
    keys = [k_in[j] for j in range(CHUNKS)]
    grams = [gram_in[j] + gram_prior for j in range(CHUNKS)]
    scale2, targets = [], []
    for j, k in enumerate(keys):
        row = jnp.where(keep, across(inv_norm(k)), 0.0)
        scale2.append(twice_tall(row * row))
        g = g_in[j].astype(BF16)
        scores = nt(g, v_in[j]) * row
        state = cross_in[j] + cross_prior
        right = nn(twice_wide(g), tall(state)) + nn(wide(scores), twice_tall(k))
        qn = q_in[j].astype(F32) * inv_norm(q_in[j])
        targets.append(jnp.concatenate([qn, right], axis=0))
    both = conjugate(targets, keys, grams, scale2, damp)
    gram = jnp.zeros((DK, DK), F32)
    cross = jnp.zeros((DK, DK), F32)
    for j in reversed(range(CHUNKS)):
        z, u = both[j][:DK], both[j][DK:]
        z_out[j] = z
        u_out[j] = u
        suf[0, j] = gram
        suf[1, j] = cross
        left = jnp.concatenate([wide(u), wide(z)], axis=0)
        right = jnp.concatenate([wide(z), wide(u)], axis=0)
        gram = gram + fold_rows(fold_cols(tn(left, right)))
        cross = cross + fold_cols(tn(g_in[j].astype(BF16), wide(z)))
    tot[0] = gram
    tot[1] = cross
    put(4)
    for n in (0, 1, 3):
        put(n)
    for j in range(CHUNKS):
        q = q_in[j]
        rq = inv_norm(q)
        qn = q.astype(F32) * rq
        u = u_out[j]
        dq_out[j] = ((u - qn * rowsum(qn * u)) * rq).astype(BF16).astype(F32)


def grads_body(seq, tables, need, made, put, dk_buf, dw_buf):
    (place,) = tables
    k_in, v_in, z_in, u_in, suf, g_in = [need(n) for n in range(6)]
    gram_after, cross_after = total_of(need, 6)
    out = made[seq]
    keep = causal(DK)
    for j in range(CHUNKS):
        k, v = k_in[j], v_in[j]
        rk = inv_norm(k)
        kn = k.astype(F32) * rk
        row = jnp.where(keep, across(rk), 0.0)
        g = g_in[j].astype(BF16)
        scores = jnp.where(keep, nt(g, v), 0.0)
        u, z = u_in[j], z_in[j]
        both = jnp.concatenate([u, z], axis=0)
        pair = nt(wide(both), twice_wide(k)) * twice_tall(row)
        left = jnp.concatenate([scores - pair[:DK], -pair[DK:]], axis=0)
        right = jnp.concatenate([z, u], axis=0)
        kk = twice_wide(k)
        cross = suf[1, j] + cross_after
        dkn = fold_rows(fold_cols(tn(wide(left), wide(right))))
        dkn = dkn + nn(twice_wide(v), tall(cross))
        dkn = dkn - rk * nn(kk, tall(suf[0, j] + gram_after))
        dk = ((dkn - kn * rowsum(kn * dkn)) * rk).astype(BF16)
        dk_buf[j * DK : (j + 1) * DK, :] = dk
        out[j, :DK] = dk.astype(F32)
        dv = rk * nt(kk, wide(cross)) + tn(tall(pair[DK:]), twice_tall(g))
        out[j, DK:] = dv.astype(BF16).astype(F32)
    put(seq)
    dw_buf[...] = jnp.transpose(tn(dk_buf[...], need(10)[...]))
    rows = made[0].shape[0]
    for step in range(seq):
        start = pl.multiple_of(lax.rem(place[0] + step, seq) * rows, rows)
        made[step][...] = dw_buf[pl.ds(start, rows), :]
        put(step)


def input_grad_body(tables, need, made, put):
    def side(n, rows):
        return jnp.concatenate([need(n)[h, rows].astype(BF16) for h in range(HEADS)], axis=1)

    total = nt(side(0, slice(0, DK)), need(2)[...])
    total = total + nt(side(1, slice(0, DK)), need(3)[...])
    total = total + nt(side(1, slice(DK, 2 * DK)), need(4)[...])
    made[0][...] = total.astype(BF16)


def shift(x, axis, by, wrap):
    size = lax.axis_size(axis)
    pairs = [(i, (i + by) % size) for i in range(size) if wrap or 0 <= i + by < size]
    return lax.ppermute(x, axis, pairs)


def exclusive(total, sign):
    one, two = shift(total, "z", sign, False), shift(total, "z", 2 * sign, False)
    third = total + one + two
    return one, two, shift(third, "z", 3 * sign, False), shift(third, "z", 6 * sign, False)


def exchange(x, axis):
    return lax.all_to_all(x, axis, 0, 0)


def gather_plane(low, high):
    y, core = lax.axis_index("y"), lax.axis_index("core")
    rows = low.shape[0]
    prev_low = shift(low, "y", 1, True)
    next_high = shift(high, "y", -1, True)
    prev_high = shift(high, "y", 1, True)
    next_low = shift(low, "y", -1, True)
    far_low = shift(prev_low, "y", 1, True)
    far_high = shift(next_high, "y", -1, True)
    pieces = [(low, 0, 0), (high, 0, rows)]
    pieces += [(shift(low, "core", 1, True), 4, 0), (shift(high, "core", 1, True), 4, rows)]
    for piece, slot, start in (
        (prev_low, 1, 0), (next_high, 2, rows), (prev_high, 1, rows), (next_low, 2, 0),
        (far_low, 3, 0), (far_high, 3, rows),
    ):
        pieces.append((piece, slot, start))
        pieces.append((shift(piece, "core", 1, True), slot + 4, start))
    ysize = lax.axis_size("y")
    places = [
        ((y + step) % ysize) * 2 + c for c in (core, 1 - core) for step in (0, -1, 1, 2)
    ] + [y * 2 + core]
    return pieces, jnp.stack(places).astype(jnp.int32)


def on_device(inputs, w_query, w_key, w_value, damping, grad_out):
    mine = inputs[0]
    tokens, width = mine.shape
    blocks = shaped(CHUNKS, tokens, DK)
    brick = shaped(CHUNKS, tokens, DK, dtype=BF16)
    pair = shaped(2, DK, DK)
    states = shaped(CHUNKS, DK, DK)
    unit = 2 * CHUNKS * tokens * DK * DK

    half = shaped(tokens // 2, width)
    low, high, upstream = call(
        prepare_body, [half, half, shaped(HEADS, tokens, DK)], [mine, grad_out[0]], 0, "prepare"
    )
    pieces, where = gather_plane(low, high)
    slots = tuple((slot, start) for _, slot, start in pieces)
    xb, q, k, v, gram_pre, cross_pre, first_tot = call(
        functools.partial(project_body, slots),
        [shaped(CHUNKS * tokens, width, dtype=BF16), brick, brick, brick, states, states, pair],
        [p for p, _, _ in pieces],
        unit * 28, "project",
        tables=[where], raw=[w_query, w_key, w_value],
        scratch=[pltpu.VMEM((3, width, DK), BF16), pltpu.SemaphoreType.DMA((3,))],
    )
    prior = exclusive(first_tot, 1)
    upstream, _ = lax.optimization_barrier((upstream, first_tot))
    g = exchange(upstream, PLANE)

    z, u, dq, suf, second_tot = call(
        solve_body, [blocks, blocks, blocks, shaped(2, CHUNKS, DK, DK), pair],
        [q, k, v, gram_pre, cross_pre, damping, g, *prior], unit * 40, "solve", tables=[where],
    )
    after = exclusive(second_tot, -1)
    dq_all = exchange(dq, PLANE)

    seq = lax.axis_size("seq")
    ctx = ("z", "y", "core")
    spread = lax.axis_size(ctx)
    rows = width // (seq * spread)
    place = lax.axis_index("seq").astype(jnp.int32).reshape(1)
    *dw, dkv = call(
        functools.partial(grads_body, seq),
        [shaped(width // seq, DK)] * seq + [shaped(CHUNKS, 2 * tokens, DK)],
        [k, v, z, u, suf, g, *after, xb], unit * 30, "grads", tables=[place],
        scratch=[pltpu.VMEM((CHUNKS * tokens, DK), BF16), pltpu.VMEM((width, DK), F32)],
    )
    dw = sum((shift(part, "seq", step, True) for step, part in enumerate(dw) if step), dw[0])
    dkv_all = exchange(dkv, PLANE)
    dw = exchange(dw.reshape(spread, rows, DK), ctx)
    dw = dw.reshape(spread // HEADS, HEADS, rows, DK)
    grad_weights = jnp.sum(dw, axis=0).transpose(1, 0, 2).reshape(rows, HEADS * DK)

    (grad_inputs,) = call(
        input_grad_body, [shaped(tokens, width, dtype=BF16)],
        [dq_all, dkv_all, w_query, w_key, w_value], unit * 24, "input_grad",
    )
    return (grad_inputs[None], grad_weights)


def solution(mesh):
    grid = Mesh(mesh.devices.reshape(4, 8, 4, 2), ("seq", "z", "y", "core"))
    ctx = ("z", "y", "core")
    in_specs = (P("seq", ctx, None), P(), P(), P(), P(), P("seq", ctx, None))
    out_specs = (P("seq", ctx, None), P(("seq",) + ctx, None))
    return jax.shard_map(
        on_device, mesh=grid, in_specs=in_specs, out_specs=out_specs, check_vma=False
    )
```

```python
import functools

import jax
import jax.numpy as jnp
from jax import lax
from jax.experimental import pallas as pl
from jax.experimental.pallas import tpu as pltpu
from jax.sharding import Mesh, PartitionSpec as P


ITERS = 2
EPSILON = 1e-06
F32 = jnp.float32
BF16 = jnp.bfloat16
HEADS = 8
DK = 128
CHUNKS = 8
PLANE = ("y", "core")


def halves(x):
    hi = x.astype(BF16)
    return hi, (x - hi.astype(F32)).astype(BF16)


def nn(a, b):
    return lax.dot_general(a, b, (((1,), (0,)), ((), ())), preferred_element_type=F32)


def nt(a, b):
    return lax.dot_general(a, b, (((1,), (1,)), ((), ())), preferred_element_type=F32)


def tn(a, b):
    return lax.dot_general(a, b, (((0,), (0,)), ((), ())), preferred_element_type=F32)


def wide(x):
    return jnp.concatenate(halves(x), axis=1)


def tall(x):
    return jnp.concatenate(halves(x), axis=0)


def twice_wide(b):
    return jnp.concatenate([b, b], axis=1)


def twice_tall(b):
    return jnp.concatenate([b, b], axis=0)


def fold_cols(m):
    half = m.shape[1] // 2
    return m[:, :half] + m[:, half:]


def fold_rows(m):
    half = m.shape[0] // 2
    return m[:half] + m[half:]


def rowsum(x):
    return jnp.sum(x, axis=-1, keepdims=True)


def causal(size):
    rows = lax.broadcasted_iota(jnp.int32, (size, size), 0)
    cols = lax.broadcasted_iota(jnp.int32, (size, size), 1)
    return rows >= cols


def inv_norm(block):
    wide_block = block.astype(F32)
    return lax.rsqrt(rowsum(wide_block * wide_block) + EPSILON)


def across(column):
    size = column.shape[0]
    return jnp.transpose(jnp.broadcast_to(column, (size, size)))


def apply_all(vectors, keys, grams, scale2, damp):
    splits = [halves(p) for p in vectors]
    cats = [jnp.concatenate(s, axis=1) for s in splits]
    raw = [nt(c, twice_wide(k)) for c, k in zip(cats, keys)]
    prior = []
    for c, s, g in zip(cats, splits, grams):
        g_hi, g_lo = halves(g)
        prior.append(nn(c, twice_tall(g_hi)) + nn(s[0], g_lo))
    inner = [wide(r * m) for r, m in zip(raw, scale2)]
    return [
        o + nn(i, twice_tall(k)) + damp * p
        for o, i, k, p in zip(prior, inner, keys, vectors)
    ]


def conjugate(targets, keys, grams, scale2, damp):
    residual = list(targets)
    direction = list(targets)
    norm_now = [rowsum(r * r) for r in residual]
    solution = None
    for sweep in range(ITERS):
        image = apply_all(direction, keys, grams, scale2, damp)
        step = [n / (rowsum(p * w) + EPSILON) for n, p, w in zip(norm_now, direction, image)]
        moved = [a * p for a, p in zip(step, direction)]
        solution = moved if solution is None else [x + m for x, m in zip(solution, moved)]
        if sweep + 1 < ITERS:
            residual = [r - a * w for r, a, w in zip(residual, step, image)]
            norm_next = [rowsum(r * r) for r in residual]
            direction = [
                r + n / (o + EPSILON) * p
                for r, n, o, p in zip(residual, norm_next, norm_now, direction)
            ]
            norm_now = norm_next
    return solution


def staged(body, counts, tables, *refs):
    n_in, n_out = counts
    sources, refs = refs[:n_in], refs[n_in:]
    targets, refs = refs[:n_out], refs[n_out:]
    held, refs = refs[:n_in], refs[n_in:]
    made, (in_sems, out_sems, *rest) = refs[:n_out], refs[n_out:]
    loads = [
        pltpu.make_async_copy(s, h, in_sems.at[n]) for n, (s, h) in enumerate(zip(sources, held))
    ]
    stores = [
        pltpu.make_async_copy(m, t, out_sems.at[n]) for n, (m, t) in enumerate(zip(made, targets))
    ]
    for load in loads:
        load.start()
    arrived, sent = set(), set()

    def need(n):
        if n not in arrived:
            arrived.add(n)
            loads[n].wait()
        return held[n]

    def put(n):
        sent.add(n)
        stores[n].start()

    body(tables, need, made, put, *rest)
    for n in range(n_in):
        need(n)
    for n in range(n_out):
        if n not in sent:
            put(n)
    for store in stores:
        store.wait()


def shaped(*dims, dtype=F32):
    return jax.ShapeDtypeStruct(dims, dtype)


def call(body, outs, args, flops, tables=(), raw=(), scratch=()):
    def kernel(*refs):
        t, r = len(tables), len(raw)
        operands = refs[t + r :]
        staged(
            functools.partial(body, *refs[t : t + r]), (len(args), len(outs)), refs[:t], *operands
        )

    moved = sum(a.size * a.dtype.itemsize for a in args) + sum(
        o.size * jnp.dtype(o.dtype).itemsize for o in outs
    )
    anywhere = pl.BlockSpec(memory_space=pl.ANY)
    return pl.pallas_call(
        kernel,
        out_shape=tuple(outs),
        in_specs=[pl.BlockSpec(memory_space=pltpu.SMEM)] * len(tables)
        + [anywhere] * (len(raw) + len(args)),
        out_specs=tuple([anywhere] * len(outs)),
        scratch_shapes=[pltpu.VMEM(a.shape, a.dtype) for a in args]
        + [pltpu.VMEM(o.shape, o.dtype) for o in outs]
        + [pltpu.SemaphoreType.DMA((len(args),)), pltpu.SemaphoreType.DMA((len(outs),))]
        + list(scratch),
        compiler_params=pltpu.CompilerParams(vmem_limit_bytes=60 << 20),
        cost_estimate=pl.CostEstimate(flops=flops, bytes_accessed=moved, transcendentals=0),
    )(*tables, *raw, *args)


def prepare_body(tables, need, made, put):
    x, (low, high, upstream) = need(0), made
    rows = low.shape[0]
    low[...] = x[:rows].astype(F32)
    put(0)
    high[...] = x[rows:].astype(F32)
    put(1)
    g = need(1)
    for h in range(HEADS):
        upstream[h] = g[:, h * DK : (h + 1) * DK].astype(F32)


def project_body(slots, wq_hbm, wk_hbm, wv_hbm, tables, need, made, put, w_buf, w_sem):
    (where,) = tables
    xb, q_out, k_out, v_out, gram_out, cross_out, tot = made
    cols = pl.ds(pl.multiple_of(where[len(where) - 1] * DK, DK), DK)
    weights = [
        pltpu.make_async_copy(w.at[:, cols], w_buf.at[n], w_sem.at[n])
        for n, w in enumerate((wq_hbm, wk_hbm, wv_hbm))
    ]
    for copy in weights:
        copy.start()
    for n, (slot, start) in enumerate(slots):
        piece = need(n)
        row = pl.multiple_of(where[slot] * DK + start, DK // 2)
        xb[pl.ds(row, piece.shape[0]), :] = piece[...].astype(BF16)
    put(0)
    for copy in weights:
        copy.wait()
    wq, wk, wv = w_buf[0], w_buf[1], w_buf[2]
    gram = jnp.zeros((DK, DK), F32)
    cross = jnp.zeros((DK, DK), F32)
    for j in range(CHUNKS):
        x = xb[j * DK : (j + 1) * DK, :]
        k = nn(x, wk).astype(BF16)
        v = nn(x, wv).astype(BF16)
        k_out[j] = k
        v_out[j] = v
        rk = inv_norm(k)
        kn = k.astype(F32) * rk
        gram_out[j] = gram
        cross_out[j] = cross
        gram = gram + fold_cols(tn(k, wide(kn * rk)))
        cross = cross + fold_cols(tn(v, wide(kn)))
    tot[0] = gram
    tot[1] = cross
    put(6)
    for n in (2, 3, 4, 5):
        put(n)
    for j in range(CHUNKS):
        q_out[j] = nn(xb[j * DK : (j + 1) * DK, :], wq).astype(BF16)


def total_of(need, first):
    near = [need(first + n) for n in range(4)]
    return [(near[0][i] + near[1][i]) + (near[2][i] + near[3][i]) for i in range(2)]


def solve_body(tables, need, made, put):
    (where,) = tables
    q_in, k_in, v_in, gram_in, cross_in, damp_in, g_in = [need(n) for n in range(7)]
    gram_prior, cross_prior = total_of(need, 7)
    z_out, u_out, dq_out, suf, tot = made
    damp = damp_in[pl.ds(where[len(where) - 1], 1), :]
    keep = causal(DK)
    keys = [k_in[j] for j in range(CHUNKS)]
    grams = [gram_in[j] + gram_prior for j in range(CHUNKS)]
    scale2, targets = [], []
    for j, k in enumerate(keys):
        row = jnp.where(keep, across(inv_norm(k)), 0.0)
        scale2.append(twice_tall(row * row))
        g = g_in[j].astype(BF16)
        scores = nt(g, v_in[j]) * row
        state = cross_in[j] + cross_prior
        right = nn(twice_wide(g), tall(state)) + nn(wide(scores), twice_tall(k))
        qn = q_in[j].astype(F32) * inv_norm(q_in[j])
        targets.append(jnp.concatenate([qn, right], axis=0))
    both = conjugate(targets, keys, grams, scale2, damp)
    gram = jnp.zeros((DK, DK), F32)
    cross = jnp.zeros((DK, DK), F32)
    for j in reversed(range(CHUNKS)):
        z, u = both[j][:DK], both[j][DK:]
        z_out[j] = z
        u_out[j] = u
        suf[0, j] = gram
        suf[1, j] = cross
        left = jnp.concatenate([wide(u), wide(z)], axis=0)
        right = jnp.concatenate([wide(z), wide(u)], axis=0)
        gram = gram + fold_rows(fold_cols(tn(left, right)))
        cross = cross + fold_cols(tn(g_in[j].astype(BF16), wide(z)))
    tot[0] = gram
    tot[1] = cross
    put(4)
    for n in (0, 1, 3):
        put(n)
    for j in range(CHUNKS):
        q = q_in[j]
        rq = inv_norm(q)
        qn = q.astype(F32) * rq
        u = u_out[j]
        dq_out[j] = ((u - qn * rowsum(qn * u)) * rq).astype(BF16).astype(F32)


def grads_body(seq, tables, need, made, put, dk_buf, dw_buf, out):
    (place,) = tables
    k_in, v_in, z_in, u_in, suf, g_in = [need(n) for n in range(6)]
    gram_after, cross_after = total_of(need, 6)
    keep = causal(DK)
    for j in range(CHUNKS):
        k, v = k_in[j], v_in[j]
        rk = inv_norm(k)
        kn = k.astype(F32) * rk
        row = jnp.where(keep, across(rk), 0.0)
        g = g_in[j].astype(BF16)
        scores = jnp.where(keep, nt(g, v), 0.0)
        u, z = u_in[j], z_in[j]
        both = jnp.concatenate([u, z], axis=0)
        pair = nt(wide(both), twice_wide(k)) * twice_tall(row)
        left = jnp.concatenate([scores - pair[:DK], -pair[DK:]], axis=0)
        right = jnp.concatenate([z, u], axis=0)
        kk = twice_wide(k)
        cross = suf[1, j] + cross_after
        dkn = fold_rows(fold_cols(tn(wide(left), wide(right))))
        dkn = dkn + nn(twice_wide(v), tall(cross))
        dkn = dkn - rk * nn(kk, tall(suf[0, j] + gram_after))
        dk = ((dkn - kn * rowsum(kn * dkn)) * rk).astype(BF16)
        dk_buf[j * DK : (j + 1) * DK, :] = dk
        out[j, :DK] = dk.astype(F32)
        dv = rk * nt(kk, wide(cross)) + tn(tall(pair[DK:]), twice_tall(g))
        out[j, DK:] = dv.astype(BF16).astype(F32)
    for step in range(CHUNKS):
        made[seq + step][...] = out[lax.rem(place[1] + step, CHUNKS)]
        put(seq + step)
    dw_buf[...] = jnp.transpose(tn(dk_buf[...], need(10)[...]))
    rows = made[0].shape[0]
    for step in range(seq):
        start = pl.multiple_of(lax.rem(place[0] + step, seq) * rows, rows)
        made[step][...] = dw_buf[pl.ds(start, rows), :]
        put(step)


def input_grad_body(tables, need, made, put, dk_cat, dv_cat):
    (place,) = tables
    dq_cat = jnp.concatenate([need(0)[h].astype(BF16) for h in range(HEADS)], axis=1)
    total = nt(dq_cat, need(1)[...])
    for step in range(HEADS):
        piece = need(4 + step)
        head = lax.rem(place[1] + HEADS - step, HEADS)
        cols = pl.ds(pl.multiple_of(head * DK, DK), DK)
        dk_cat[:, cols] = piece[:DK].astype(BF16)
        dv_cat[:, cols] = piece[DK:].astype(BF16)
    total = total + nt(dk_cat[...], need(2)[...])
    total = total + nt(dv_cat[...], need(3)[...])
    made[0][...] = total.astype(BF16)


def shift(x, axis, by, wrap):
    size = lax.axis_size(axis)
    pairs = [(i, (i + by) % size) for i in range(size) if wrap or 0 <= i + by < size]
    return lax.ppermute(x, axis, pairs)


def exclusive(total, sign):
    one, two = shift(total, "z", sign, False), shift(total, "z", 2 * sign, False)
    third = total + one + two
    return one, two, shift(third, "z", 3 * sign, False), shift(third, "z", 6 * sign, False)


def exchange(x, axis):
    return lax.all_to_all(x, axis, 0, 0)


def gather_plane(low, high):
    y, core = lax.axis_index("y"), lax.axis_index("core")
    rows = low.shape[0]
    prev_low = shift(low, "y", 1, True)
    next_high = shift(high, "y", -1, True)
    prev_high = shift(high, "y", 1, True)
    next_low = shift(low, "y", -1, True)
    far_low = shift(prev_low, "y", 1, True)
    far_high = shift(next_high, "y", -1, True)
    pieces = [(low, 0, 0), (high, 0, rows)]
    pieces += [(shift(low, "core", 1, True), 4, 0), (shift(high, "core", 1, True), 4, rows)]
    for piece, slot, start in (
        (prev_low, 1, 0), (next_high, 2, rows), (prev_high, 1, rows), (next_low, 2, 0),
        (far_low, 3, 0), (far_high, 3, rows),
    ):
        pieces.append((piece, slot, start))
        pieces.append((shift(piece, "core", 1, True), slot + 4, start))
    ysize = lax.axis_size("y")
    places = [
        ((y + step) % ysize) * 2 + c for c in (core, 1 - core) for step in (0, -1, 1, 2)
    ] + [y * 2 + core]
    return pieces, jnp.stack(places).astype(jnp.int32)


def on_device(inputs, w_query, w_key, w_value, damping, grad_out):
    mine = inputs[0]
    tokens, width = mine.shape
    blocks = shaped(CHUNKS, tokens, DK)
    brick = shaped(CHUNKS, tokens, DK, dtype=BF16)
    pair = shaped(2, DK, DK)
    states = shaped(CHUNKS, DK, DK)
    unit = 2 * CHUNKS * tokens * DK * DK

    half = shaped(tokens // 2, width)
    low, high, upstream = call(
        prepare_body, [half, half, shaped(HEADS, tokens, DK)], [mine, grad_out[0]], 0
    )
    pieces, where = gather_plane(low, high)
    slots = tuple((slot, start) for _, slot, start in pieces)
    xb, q, k, v, gram_pre, cross_pre, first_tot = call(
        functools.partial(project_body, slots),
        [shaped(CHUNKS * tokens, width, dtype=BF16), brick, brick, brick, states, states, pair],
        [p for p, _, _ in pieces],
        unit * 28,
        tables=[where], raw=[w_query, w_key, w_value],
        scratch=[pltpu.VMEM((3, width, DK), BF16), pltpu.SemaphoreType.DMA((3,))],
    )
    prior = exclusive(first_tot, 1)
    upstream, _ = lax.optimization_barrier((upstream, first_tot))
    g = exchange(upstream, PLANE)

    z, u, dq, suf, second_tot = call(
        solve_body, [blocks, blocks, blocks, shaped(2, CHUNKS, DK, DK), pair],
        [q, k, v, gram_pre, cross_pre, damping, g, *prior], unit * 40, tables=[where],
    )
    after = exclusive(second_tot, -1)
    dq_all = exchange(dq, PLANE)

    seq = lax.axis_size("seq")
    ctx = ("z", "y", "core")
    spread = lax.axis_size(ctx)
    rows = width // (seq * spread)
    place = jnp.stack(
        [lax.axis_index("seq"), lax.axis_index("y") * 2 + lax.axis_index("core")]
    ).astype(jnp.int32)
    pieces = call(
        functools.partial(grads_body, seq),
        [shaped(width // seq, DK)] * seq + [shaped(2 * tokens, DK)] * CHUNKS,
        [k, v, z, u, suf, g, *after, xb], unit * 30, tables=[place],
        scratch=[
            pltpu.VMEM((CHUNKS * tokens, DK), BF16), pltpu.VMEM((width, DK), F32),
            pltpu.VMEM((CHUNKS, 2 * tokens, DK), F32),
        ],
    )
    dw, dkv = pieces[:seq], pieces[seq:]
    dw = sum((shift(part, "seq", step, True) for step, part in enumerate(dw) if step), dw[0])
    dkv = [shift(p, PLANE, step, True) if step else p for step, p in enumerate(dkv)]
    dw = exchange(dw.reshape(spread, rows, DK), ctx)
    dw = dw.reshape(spread // HEADS, HEADS, rows, DK)
    grad_weights = jnp.sum(dw, axis=0).transpose(1, 0, 2).reshape(rows, HEADS * DK)

    (grad_inputs,) = call(
        input_grad_body, [shaped(tokens, width, dtype=BF16)],
        [dq_all, w_query, w_key, w_value, *dkv], unit * 24, tables=[place],
        scratch=[pltpu.VMEM((tokens, width), BF16)] * 2,
    )
    return (grad_inputs[None], grad_weights)


def solution(mesh):
    grid = Mesh(mesh.devices.reshape(4, 8, 4, 2), ("seq", "z", "y", "core"))
    ctx = ("z", "y", "core")
    in_specs = (P("seq", ctx, None), P(), P(), P(), P(), P("seq", ctx, None))
    out_specs = (P("seq", ctx, None), P(("seq",) + ctx, None))

    return jax.shard_map(on_device, mesh=grid, in_specs=in_specs, out_specs=out_specs, check_vma=False)
```

```python
import functools

import jax
import jax.numpy as jnp
from jax import lax
from jax.experimental import pallas as pl
from jax.experimental.pallas import tpu as pltpu
from jax.sharding import Mesh, PartitionSpec as P


ITERS = 2
EPSILON = 1e-06
F32 = jnp.float32
BF16 = jnp.bfloat16
HEADS = 8
DK = 128
CHUNKS = 8
PLANE = ("y", "core")


def halves(x):
    hi = x.astype(BF16)
    return hi, (x - hi.astype(F32)).astype(BF16)


def nn(a, b):
    return lax.dot_general(a, b, (((1,), (0,)), ((), ())), preferred_element_type=F32)


def nt(a, b):
    return lax.dot_general(a, b, (((1,), (1,)), ((), ())), preferred_element_type=F32)


def tn(a, b):
    return lax.dot_general(a, b, (((0,), (0,)), ((), ())), preferred_element_type=F32)


def wide(x):
    return jnp.concatenate(halves(x), axis=1)


def tall(x):
    return jnp.concatenate(halves(x), axis=0)


def twice_wide(b):
    return jnp.concatenate([b, b], axis=1)


def twice_tall(b):
    return jnp.concatenate([b, b], axis=0)


def fold_cols(m):
    half = m.shape[1] // 2
    return m[:, :half] + m[:, half:]


def fold_rows(m):
    half = m.shape[0] // 2
    return m[:half] + m[half:]


def rowsum(x):
    return jnp.sum(x, axis=-1, keepdims=True)


def causal(size):
    rows = lax.broadcasted_iota(jnp.int32, (size, size), 0)
    cols = lax.broadcasted_iota(jnp.int32, (size, size), 1)
    return rows >= cols


def inv_norm(block):
    wide_block = block.astype(F32)
    return lax.rsqrt(rowsum(wide_block * wide_block) + EPSILON)


def across(column):
    size = column.shape[0]
    return jnp.transpose(jnp.broadcast_to(column, (size, size)))


def apply_all(vectors, keys, grams, scale2, damp):
    splits = [halves(p) for p in vectors]
    cats = [jnp.concatenate(s, axis=1) for s in splits]
    raw = [nt(c, twice_wide(k)) for c, k in zip(cats, keys)]
    prior = []
    for c, s, g in zip(cats, splits, grams):
        g_hi, g_lo = halves(g)
        prior.append(nn(c, twice_tall(g_hi)) + nn(s[0], g_lo))
    inner = [wide(r * m) for r, m in zip(raw, scale2)]
    return [
        o + nn(i, twice_tall(k)) + damp * p
        for o, i, k, p in zip(prior, inner, keys, vectors)
    ]


def conjugate(targets, keys, grams, scale2, damp):
    residual = list(targets)
    direction = list(targets)
    norm_now = [rowsum(r * r) for r in residual]
    solution = None
    for sweep in range(ITERS):
        image = apply_all(direction, keys, grams, scale2, damp)
        step = [n / (rowsum(p * w) + EPSILON) for n, p, w in zip(norm_now, direction, image)]
        moved = [a * p for a, p in zip(step, direction)]
        solution = moved if solution is None else [x + m for x, m in zip(solution, moved)]
        if sweep + 1 < ITERS:
            residual = [r - a * w for r, a, w in zip(residual, step, image)]
            norm_next = [rowsum(r * r) for r in residual]
            direction = [
                r + n / (o + EPSILON) * p
                for r, n, o, p in zip(residual, norm_next, norm_now, direction)
            ]
            norm_now = norm_next
    return solution


def staged(body, counts, tables, *refs):
    n_in, n_out = counts
    sources, refs = refs[:n_in], refs[n_in:]
    targets, refs = refs[:n_out], refs[n_out:]
    held, refs = refs[:n_in], refs[n_in:]
    made, (in_sems, out_sems, *rest) = refs[:n_out], refs[n_out:]
    loads = [
        pltpu.make_async_copy(s, h, in_sems.at[n]) for n, (s, h) in enumerate(zip(sources, held))
    ]
    stores = [
        pltpu.make_async_copy(m, t, out_sems.at[n]) for n, (m, t) in enumerate(zip(made, targets))
    ]
    for load in loads:
        load.start()
    arrived, sent = set(), set()

    def need(n):
        if n not in arrived:
            arrived.add(n)
            loads[n].wait()
        return held[n]

    def put(n):
        sent.add(n)
        stores[n].start()

    body(tables, need, made, put, *rest)
    for n in range(n_in):
        need(n)
    for n in range(n_out):
        if n not in sent:
            put(n)
    for store in stores:
        store.wait()


def shaped(*dims, dtype=F32):
    return jax.ShapeDtypeStruct(dims, dtype)


def call(body, outs, args, flops, tables=(), raw=(), scratch=()):
    def kernel(*refs):
        t, r = len(tables), len(raw)
        operands = refs[t + r :]
        staged(
            functools.partial(body, *refs[t : t + r]), (len(args), len(outs)), refs[:t], *operands
        )

    moved = sum(a.size * a.dtype.itemsize for a in args) + sum(
        o.size * jnp.dtype(o.dtype).itemsize for o in outs
    )
    anywhere = pl.BlockSpec(memory_space=pl.ANY)
    return pl.pallas_call(
        kernel,
        out_shape=tuple(outs),
        in_specs=[pl.BlockSpec(memory_space=pltpu.SMEM)] * len(tables)
        + [anywhere] * (len(raw) + len(args)),
        out_specs=tuple([anywhere] * len(outs)),
        scratch_shapes=[pltpu.VMEM(a.shape, a.dtype) for a in args]
        + [pltpu.VMEM(o.shape, o.dtype) for o in outs]
        + [pltpu.SemaphoreType.DMA((len(args),)), pltpu.SemaphoreType.DMA((len(outs),))]
        + list(scratch),
        compiler_params=pltpu.CompilerParams(vmem_limit_bytes=60 << 20),
        cost_estimate=pl.CostEstimate(flops=flops, bytes_accessed=moved, transcendentals=0),
    )(*tables, *raw, *args)


def fold_symmetric(m):
    half = m.shape[0] // 2
    rows = lax.broadcasted_iota(jnp.int32, (half, 2 * half), 0)
    cols = lax.broadcasted_iota(jnp.int32, (half, 2 * half), 1)
    low = pltpu.roll(m[half:], half, 1)
    diagonal = jnp.sum(jnp.where(rows == cols, low, 0.0), axis=0, keepdims=True)
    mixed = jnp.where((cols > rows) & (cols < half), low, m[:half])
    return jnp.concatenate([mixed, jnp.broadcast_to(diagonal, (8, 2 * half))], axis=0)


def unfold_symmetric(f):
    half = f.shape[1] // 2
    rows = lax.broadcasted_iota(jnp.int32, (half, 2 * half), 0)
    cols = lax.broadcasted_iota(jnp.int32, (half, 2 * half), 1)
    mixed, diagonal = f[:half], f[half : half + 1]
    turned = jnp.transpose(jnp.concatenate([mixed, jnp.zeros_like(mixed)], axis=0))
    top = jnp.where((cols > rows) & (cols < half), turned[:half], mixed)
    last = jnp.where(cols > rows, mixed, jnp.where(cols < rows, turned[:half], diagonal))
    low = jnp.where(cols < half, turned[half:], pltpu.roll(last, half, 1))
    return jnp.concatenate([top, low], axis=0)


FOLDED = DK // 2 + 8
STATE = FOLDED + DK


def total_of(need, first):
    near = [need(first + n) for n in range(4)]
    state = (near[0][...] + near[1][...]) + (near[2][...] + near[3][...])
    return unfold_symmetric(state[:FOLDED]), state[FOLDED:]


def chunk(j):
    return slice(j * DK, (j + 1) * DK)


def prepare_body(tables, need, made, put):
    x, (low, high) = need(0), made
    rows = low.shape[0]
    low[...] = x[:rows].astype(F32)
    put(0)
    high[...] = x[rows:].astype(F32)


def upstream_body(tables, need, made, put):
    for h in range(HEADS):
        made[0][h] = need(0)[:, chunk(h)].astype(F32)


def project_body(slots, wk_hbm, wv_hbm, tables, need, made, put, w_buf, w_sem):
    (where,) = tables
    xb, k_out, v_out, tot = made
    cols = pl.ds(pl.multiple_of(where[len(where) - 1] * DK, DK), DK)
    weights = [
        pltpu.make_async_copy(w.at[:, cols], w_buf.at[:, chunk(n)], w_sem.at[n])
        for n, w in enumerate((wk_hbm, wv_hbm))
    ]
    for copy in weights:
        copy.start()
    for n, (slot, start) in enumerate(slots):
        piece = need(n)
        row = pl.multiple_of(where[slot] * DK + start, DK // 2)
        xb[pl.ds(row, piece.shape[0]), :] = piece[...].astype(BF16)
    put(0)
    for copy in weights:
        copy.wait()
    both = nn(xb[...], w_buf[...]).astype(BF16)
    k, v = both[:, :DK], both[:, DK:]
    k_out[...] = k
    v_out[...] = v
    put(1)
    put(2)
    rk = inv_norm(k)
    kn = k.astype(F32) * rk
    tot[:FOLDED] = fold_symmetric(fold_cols(tn(k, wide(kn * rk))))
    tot[FOLDED:] = fold_cols(tn(v, wide(kn)))


def states_body(wq_hbm, tables, need, made, put, w_buf, w_sem):
    (where,) = tables
    q_out, gram_out = made
    cols = pl.ds(pl.multiple_of(where[len(where) - 1] * DK, DK), DK)
    weight = pltpu.make_async_copy(wq_hbm.at[:, cols], w_buf, w_sem.at[0])
    weight.start()
    k_in = need(0)
    gram = jnp.zeros((DK, DK), F32)
    for j in range(CHUNKS):
        gram_out[j] = gram
        if j + 1 < CHUNKS:
            k = k_in[chunk(j), :]
            rk = inv_norm(k)
            gram = gram + fold_cols(tn(k, wide(k.astype(F32) * (rk * rk))))
    put(1)
    weight.wait()
    q_out[...] = nn(need(1)[...], w_buf[...]).astype(BF16)


def targets_body(tables, need, made, put):
    k_in, v_in, g_in = need(0), need(1), need(2)
    keep = causal(DK)
    cross = jnp.zeros((DK, DK), F32)
    for j in range(CHUNKS):
        k, v, g = k_in[chunk(j), :], v_in[chunk(j), :], g_in[j].astype(BF16)
        rk = inv_norm(k)
        scores = nt(g, v) * jnp.where(keep, across(rk), 0.0)
        made[0][j] = nn(twice_wide(g), tall(cross)) + nn(wide(scores), twice_tall(k))
        if j + 1 < CHUNKS:
            cross = cross + fold_cols(tn(v, wide(k.astype(F32) * rk)))


def solve_body(tables, need, made, put):
    (where,) = tables
    q_in, k_in, gram_in, part, g_in, damp_in = [need(n) for n in range(6)]
    gram_prior, cross_prior = total_of(need, 6)
    z_out, u_out, tot = made
    damp = damp_in[pl.ds(where[len(where) - 1], 1), :]
    keep = causal(DK)
    keys = [k_in[chunk(j), :] for j in range(CHUNKS)]
    grams = [gram_in[j] + gram_prior for j in range(CHUNKS)]
    cross_tall = tall(cross_prior)
    scale2, targets = [], []
    for j, k in enumerate(keys):
        rk = inv_norm(k)
        row = jnp.where(keep, across(rk * rk), 0.0)
        scale2.append(twice_tall(row))
        right = part[j] + nn(twice_wide(g_in[j].astype(BF16)), cross_tall)
        q = q_in[chunk(j), :]
        targets.append(jnp.concatenate([q.astype(F32) * inv_norm(q), right], axis=0))
    both = conjugate(targets, keys, grams, scale2, damp)
    gram = jnp.zeros((DK, DK), F32)
    cross = jnp.zeros((DK, DK), F32)
    for j in range(CHUNKS):
        z, u = both[j][:DK], both[j][DK:]
        z_out[j] = z
        u_out[j] = u
        z_wide, u_wide = wide(z), wide(u)
        left = jnp.concatenate([u_wide, z_wide], axis=0)
        right = jnp.concatenate([z_wide, u_wide], axis=0)
        gram = gram + fold_rows(fold_cols(tn(left, right)))
        cross = cross + fold_cols(tn(g_in[j].astype(BF16), z_wide))
    tot[:FOLDED] = fold_symmetric(gram)
    tot[FOLDED:] = cross


def local_body(tables, need, made, put):
    q_in, k_in, v_in, g_in, z_in, u_in = [need(n) for n in range(6)]
    dq_out, dk_out, dv_out = made
    keep = causal(DK)
    for j in range(CHUNKS):
        q, u = q_in[chunk(j), :], u_in[j]
        rq = inv_norm(q)
        qn = q.astype(F32) * rq
        dq_out[j] = ((u - qn * rowsum(qn * u)) * rq).astype(BF16).astype(F32)
    put(0)
    gram = jnp.zeros((DK, DK), F32)
    cross = jnp.zeros((DK, DK), F32)
    for j in reversed(range(CHUNKS)):
        k, v = k_in[chunk(j), :], v_in[chunk(j), :]
        rk = inv_norm(k)
        row = jnp.where(keep, across(rk), 0.0)
        g = g_in[j].astype(BF16)
        scores = jnp.where(keep, nt(g, v), 0.0)
        u, z = u_in[j], z_in[j]
        u_wide, z_wide = wide(u), wide(z)
        kk = twice_wide(k)
        pair = nt(jnp.concatenate([u_wide, z_wide], axis=0), kk) * twice_tall(row)
        left = jnp.concatenate([scores - pair[:DK], -pair[DK:]], axis=0)
        right = jnp.concatenate([z_wide, u_wide], axis=0)
        dkn = fold_rows(fold_cols(tn(wide(left), right)))
        dkn = dkn + nn(twice_wide(v), tall(cross))
        dk_out[j] = dkn - rk * nn(kk, tall(gram))
        dv_out[j] = rk * nt(kk, wide(cross)) + tn(tall(pair[DK:]), twice_tall(g))
        if j:
            swapped = jnp.concatenate([u_wide, z_wide], axis=0)
            gram = gram + fold_rows(fold_cols(tn(swapped, right)))
            cross = cross + fold_cols(tn(g, z_wide))


def grads_body(seq, tables, need, made, put, dk_buf, dw_buf, out):
    (place,) = tables
    k_in, v_in, dk_part, dv_part = [need(n) for n in range(4)]
    gram_after, cross_after = total_of(need, 4)
    gram_tall, cross_tall, cross_wide = tall(gram_after), tall(cross_after), wide(cross_after)
    for j in range(CHUNKS):
        k, v = k_in[chunk(j), :], v_in[chunk(j), :]
        rk = inv_norm(k)
        kn = k.astype(F32) * rk
        kk = twice_wide(k)
        dkn = dk_part[j] + nn(twice_wide(v), cross_tall) - rk * nn(kk, gram_tall)
        dk = ((dkn - kn * rowsum(kn * dkn)) * rk).astype(BF16)
        dk_buf[chunk(j), :] = dk
        out[j, :DK] = dk.astype(F32)
        dv = dv_part[j] + rk * nt(kk, cross_wide)
        out[j, DK:] = dv.astype(BF16).astype(F32)
    dw_buf[...] = jnp.transpose(tn(dk_buf[...], need(8)[...]))
    rows = made[0].shape[0]
    for step in range(seq):
        start = pl.multiple_of(lax.rem(place[0] + step, seq) * rows, rows)
        made[step][...] = dw_buf[pl.ds(start, rows), :]
        put(step)
    for step in range(CHUNKS):
        made[seq + step][...] = out[lax.rem(place[1] + step, CHUNKS)]
        put(seq + step)


def input_grad_body(tables, need, made, put, dk_cat, dv_cat):
    (place,) = tables
    dq_cat = jnp.concatenate([need(0)[h].astype(BF16) for h in range(HEADS)], axis=1)
    total = nt(dq_cat, need(1)[...])
    for step in range(HEADS):
        piece = need(4 + step)
        head = lax.rem(place[1] + HEADS - step, HEADS)
        cols = pl.ds(pl.multiple_of(head * DK, DK), DK)
        dk_cat[:, cols] = piece[:DK].astype(BF16)
        dv_cat[:, cols] = piece[DK:].astype(BF16)
    total = total + nt(dk_cat[...], need(2)[...])
    total = total + nt(dv_cat[...], need(3)[...])
    made[0][...] = total.astype(BF16)


def shift(x, axis, by, wrap):
    size = lax.axis_size(axis)
    pairs = [(i, (i + by) % size) for i in range(size) if wrap or 0 <= i + by < size]
    return lax.ppermute(x, axis, pairs)


def exclusive(total, sign):
    one, two = shift(total, "z", sign, False), shift(total, "z", 2 * sign, False)
    third = total + one + two
    return one, two, shift(third, "z", 3 * sign, False), shift(third, "z", 6 * sign, False)


def exchange(x, axis):
    return lax.all_to_all(x, axis, 0, 0)


def gather_plane(low, high):
    y, core = lax.axis_index("y"), lax.axis_index("core")
    rows = low.shape[0]
    prev_low = shift(low, "y", 1, True)
    next_high = shift(high, "y", -1, True)
    prev_high = shift(high, "y", 1, True)
    next_low = shift(low, "y", -1, True)
    far_low = shift(prev_low, "y", 1, True)
    far_high = shift(next_high, "y", -1, True)
    pieces = [(low, 0, 0), (high, 0, rows)]
    pieces += [(shift(low, "core", 1, True), 4, 0), (shift(high, "core", 1, True), 4, rows)]
    for piece, slot, start in (
        (prev_low, 1, 0), (next_high, 2, rows), (prev_high, 1, rows), (next_low, 2, 0),
        (far_low, 3, 0), (far_high, 3, rows),
    ):
        pieces.append((piece, slot, start))
        pieces.append((shift(piece, "core", 1, True), slot + 4, start))
    ysize = lax.axis_size("y")
    places = [
        ((y + step) % ysize) * 2 + c for c in (core, 1 - core) for step in (0, -1, 1, 2)
    ] + [y * 2 + core]
    return pieces, jnp.stack(places).astype(jnp.int32)


def on_device(inputs, w_query, w_key, w_value, damping, grad_out):
    mine = inputs[0]
    tokens, width = mine.shape
    plane = CHUNKS * tokens
    blocks = shaped(CHUNKS, tokens, DK)
    brick = shaped(plane, DK, dtype=BF16)
    state = shaped(STATE, DK)
    unit = 2 * plane * DK * DK

    half = shaped(tokens // 2, width)
    low, high = call(prepare_body, [half, half], [mine], 0)
    pieces, where = gather_plane(low, high)
    slots = tuple((slot, start) for _, slot, start in pieces)
    pieces = [p for p, _, _ in pieces]
    upstream, _ = lax.optimization_barrier((grad_out[0], pieces[4]))
    (upstream,) = call(upstream_body, [shaped(HEADS, tokens, DK)], [upstream], 0)
    xb, k, v, first_tot = call(
        functools.partial(project_body, slots),
        [shaped(plane, width, dtype=BF16), brick, brick, state],
        pieces, unit * 28, tables=[where], raw=[w_key, w_value],
        scratch=[pltpu.VMEM((width, 2 * DK), BF16), pltpu.SemaphoreType.DMA((2,))],
    )
    prior = exclusive(first_tot, 1)
    upstream, _ = lax.optimization_barrier((upstream, first_tot))
    g = exchange(upstream, PLANE)
    q, gram_pre = call(
        states_body, [brick, shaped(CHUNKS, DK, DK)], [k, xb], unit * 10,
        tables=[where], raw=[w_query],
        scratch=[pltpu.VMEM((width, DK), BF16), pltpu.SemaphoreType.DMA((1,))],
    )
    (part,) = call(targets_body, [blocks], [k, v, g], unit * 8)

    z, u, second_tot = call(
        solve_body, [blocks, blocks, state],
        [q, k, gram_pre, part, g, damping, *prior], unit * 40, tables=[where],
    )
    after = exclusive(second_tot, -1)
    dq, dk_part, dv_part = call(local_body, [blocks, blocks, blocks], [q, k, v, g, z, u], unit * 30)
    dq_all = exchange(dq, PLANE)

    seq = lax.axis_size("seq")
    ctx = ("z", "y", "core")
    spread = lax.axis_size(ctx)
    rows = width // (seq * spread)
    place = jnp.stack(
        [lax.axis_index("seq"), lax.axis_index("y") * 2 + lax.axis_index("core")]
    ).astype(jnp.int32)
    pieces = call(
        functools.partial(grads_body, seq),
        [shaped(width // seq, DK)] * seq + [shaped(2 * tokens, DK)] * CHUNKS,
        [k, v, dk_part, dv_part, *after, xb], unit * 14, tables=[place],
        scratch=[
            pltpu.VMEM((plane, DK), BF16), pltpu.VMEM((width, DK), F32),
            pltpu.VMEM((CHUNKS, 2 * tokens, DK), F32),
        ],
    )
    dw, dkv = pieces[:seq], pieces[seq:]
    dw = sum((shift(part, "seq", step, True) for step, part in enumerate(dw) if step), dw[0])
    dkv = [shift(p, PLANE, step, True) if step else p for step, p in enumerate(dkv)]
    dw = exchange(dw.reshape(spread, rows, DK), ctx)
    dw = dw.reshape(spread // HEADS, HEADS, rows, DK)
    grad_weights = jnp.sum(dw, axis=0).transpose(1, 0, 2).reshape(rows, HEADS * DK)

    (grad_inputs,) = call(
        input_grad_body, [shaped(tokens, width, dtype=BF16)],
        [dq_all, w_query, w_key, w_value, *dkv], unit * 24, tables=[place],
        scratch=[pltpu.VMEM((tokens, width), BF16)] * 2,
    )
    return (grad_inputs[None], grad_weights)


def solution(mesh):
    grid = Mesh(mesh.devices.reshape(4, 8, 4, 2), ("seq", "z", "y", "core"))
    ctx = ("z", "y", "core")
    in_specs = (P("seq", ctx, None), P(), P(), P(), P(), P("seq", ctx, None))
    out_specs = (P("seq", ctx, None), P(("seq",) + ctx, None))

    return jax.shard_map(on_device, mesh=grid, in_specs=in_specs, out_specs=out_specs, check_vma=False)
```

```python
import functools

import jax
import jax.numpy as jnp
from jax import lax
from jax.experimental import pallas as pl
from jax.experimental.pallas import tpu as pltpu
from jax.sharding import Mesh, PartitionSpec as P


ITERS = 2
EPSILON = 1e-06
F32 = jnp.float32
BF16 = jnp.bfloat16
HEADS = 8
DK = 128
CHUNKS = 8
PLANE = ("y", "core")


def halves(x):
    hi = x.astype(BF16)
    return hi, (x - hi.astype(F32)).astype(BF16)


def nn(a, b):
    return lax.dot_general(a, b, (((1,), (0,)), ((), ())), preferred_element_type=F32)


def nt(a, b):
    return lax.dot_general(a, b, (((1,), (1,)), ((), ())), preferred_element_type=F32)


def tn(a, b):
    return lax.dot_general(a, b, (((0,), (0,)), ((), ())), preferred_element_type=F32)


def wide(x):
    return jnp.concatenate(halves(x), axis=1)


def tall(x):
    return jnp.concatenate(halves(x), axis=0)


def twice_wide(b):
    return jnp.concatenate([b, b], axis=1)


def twice_tall(b):
    return jnp.concatenate([b, b], axis=0)


def fold_cols(m):
    half = m.shape[1] // 2
    return m[:, :half] + m[:, half:]


def fold_rows(m):
    half = m.shape[0] // 2
    return m[:half] + m[half:]


def rowsum(x):
    return jnp.sum(x, axis=-1, keepdims=True)


def causal(size):
    rows = lax.broadcasted_iota(jnp.int32, (size, size), 0)
    cols = lax.broadcasted_iota(jnp.int32, (size, size), 1)
    return rows >= cols


def inv_norm(block):
    wide_block = block.astype(F32)
    return lax.rsqrt(rowsum(wide_block * wide_block) + EPSILON)


def across(column):
    size = column.shape[0]
    return jnp.transpose(jnp.broadcast_to(column, (size, size)))


def system(key, gram):
    turned = jnp.transpose(key)
    hi, lo = halves(gram)
    upper = jnp.concatenate([turned, hi, lo], axis=1)
    lower = jnp.concatenate([turned, hi, jnp.zeros_like(lo)], axis=1)
    return jnp.concatenate([upper, lower], axis=0), twice_tall(key)


def apply_all(vectors, systems, scale2, damp):
    firsts = [nn(wide(p), s[0]) for p, s in zip(vectors, systems)]
    inner = [wide(f[:, :DK] * m) for f, m in zip(firsts, scale2)]
    return [
        nn(i, s[1]) + (f[:, DK : 2 * DK] + f[:, 2 * DK :]) + damp * p
        for i, s, f, p in zip(inner, systems, firsts, vectors)
    ]


def conjugate(targets, systems, scale2, damp):
    residual = list(targets)
    direction = list(targets)
    norm_now = [rowsum(r * r) for r in residual]
    solution = None
    for sweep in range(ITERS):
        image = apply_all(direction, systems, scale2, damp)
        step = [n / (rowsum(p * w) + EPSILON) for n, p, w in zip(norm_now, direction, image)]
        moved = [a * p for a, p in zip(step, direction)]
        solution = moved if solution is None else [x + m for x, m in zip(solution, moved)]
        if sweep + 1 < ITERS:
            residual = [r - a * w for r, a, w in zip(residual, step, image)]
            norm_next = [rowsum(r * r) for r in residual]
            direction = [
                r + n / (o + EPSILON) * p
                for r, n, o, p in zip(residual, norm_next, norm_now, direction)
            ]
            norm_now = norm_next
    return solution


def staged(body, counts, late, tables, *refs):
    n_in, n_out = counts
    sources, refs = refs[:n_in], refs[n_in:]
    targets, refs = refs[:n_out], refs[n_out:]
    held, refs = refs[:n_in], refs[n_in:]
    made, (in_sems, out_sems, *rest) = refs[:n_out], refs[n_out:]
    loads = [
        pltpu.make_async_copy(s, h, in_sems.at[n]) for n, (s, h) in enumerate(zip(sources, held))
    ]
    stores = [
        pltpu.make_async_copy(m, t, out_sems.at[n]) for n, (m, t) in enumerate(zip(made, targets))
    ]
    begun, arrived, sent = set(), set(), set()

    def begin(n):
        if n not in begun:
            begun.add(n)
            loads[n].start()

    for n in range(n_in - late):
        begin(n)

    def need(n):
        begin(n)
        if n not in arrived:
            arrived.add(n)
            loads[n].wait()
        return held[n]

    need.begin = begin

    def put(n):
        sent.add(n)
        stores[n].start()

    body(tables, need, made, put, *rest)
    for n in range(n_in):
        need(n)
    for n in range(n_out):
        if n not in sent:
            put(n)
    for store in stores:
        store.wait()


def shaped(*dims, dtype=F32):
    return jax.ShapeDtypeStruct(dims, dtype)


ANYWHERE = pl.BlockSpec(memory_space=pl.ANY)


def call(body, outs, args, flops, tables=(), raw=(), scratch=(), late=0, raw_spec=ANYWHERE, grant=60):
    def kernel(*refs):
        t, r = len(tables), len(raw)
        operands = refs[t + r :]
        staged(
            functools.partial(body, *refs[t : t + r]), (len(args), len(outs)), late, refs[:t],
            *operands,
        )

    moved = sum(a.size * a.dtype.itemsize for a in args) + sum(
        o.size * jnp.dtype(o.dtype).itemsize for o in outs
    )
    return pl.pallas_call(
        kernel,
        out_shape=tuple(outs),
        in_specs=[pl.BlockSpec(memory_space=pltpu.SMEM)] * len(tables)
        + [raw_spec] * len(raw) + [ANYWHERE] * len(args),
        out_specs=tuple([ANYWHERE] * len(outs)),
        scratch_shapes=[pltpu.VMEM(a.shape, a.dtype) for a in args]
        + [pltpu.VMEM(o.shape, o.dtype) for o in outs]
        + [pltpu.SemaphoreType.DMA((len(args),)), pltpu.SemaphoreType.DMA((len(outs),))]
        + list(scratch),
        compiler_params=pltpu.CompilerParams(vmem_limit_bytes=grant << 20),
        cost_estimate=pl.CostEstimate(flops=flops, bytes_accessed=moved, transcendentals=0),
    )(*tables, *raw, *args)


def fold_symmetric(m):
    half = m.shape[0] // 2
    rows = lax.broadcasted_iota(jnp.int32, (half, 2 * half), 0)
    cols = lax.broadcasted_iota(jnp.int32, (half, 2 * half), 1)
    low = pltpu.roll(m[half:], half, 1)
    diagonal = jnp.sum(jnp.where(rows == cols, low, 0.0), axis=0, keepdims=True)
    mixed = jnp.where((cols > rows) & (cols < half), low, m[:half])
    return jnp.concatenate([mixed, jnp.broadcast_to(diagonal, (8, 2 * half))], axis=0)


def unfold_symmetric(f):
    half = f.shape[1] // 2
    rows = lax.broadcasted_iota(jnp.int32, (half, 2 * half), 0)
    cols = lax.broadcasted_iota(jnp.int32, (half, 2 * half), 1)
    mixed, diagonal = f[:half], f[half : half + 1]
    turned = jnp.transpose(jnp.concatenate([mixed, jnp.zeros_like(mixed)], axis=0))
    top = jnp.where((cols > rows) & (cols < half), turned[:half], mixed)
    last = jnp.where(cols > rows, mixed, jnp.where(cols < rows, turned[:half], diagonal))
    low = jnp.where(cols < half, turned[half:], pltpu.roll(last, half, 1))
    return jnp.concatenate([top, low], axis=0)


FOLDED = DK // 2 + 8
STATE = FOLDED + DK


def total_of(need, first):
    near = [need(first + n) for n in range(4)]
    state = (near[0][...] + near[1][...]) + (near[2][...] + near[3][...])
    return unfold_symmetric(state[:FOLDED]), state[FOLDED:]


def chunk(j):
    return slice(j * DK, (j + 1) * DK)


def prepare_body(tables, need, made, put):
    x, (low, high) = need(0), made
    rows = low.shape[0]
    low[...] = x[:rows].astype(F32)
    put(0)
    high[...] = x[rows:].astype(F32)


def upstream_body(tables, need, made, put):
    for h in range(HEADS):
        made[0][h] = need(0)[:, chunk(h)].astype(F32)


def project_body(slots, wk_hbm, wv_hbm, wq_hbm, tables, need, made, put, w_buf, w_sem):
    (where,) = tables
    xb, k_out, v_out, q_out, tot = made
    cols = pl.ds(pl.multiple_of(where[len(where) - 1] * DK, DK), DK)
    weights = [
        pltpu.make_async_copy(w.at[:, cols], w_buf.at[:, chunk(n)], w_sem.at[n])
        for n, w in enumerate((wk_hbm, wv_hbm, wq_hbm))
    ]
    for copy in weights:
        copy.start()
    for n, (slot, start) in enumerate(slots):
        piece = need(n)
        row = pl.multiple_of(where[slot] * DK + start, DK // 2)
        xb[pl.ds(row, piece.shape[0]), :] = piece[...].astype(BF16)
    put(0)
    for copy in weights:
        copy.wait()
    both = nn(xb[...], w_buf[:, : 2 * DK]).astype(BF16)
    k, v = both[:, :DK], both[:, DK:]
    k_out[...] = k
    v_out[...] = v
    put(1)
    put(2)
    rk = inv_norm(k)
    kn = k.astype(F32) * rk
    tot[:FOLDED] = fold_symmetric(fold_cols(tn(k, wide(kn * rk))))
    tot[FOLDED:] = fold_cols(tn(v, wide(kn)))
    put(4)
    q_out[...] = nn(xb[...], w_buf[:, 2 * DK :]).astype(BF16)


def targets_body(tables, need, made, put):
    k_in = need(0)
    part, gram_out = made
    gram = jnp.zeros((DK, DK), F32)
    for j in range(CHUNKS):
        gram_out[j] = gram
        if j + 1 < CHUNKS:
            k = k_in[chunk(j), :]
            rk = inv_norm(k)
            gram = gram + fold_cols(tn(k, wide(k.astype(F32) * (rk * rk))))
    put(1)
    v_in, g_in = need(1), need(2)
    keep = causal(DK)
    cross = jnp.zeros((DK, DK), F32)
    for j in range(CHUNKS):
        k, v, g = k_in[chunk(j), :], v_in[chunk(j), :], g_in[j].astype(BF16)
        rk = inv_norm(k)
        scores = nt(g, v) * jnp.where(keep, across(rk), 0.0)
        part[j] = nn(twice_wide(g), tall(cross)) + nn(wide(scores), twice_tall(k))
        if j + 1 < CHUNKS:
            cross = cross + fold_cols(tn(v, wide(k.astype(F32) * rk)))


def solve_body(tables, need, made, put):
    (where,) = tables
    q_in, k_in, gram_in, part, g_in, damp_in = [need(n) for n in range(6)]
    gram_prior, cross_prior = total_of(need, 6)
    z_out, u_out, tot = made
    damp = damp_in[pl.ds(where[len(where) - 1], 1), :]
    keep = causal(DK)
    keys = [k_in[chunk(j), :] for j in range(CHUNKS)]
    systems = [system(k, gram_in[j] + gram_prior) for j, k in enumerate(keys)]
    cross_tall = tall(cross_prior)
    scale2, targets = [], []
    for j, k in enumerate(keys):
        rk = inv_norm(k)
        row = jnp.where(keep, across(rk * rk), 0.0)
        scale2.append(twice_tall(row))
        right = part[j] + nn(twice_wide(g_in[j].astype(BF16)), cross_tall)
        q = q_in[chunk(j), :]
        targets.append(jnp.concatenate([q.astype(F32) * inv_norm(q), right], axis=0))
    both = conjugate(targets, systems, scale2, damp)
    gram = jnp.zeros((DK, DK), F32)
    cross = jnp.zeros((DK, DK), F32)
    for j in range(CHUNKS):
        z, u = both[j][:DK], both[j][DK:]
        z_out[j] = z
        u_out[j] = u
        z_wide, u_wide = wide(z), wide(u)
        left = jnp.concatenate([u_wide, z_wide], axis=0)
        right = jnp.concatenate([z_wide, u_wide], axis=0)
        gram = gram + fold_rows(fold_cols(tn(left, right)))
        cross = cross + fold_cols(tn(g_in[j].astype(BF16), z_wide))
    tot[:FOLDED] = fold_symmetric(gram)
    tot[FOLDED:] = cross


def local_body(tables, need, made, put):
    q_in, k_in, v_in, g_in, z_in, u_in = [need(n) for n in range(6)]
    dq_out, dk_out, dv_out = made
    keep = causal(DK)
    for j in range(CHUNKS):
        q, u = q_in[chunk(j), :], u_in[j]
        rq = inv_norm(q)
        qn = q.astype(F32) * rq
        dq_out[j] = ((u - qn * rowsum(qn * u)) * rq).astype(BF16).astype(F32)
    put(0)
    gram = jnp.zeros((DK, DK), F32)
    cross = jnp.zeros((DK, DK), F32)
    for j in reversed(range(CHUNKS)):
        k, v = k_in[chunk(j), :], v_in[chunk(j), :]
        rk = inv_norm(k)
        row = jnp.where(keep, across(rk), 0.0)
        g = g_in[j].astype(BF16)
        scores = jnp.where(keep, nt(g, v), 0.0)
        u, z = u_in[j], z_in[j]
        u_wide, z_wide = wide(u), wide(z)
        kk = twice_wide(k)
        pair = nt(jnp.concatenate([u_wide, z_wide], axis=0), kk) * twice_tall(row)
        left = jnp.concatenate([scores - pair[:DK], -pair[DK:]], axis=0)
        right = jnp.concatenate([z_wide, u_wide], axis=0)
        dkn = fold_rows(fold_cols(tn(wide(left), right)))
        dkn = dkn + nn(twice_wide(v), tall(cross))
        dk_out[j] = dkn - rk * nn(kk, tall(gram))
        dv_out[j] = rk * nt(kk, wide(cross)) + tn(tall(pair[DK:]), twice_tall(g))
        if j:
            swapped = jnp.concatenate([u_wide, z_wide], axis=0)
            gram = gram + fold_rows(fold_cols(tn(swapped, right)))
            cross = cross + fold_cols(tn(g, z_wide))


def grads_body(seq, tables, need, made, put, dk_buf, dw_buf, out):
    (place,) = tables
    k_in, v_in, dk_part, dv_part = [need(n) for n in range(4)]
    gram_after, cross_after = total_of(need, 4)
    need.begin(8)
    gram_tall, cross_tall, cross_wide = tall(gram_after), tall(cross_after), wide(cross_after)
    for j in range(CHUNKS):
        k, v = k_in[chunk(j), :], v_in[chunk(j), :]
        rk = inv_norm(k)
        kn = k.astype(F32) * rk
        kk = twice_wide(k)
        dkn = dk_part[j] + nn(twice_wide(v), cross_tall) - rk * nn(kk, gram_tall)
        dk = ((dkn - kn * rowsum(kn * dkn)) * rk).astype(BF16)
        dk_buf[chunk(j), :] = dk
        out[j, :DK] = dk.astype(F32)
        dv = dv_part[j] + rk * nt(kk, cross_wide)
        out[j, DK:] = dv.astype(BF16).astype(F32)
    dw_buf[...] = jnp.transpose(tn(dk_buf[...], need(8)[...]))
    rows = made[0].shape[0]
    for step in range(seq):
        start = pl.multiple_of(lax.rem(place[0] + step, seq) * rows, rows)
        made[step][...] = dw_buf[pl.ds(start, rows), :]
        put(step)
    for step in range(CHUNKS):
        made[seq + step][...] = out[lax.rem(place[1] + step, CHUNKS)]
        put(seq + step)


def input_grad_body(wq, tables, need, made, put, dk_cat, dv_cat):
    (place,) = tables
    dq_cat = jnp.concatenate([need(0)[h].astype(BF16) for h in range(HEADS)], axis=1)
    total = nt(dq_cat, wq[...])
    for step in range(HEADS):
        piece = need(1 + step)
        head = lax.rem(place[1] + HEADS - step, HEADS)
        cols = pl.ds(pl.multiple_of(head * DK, DK), DK)
        dk_cat[:, cols] = piece[:DK].astype(BF16)
        dv_cat[:, cols] = piece[DK:].astype(BF16)
    total = total + nt(dk_cat[...], need(1 + HEADS)[...])
    total = total + nt(dv_cat[...], need(2 + HEADS)[...])
    made[0][...] = total.astype(BF16)


def shift(x, axis, by, wrap):
    size = lax.axis_size(axis)
    pairs = [(i, (i + by) % size) for i in range(size) if wrap or 0 <= i + by < size]
    return lax.ppermute(x, axis, pairs)


def exclusive(total, sign):
    one, two = shift(total, "z", sign, False), shift(total, "z", 2 * sign, False)
    third = total + one + two
    return one, two, shift(third, "z", 3 * sign, False), shift(third, "z", 6 * sign, False)


def exchange(x, axis):
    return lax.all_to_all(x, axis, 0, 0)


def gather_plane(low, high):
    y, core = lax.axis_index("y"), lax.axis_index("core")
    rows = low.shape[0]
    prev_low = shift(low, "y", 1, True)
    next_high = shift(high, "y", -1, True)
    prev_high = shift(high, "y", 1, True)
    next_low = shift(low, "y", -1, True)
    far_low = shift(prev_low, "y", 1, True)
    far_high = shift(next_high, "y", -1, True)
    pieces = [(low, 0, 0), (high, 0, rows)]
    pieces += [(shift(low, "core", 1, True), 4, 0), (shift(high, "core", 1, True), 4, rows)]
    for piece, slot, start in (
        (prev_low, 1, 0), (next_high, 2, rows), (prev_high, 1, rows), (next_low, 2, 0),
        (far_low, 3, 0), (far_high, 3, rows),
    ):
        pieces.append((piece, slot, start))
        pieces.append((shift(piece, "core", 1, True), slot + 4, start))
    ysize = lax.axis_size("y")
    places = [
        ((y + step) % ysize) * 2 + c for c in (core, 1 - core) for step in (0, -1, 1, 2)
    ] + [y * 2 + core]
    return pieces, jnp.stack(places).astype(jnp.int32)


def on_device(inputs, w_query, w_key, w_value, damping, grad_out):
    mine = inputs[0]
    tokens, width = mine.shape
    plane = CHUNKS * tokens
    blocks = shaped(CHUNKS, tokens, DK)
    brick = shaped(plane, DK, dtype=BF16)
    state = shaped(STATE, DK)
    unit = 2 * plane * DK * DK

    half = shaped(tokens // 2, width)
    low, high = call(prepare_body, [half, half], [mine], 0)
    pieces, where = gather_plane(low, high)
    slots = tuple((slot, start) for _, slot, start in pieces)
    pieces = [p for p, _, _ in pieces]
    (upstream,) = call(upstream_body, [shaped(HEADS, tokens, DK)], [grad_out[0]], 0)
    xb, k, v, q, first_tot = call(
        functools.partial(project_body, slots),
        [shaped(plane, width, dtype=BF16), brick, brick, brick, state],
        pieces, unit * 28, tables=[where], raw=[w_key, w_value, w_query],
        scratch=[pltpu.VMEM((width, 3 * DK), BF16), pltpu.SemaphoreType.DMA((3,))],
    )
    prior = exclusive(first_tot, 1)
    upstream, _ = lax.optimization_barrier((upstream, first_tot))
    g = exchange(upstream, PLANE)
    part, gram_pre = call(targets_body, [blocks, shaped(CHUNKS, DK, DK)], [k, v, g], unit * 10)

    z, u, second_tot = call(
        solve_body, [blocks, blocks, state],
        [q, k, gram_pre, part, g, damping, *prior], unit * 40, tables=[where],
    )
    after = exclusive(second_tot, -1)
    dq, dk_part, dv_part = call(local_body, [blocks, blocks, blocks], [q, k, v, g, z, u], unit * 30)
    dq_all = exchange(dq, PLANE)

    seq = lax.axis_size("seq")
    ctx = ("z", "y", "core")
    spread = lax.axis_size(ctx)
    rows = width // (seq * spread)
    place = jnp.stack(
        [lax.axis_index("seq"), lax.axis_index("y") * 2 + lax.axis_index("core")]
    ).astype(jnp.int32)
    pieces = call(
        functools.partial(grads_body, seq),
        [shaped(width // seq, DK)] * seq + [shaped(2 * tokens, DK)] * CHUNKS,
        [k, v, dk_part, dv_part, *after, xb], unit * 14, tables=[place], late=1,
        scratch=[
            pltpu.VMEM((plane, DK), BF16), pltpu.VMEM((width, DK), F32),
            pltpu.VMEM((CHUNKS, 2 * tokens, DK), F32),
        ],
    )
    dw, dkv = pieces[:seq], pieces[seq:]
    dw = sum((shift(part, "seq", step, True) for step, part in enumerate(dw) if step), dw[0])
    dkv = [shift(p, PLANE, step, True) if step else p for step, p in enumerate(dkv)]
    dw = exchange(dw.reshape(spread, rows, DK), ctx)
    dw = dw.reshape(spread // HEADS, HEADS, rows, DK)
    grad_weights = jnp.sum(dw, axis=0).transpose(1, 0, 2).reshape(rows, HEADS * DK)

    (grad_inputs,) = call(
        input_grad_body, [shaped(tokens, width, dtype=BF16)],
        [dq_all, *dkv, w_key, w_value], unit * 24, tables=[place], raw=[w_query],
        raw_spec=pl.BlockSpec(memory_space=pltpu.VMEM), grant=24,
        scratch=[pltpu.VMEM((tokens, width), BF16)] * 2,
    )
    return (grad_inputs[None], grad_weights)


def solution(mesh):
    grid = Mesh(mesh.devices.reshape(4, 8, 4, 2), ("seq", "z", "y", "core"))
    ctx = ("z", "y", "core")
    in_specs = (P("seq", ctx, None), P(), P(), P(), P(), P("seq", ctx, None))
    out_specs = (P("seq", ctx, None), P(("seq",) + ctx, None))

    return jax.shard_map(on_device, mesh=grid, in_specs=in_specs, out_specs=out_specs, check_vma=False)
```

```python
import functools

import jax
import jax.numpy as jnp
from jax import lax
from jax.experimental import pallas as pl
from jax.experimental.pallas import tpu as pltpu
from jax.sharding import Mesh, PartitionSpec as P


ITERS = 2
EPSILON = 1e-06
F32 = jnp.float32
BF16 = jnp.bfloat16
HEADS = 8
DK = 128
CHUNKS = 8
PLANE = ("y", "core")


def halves(x):
    hi = x.astype(BF16)
    return hi, (x - hi.astype(F32)).astype(BF16)


def nn(a, b):
    return lax.dot_general(a, b, (((1,), (0,)), ((), ())), preferred_element_type=F32)


def nt(a, b):
    return lax.dot_general(a, b, (((1,), (1,)), ((), ())), preferred_element_type=F32)


def tn(a, b):
    return lax.dot_general(a, b, (((0,), (0,)), ((), ())), preferred_element_type=F32)


def wide(x):
    return jnp.concatenate(halves(x), axis=1)


def tall(x):
    return jnp.concatenate(halves(x), axis=0)


def twice_wide(b):
    return jnp.concatenate([b, b], axis=1)


def twice_tall(b):
    return jnp.concatenate([b, b], axis=0)


def fold_cols(m):
    half = m.shape[1] // 2
    return m[:, :half] + m[:, half:]


def fold_rows(m):
    half = m.shape[0] // 2
    return m[:half] + m[half:]


def rowsum(x):
    return jnp.sum(x, axis=-1, keepdims=True)


def causal(size):
    rows = lax.broadcasted_iota(jnp.int32, (size, size), 0)
    cols = lax.broadcasted_iota(jnp.int32, (size, size), 1)
    return rows >= cols


def inv_norm(block):
    wide_block = block.astype(F32)
    return lax.rsqrt(rowsum(wide_block * wide_block) + EPSILON)


def across(column):
    size = column.shape[0]
    return jnp.transpose(jnp.broadcast_to(column, (size, size)))


def system(key, gram):
    turned = jnp.transpose(key)
    hi, lo = halves(gram)
    upper = jnp.concatenate([turned, hi, lo], axis=1)
    lower = jnp.concatenate([turned, hi, jnp.zeros_like(lo)], axis=1)
    return jnp.concatenate([upper, lower], axis=0), twice_tall(key)


def apply_all(vectors, systems, scale2, damp):
    firsts = [nn(wide(p), s[0]) for p, s in zip(vectors, systems)]
    inner = [wide(f[:, :DK] * m) for f, m in zip(firsts, scale2)]
    return [
        nn(i, s[1]) + (f[:, DK : 2 * DK] + f[:, 2 * DK :]) + damp * p
        for i, s, f, p in zip(inner, systems, firsts, vectors)
    ]


def conjugate(targets, systems, scale2, damp):
    residual = list(targets)
    direction = list(targets)
    norm_now = [rowsum(r * r) for r in residual]
    solution = None
    for sweep in range(ITERS):
        image = apply_all(direction, systems, scale2, damp)
        step = [n / (rowsum(p * w) + EPSILON) for n, p, w in zip(norm_now, direction, image)]
        moved = [a * p for a, p in zip(step, direction)]
        solution = moved if solution is None else [x + m for x, m in zip(solution, moved)]
        if sweep + 1 < ITERS:
            residual = [r - a * w for r, a, w in zip(residual, step, image)]
            norm_next = [rowsum(r * r) for r in residual]
            direction = [
                r + n / (o + EPSILON) * p
                for r, n, o, p in zip(residual, norm_next, norm_now, direction)
            ]
            norm_now = norm_next
    return solution


def staged(body, counts, tables, *refs):
    n_in, n_out = counts
    sources, refs = refs[:n_in], refs[n_in:]
    targets, refs = refs[:n_out], refs[n_out:]
    held, refs = refs[:n_in], refs[n_in:]
    made, (in_sems, out_sems, *rest) = refs[:n_out], refs[n_out:]
    loads = [
        pltpu.make_async_copy(s, h, in_sems.at[n]) for n, (s, h) in enumerate(zip(sources, held))
    ]
    stores = [
        pltpu.make_async_copy(m, t, out_sems.at[n]) for n, (m, t) in enumerate(zip(made, targets))
    ]
    for load in loads:
        load.start()
    arrived, sent = set(), set()

    def need(n):
        if n not in arrived:
            arrived.add(n)
            loads[n].wait()
        return held[n]

    def put(n):
        sent.add(n)
        stores[n].start()

    body(tables, need, made, put, *rest)
    for n in range(n_in):
        need(n)
    for n in range(n_out):
        if n not in sent:
            put(n)
    for store in stores:
        store.wait()


def shaped(*dims, dtype=F32):
    return jax.ShapeDtypeStruct(dims, dtype)


ANYWHERE = pl.BlockSpec(memory_space=pl.ANY)


def call(body, outs, args, flops, tables=(), raw=(), scratch=()):
    def kernel(*refs):
        t, r = len(tables), len(raw)
        operands = refs[t + r :]
        staged(
            functools.partial(body, *refs[t : t + r]), (len(args), len(outs)), refs[:t],
            *operands,
        )

    moved = sum(a.size * a.dtype.itemsize for a in args) + sum(
        o.size * jnp.dtype(o.dtype).itemsize for o in outs
    )
    return pl.pallas_call(
        kernel,
        out_shape=tuple(outs),
        in_specs=[pl.BlockSpec(memory_space=pltpu.SMEM)] * len(tables)
        + [ANYWHERE] * (len(raw) + len(args)),
        out_specs=tuple([ANYWHERE] * len(outs)),
        scratch_shapes=[pltpu.VMEM(a.shape, a.dtype) for a in args]
        + [pltpu.VMEM(o.shape, o.dtype) for o in outs]
        + [pltpu.SemaphoreType.DMA((len(args),)), pltpu.SemaphoreType.DMA((len(outs),))]
        + list(scratch),
        compiler_params=pltpu.CompilerParams(vmem_limit_bytes=60 << 20),
        cost_estimate=pl.CostEstimate(flops=flops, bytes_accessed=moved, transcendentals=0),
    )(*tables, *raw, *args)


def fold_symmetric(m):
    half = m.shape[0] // 2
    rows = lax.broadcasted_iota(jnp.int32, (half, 2 * half), 0)
    cols = lax.broadcasted_iota(jnp.int32, (half, 2 * half), 1)
    low = pltpu.roll(m[half:], half, 1)
    diagonal = jnp.sum(jnp.where(rows == cols, low, 0.0), axis=0, keepdims=True)
    mixed = jnp.where((cols > rows) & (cols < half), low, m[:half])
    return jnp.concatenate([mixed, jnp.broadcast_to(diagonal, (8, 2 * half))], axis=0)


def unfold_symmetric(f):
    half = f.shape[1] // 2
    rows = lax.broadcasted_iota(jnp.int32, (half, 2 * half), 0)
    cols = lax.broadcasted_iota(jnp.int32, (half, 2 * half), 1)
    mixed, diagonal = f[:half], f[half : half + 1]
    turned = jnp.transpose(jnp.concatenate([mixed, jnp.zeros_like(mixed)], axis=0))
    top = jnp.where((cols > rows) & (cols < half), turned[:half], mixed)
    last = jnp.where(cols > rows, mixed, jnp.where(cols < rows, turned[:half], diagonal))
    low = jnp.where(cols < half, turned[half:], pltpu.roll(last, half, 1))
    return jnp.concatenate([top, low], axis=0)


FOLDED = DK // 2 + 8
STATE = FOLDED + DK


def total_of(need, first):
    near = [need(first + n) for n in range(4)]
    state = (near[0][...] + near[1][...]) + (near[2][...] + near[3][...])
    return unfold_symmetric(state[:FOLDED]), state[FOLDED:]


def chunk(j):
    return slice(j * DK, (j + 1) * DK)


def prepare_body(tables, need, made, put):
    x, (low, high) = need(0), made
    rows = low.shape[0]
    low[...] = x[:rows].astype(F32)
    put(0)
    high[...] = x[rows:].astype(F32)


def upstream_body(tables, need, made, put):
    for h in range(HEADS):
        made[0][h] = need(0)[:, chunk(h)].astype(F32)


def project_body(slots, wk_hbm, wv_hbm, tables, need, made, put, w_buf, w_sem):
    (where,) = tables
    xb, k_out, v_out, tot = made
    cols = pl.ds(pl.multiple_of(where[len(where) - 1] * DK, DK), DK)
    weights = [
        pltpu.make_async_copy(w.at[:, cols], w_buf.at[:, chunk(n)], w_sem.at[n])
        for n, w in enumerate((wk_hbm, wv_hbm))
    ]
    for copy in weights:
        copy.start()
    for n, (slot, start) in enumerate(slots):
        piece = need(n)
        row = pl.multiple_of(where[slot] * DK + start, DK // 2)
        xb[pl.ds(row, piece.shape[0]), :] = piece[...].astype(BF16)
    put(0)
    for copy in weights:
        copy.wait()
    both = nn(xb[...], w_buf[...]).astype(BF16)
    k, v = both[:, :DK], both[:, DK:]
    k_out[...] = k
    v_out[...] = v
    put(1)
    put(2)
    rk = inv_norm(k)
    kn = k.astype(F32) * rk
    tot[:FOLDED] = fold_symmetric(fold_cols(tn(k, wide(kn * rk))))
    tot[FOLDED:] = fold_cols(tn(v, wide(kn)))


def states_body(wq_hbm, tables, need, made, put, w_buf, w_sem):
    (where,) = tables
    q_out, gram_out = made
    cols = pl.ds(pl.multiple_of(where[len(where) - 1] * DK, DK), DK)
    weight = pltpu.make_async_copy(wq_hbm.at[:, cols], w_buf, w_sem.at[0])
    weight.start()
    k_in = need(0)
    gram = jnp.zeros((DK, DK), F32)
    for j in range(CHUNKS):
        gram_out[j] = gram
        if j + 1 < CHUNKS:
            k = k_in[chunk(j), :]
            rk = inv_norm(k)
            gram = gram + fold_cols(tn(k, wide(k.astype(F32) * (rk * rk))))
    put(1)
    weight.wait()
    q_out[...] = nn(need(1)[...], w_buf[...]).astype(BF16)


def targets_body(tables, need, made, put):
    k_in, v_in, g_in = need(0), need(1), need(2)
    keep = causal(DK)
    cross = jnp.zeros((DK, DK), F32)
    for j in range(CHUNKS):
        k, v, g = k_in[chunk(j), :], v_in[chunk(j), :], g_in[j].astype(BF16)
        rk = inv_norm(k)
        scores = nt(g, v) * jnp.where(keep, across(rk), 0.0)
        made[0][j] = nn(twice_wide(g), tall(cross)) + nn(wide(scores), twice_tall(k))
        if j + 1 < CHUNKS:
            cross = cross + fold_cols(tn(v, wide(k.astype(F32) * rk)))


def solve_body(tables, need, made, put):
    (where,) = tables
    q_in, k_in, gram_in, part, g_in, damp_in = [need(n) for n in range(6)]
    gram_prior, cross_prior = total_of(need, 6)
    z_out, u_out, tot = made
    damp = damp_in[pl.ds(where[len(where) - 1], 1), :]
    keep = causal(DK)
    keys = [k_in[chunk(j), :] for j in range(CHUNKS)]
    systems = [system(k, gram_in[j] + gram_prior) for j, k in enumerate(keys)]
    cross_tall = tall(cross_prior)
    scale2, targets = [], []
    for j, k in enumerate(keys):
        rk = inv_norm(k)
        row = jnp.where(keep, across(rk * rk), 0.0)
        scale2.append(twice_tall(row))
        right = part[j] + nn(twice_wide(g_in[j].astype(BF16)), cross_tall)
        q = q_in[chunk(j), :]
        targets.append(jnp.concatenate([q.astype(F32) * inv_norm(q), right], axis=0))
    both = conjugate(targets, systems, scale2, damp)
    gram = jnp.zeros((DK, DK), F32)
    cross = jnp.zeros((DK, DK), F32)
    for j in range(CHUNKS):
        z, u = both[j][:DK], both[j][DK:]
        z_out[j] = z
        u_out[j] = u
        z_wide, u_wide = wide(z), wide(u)
        left = jnp.concatenate([u_wide, z_wide], axis=0)
        right = jnp.concatenate([z_wide, u_wide], axis=0)
        gram = gram + fold_rows(fold_cols(tn(left, right)))
        cross = cross + fold_cols(tn(g_in[j].astype(BF16), z_wide))
    tot[:FOLDED] = fold_symmetric(gram)
    tot[FOLDED:] = cross


def local_body(tables, need, made, put):
    q_in, k_in, v_in, g_in, z_in, u_in = [need(n) for n in range(6)]
    dq_out, dk_out, dv_out = made
    keep = causal(DK)
    for j in range(CHUNKS):
        q, u = q_in[chunk(j), :], u_in[j]
        rq = inv_norm(q)
        qn = q.astype(F32) * rq
        dq_out[j] = ((u - qn * rowsum(qn * u)) * rq).astype(BF16).astype(F32)
    put(0)
    gram = jnp.zeros((DK, DK), F32)
    cross = jnp.zeros((DK, DK), F32)
    for j in reversed(range(CHUNKS)):
        k, v = k_in[chunk(j), :], v_in[chunk(j), :]
        rk = inv_norm(k)
        row = jnp.where(keep, across(rk), 0.0)
        g = g_in[j].astype(BF16)
        scores = jnp.where(keep, nt(g, v), 0.0)
        u, z = u_in[j], z_in[j]
        u_wide, z_wide = wide(u), wide(z)
        kk = twice_wide(k)
        pair = nt(jnp.concatenate([u_wide, z_wide], axis=0), kk) * twice_tall(row)
        left = jnp.concatenate([scores - pair[:DK], -pair[DK:]], axis=0)
        right = jnp.concatenate([z_wide, u_wide], axis=0)
        dkn = fold_rows(fold_cols(tn(wide(left), right)))
        dkn = dkn + nn(twice_wide(v), tall(cross))
        dk_out[j] = dkn - rk * nn(kk, tall(gram))
        dv_out[j] = rk * nt(kk, wide(cross)) + tn(tall(pair[DK:]), twice_tall(g))
        if j:
            swapped = jnp.concatenate([u_wide, z_wide], axis=0)
            gram = gram + fold_rows(fold_cols(tn(swapped, right)))
            cross = cross + fold_cols(tn(g, z_wide))


def grads_body(seq, tables, need, made, put, dk_buf, dw_buf, out):
    (place,) = tables
    k_in, v_in, dk_part, dv_part, dq_in = [need(n) for n in range(5)]
    gram_after, cross_after = total_of(need, 5)
    gram_tall, cross_tall, cross_wide = tall(gram_after), tall(cross_after), wide(cross_after)
    for j in range(CHUNKS):
        k, v = k_in[chunk(j), :], v_in[chunk(j), :]
        rk = inv_norm(k)
        kn = k.astype(F32) * rk
        kk = twice_wide(k)
        dkn = dk_part[j] + nn(twice_wide(v), cross_tall) - rk * nn(kk, gram_tall)
        dk = ((dkn - kn * rowsum(kn * dkn)) * rk).astype(BF16)
        dk_buf[chunk(j), :] = dk
        out[j, :DK] = dk.astype(F32)
        dv = dv_part[j] + rk * nt(kk, cross_wide)
        out[j, DK : 2 * DK] = dv.astype(BF16).astype(F32)
        out[j, 2 * DK :] = dq_in[j]
    dw_buf[...] = jnp.transpose(tn(dk_buf[...], need(9)[...]))
    rows = made[0].shape[0]
    for step in range(seq):
        start = pl.multiple_of(lax.rem(place[0] + step, seq) * rows, rows)
        made[step][...] = dw_buf[pl.ds(start, rows), :]
        put(step)
    for step in range(CHUNKS):
        made[seq + step][...] = out[lax.rem(place[1] + step, CHUNKS)]
        put(seq + step)


def input_grad_body(tables, need, made, put, *sides):
    (place,) = tables
    for step in range(HEADS):
        piece = need(step)
        head = lax.rem(place[1] + HEADS - step, HEADS)
        cols = pl.ds(pl.multiple_of(head * DK, DK), DK)
        for n, side in enumerate(sides):
            side[:, cols] = piece[chunk(n), :].astype(BF16)
    total = nt(sides[0][...], need(HEADS)[...])
    for n in (1, 2):
        total = total + nt(sides[n][...], need(HEADS + n)[...])
    made[0][...] = total.astype(BF16)


def shift(x, axis, by, wrap):
    size = lax.axis_size(axis)
    pairs = [(i, (i + by) % size) for i in range(size) if wrap or 0 <= i + by < size]
    return lax.ppermute(x, axis, pairs)


def exclusive(total, sign):
    one, two = shift(total, "z", sign, False), shift(total, "z", 2 * sign, False)
    third = total + one + two
    return one, two, shift(third, "z", 3 * sign, False), shift(third, "z", 6 * sign, False)


def exchange(x, axis):
    return lax.all_to_all(x, axis, 0, 0)


def gather_plane(low, high):
    y, core = lax.axis_index("y"), lax.axis_index("core")
    rows = low.shape[0]
    prev_low = shift(low, "y", 1, True)
    next_high = shift(high, "y", -1, True)
    prev_high = shift(high, "y", 1, True)
    next_low = shift(low, "y", -1, True)
    far_low = shift(prev_low, "y", 1, True)
    far_high = shift(next_high, "y", -1, True)
    pieces = [(low, 0, 0), (high, 0, rows)]
    pieces += [(shift(low, "core", 1, True), 4, 0), (shift(high, "core", 1, True), 4, rows)]
    for piece, slot, start in (
        (prev_low, 1, 0), (next_high, 2, rows), (prev_high, 1, rows), (next_low, 2, 0),
        (far_low, 3, 0), (far_high, 3, rows),
    ):
        pieces.append((piece, slot, start))
        pieces.append((shift(piece, "core", 1, True), slot + 4, start))
    ysize = lax.axis_size("y")
    places = [
        ((y + step) % ysize) * 2 + c for c in (core, 1 - core) for step in (0, -1, 1, 2)
    ] + [y * 2 + core]
    return pieces, jnp.stack(places).astype(jnp.int32)


def on_device(inputs, w_query, w_key, w_value, damping, grad_out):
    mine = inputs[0]
    tokens, width = mine.shape
    plane = CHUNKS * tokens
    blocks = shaped(CHUNKS, tokens, DK)
    brick = shaped(plane, DK, dtype=BF16)
    state = shaped(STATE, DK)
    unit = 2 * plane * DK * DK

    half = shaped(tokens // 2, width)
    low, high = call(prepare_body, [half, half], [mine], 0)
    pieces, where = gather_plane(low, high)
    slots = tuple((slot, start) for _, slot, start in pieces)
    pieces = [p for p, _, _ in pieces]
    (upstream,) = call(upstream_body, [shaped(HEADS, tokens, DK)], [grad_out[0]], 0)
    xb, k, v, first_tot = call(
        functools.partial(project_body, slots),
        [shaped(plane, width, dtype=BF16), brick, brick, state],
        pieces, unit * 28, tables=[where], raw=[w_key, w_value],
        scratch=[pltpu.VMEM((width, 2 * DK), BF16), pltpu.SemaphoreType.DMA((2,))],
    )
    prior = exclusive(first_tot, 1)
    upstream, _ = lax.optimization_barrier((upstream, first_tot))
    g = exchange(upstream, PLANE)
    q, gram_pre = call(
        states_body, [brick, shaped(CHUNKS, DK, DK)], [k, xb], unit * 10,
        tables=[where], raw=[w_query],
        scratch=[pltpu.VMEM((width, DK), BF16), pltpu.SemaphoreType.DMA((1,))],
    )
    (part,) = call(targets_body, [blocks], [k, v, g], unit * 8)

    z, u, second_tot = call(
        solve_body, [blocks, blocks, state],
        [q, k, gram_pre, part, g, damping, *prior], unit * 40, tables=[where],
    )
    after = exclusive(second_tot, -1)
    dq, dk_part, dv_part = call(local_body, [blocks, blocks, blocks], [q, k, v, g, z, u], unit * 30)
    seq = lax.axis_size("seq")
    ctx = ("z", "y", "core")
    spread = lax.axis_size(ctx)
    rows = width // (seq * spread)
    place = jnp.stack(
        [lax.axis_index("seq"), lax.axis_index("y") * 2 + lax.axis_index("core")]
    ).astype(jnp.int32)
    pieces = call(
        functools.partial(grads_body, seq),
        [shaped(width // seq, DK)] * seq + [shaped(3 * tokens, DK)] * CHUNKS,
        [k, v, dk_part, dv_part, dq, *after, xb], unit * 14, tables=[place],
        scratch=[
            pltpu.VMEM((plane, DK), BF16), pltpu.VMEM((width, DK), F32),
            pltpu.VMEM((CHUNKS, 3 * tokens, DK), F32),
        ],
    )
    dw, dkv = pieces[:seq], pieces[seq:]
    dw = sum((shift(part, "seq", step, True) for step, part in enumerate(dw) if step), dw[0])
    dkv = [shift(p, PLANE, step, True) if step else p for step, p in enumerate(dkv)]
    dw = exchange(dw.reshape(spread, rows, DK), ctx)
    dw = dw.reshape(spread // HEADS, HEADS, rows, DK)
    grad_weights = jnp.sum(dw, axis=0).transpose(1, 0, 2).reshape(rows, HEADS * DK)

    (grad_inputs,) = call(
        input_grad_body, [shaped(tokens, width, dtype=BF16)],
        [*dkv, w_key, w_value, w_query], unit * 24, tables=[place],
        scratch=[pltpu.VMEM((tokens, width), BF16)] * 3,
    )
    return (grad_inputs[None], grad_weights)


def solution(mesh):
    grid = Mesh(mesh.devices.reshape(4, 8, 4, 2), ("seq", "z", "y", "core"))
    ctx = ("z", "y", "core")
    in_specs = (P("seq", ctx, None), P(), P(), P(), P(), P("seq", ctx, None))
    out_specs = (P("seq", ctx, None), P(("seq",) + ctx, None))

    return jax.shard_map(on_device, mesh=grid, in_specs=in_specs, out_specs=out_specs, check_vma=False)
```

```python
import functools

import jax
import jax.numpy as jnp
from jax import lax
from jax.experimental import pallas as pl
from jax.experimental.pallas import tpu as pltpu
from jax.sharding import Mesh, PartitionSpec as P


ITERS = 2
EPSILON = 1e-06
F32 = jnp.float32
BF16 = jnp.bfloat16
HEADS = 8
DK = 128
CHUNKS = 8
PLANE = ("y", "core")


def halves(x):
    hi = x.astype(BF16)
    return hi, (x - hi.astype(F32)).astype(BF16)


def nn(a, b):
    return lax.dot_general(a, b, (((1,), (0,)), ((), ())), preferred_element_type=F32)


def nt(a, b):
    return lax.dot_general(a, b, (((1,), (1,)), ((), ())), preferred_element_type=F32)


def tn(a, b):
    return lax.dot_general(a, b, (((0,), (0,)), ((), ())), preferred_element_type=F32)


def wide(x):
    return jnp.concatenate(halves(x), axis=1)


def tall(x):
    return jnp.concatenate(halves(x), axis=0)


def twice_wide(b):
    return jnp.concatenate([b, b], axis=1)


def twice_tall(b):
    return jnp.concatenate([b, b], axis=0)


def fold_cols(m):
    half = m.shape[1] // 2
    return m[:, :half] + m[:, half:]


def fold_rows(m):
    half = m.shape[0] // 2
    return m[:half] + m[half:]


def rowsum(x):
    return jnp.sum(x, axis=-1, keepdims=True)


def causal(size):
    rows = lax.broadcasted_iota(jnp.int32, (size, size), 0)
    cols = lax.broadcasted_iota(jnp.int32, (size, size), 1)
    return rows >= cols


def inv_norm(block):
    wide_block = block.astype(F32)
    return lax.rsqrt(rowsum(wide_block * wide_block) + EPSILON)


def across(column):
    size = column.shape[0]
    return jnp.transpose(jnp.broadcast_to(column, (size, size)))


def system(key, gram):
    turned = jnp.transpose(key)
    hi, lo = halves(gram)
    upper = jnp.concatenate([turned, hi, lo], axis=1)
    lower = jnp.concatenate([turned, hi, jnp.zeros_like(lo)], axis=1)
    return jnp.concatenate([upper, lower], axis=0), twice_tall(key)


def apply_all(vectors, systems, scale2, damp):
    firsts = [nn(wide(p), s[0]) for p, s in zip(vectors, systems)]
    inner = [wide(f[:, :DK] * m) for f, m in zip(firsts, scale2)]
    return [
        nn(i, s[1]) + (f[:, DK : 2 * DK] + f[:, 2 * DK :]) + damp * p
        for i, s, f, p in zip(inner, systems, firsts, vectors)
    ]


def conjugate(targets, systems, scale2, damp):
    residual = list(targets)
    direction = list(targets)
    norm_now = [rowsum(r * r) for r in residual]
    solution = None
    for sweep in range(ITERS):
        image = apply_all(direction, systems, scale2, damp)
        step = [n / (rowsum(p * w) + EPSILON) for n, p, w in zip(norm_now, direction, image)]
        moved = [a * p for a, p in zip(step, direction)]
        solution = moved if solution is None else [x + m for x, m in zip(solution, moved)]
        if sweep + 1 < ITERS:
            residual = [r - a * w for r, a, w in zip(residual, step, image)]
            norm_next = [rowsum(r * r) for r in residual]
            direction = [
                r + n / (o + EPSILON) * p
                for r, n, o, p in zip(residual, norm_next, norm_now, direction)
            ]
            norm_now = norm_next
    return solution


def staged(body, counts, tables, *refs):
    n_in, n_out = counts
    sources, refs = refs[:n_in], refs[n_in:]
    targets, refs = refs[:n_out], refs[n_out:]
    held, refs = refs[:n_in], refs[n_in:]
    made, (in_sems, out_sems, *rest) = refs[:n_out], refs[n_out:]
    loads = [
        pltpu.make_async_copy(s, h, in_sems.at[n]) for n, (s, h) in enumerate(zip(sources, held))
    ]
    stores = [
        pltpu.make_async_copy(m, t, out_sems.at[n]) for n, (m, t) in enumerate(zip(made, targets))
    ]
    for load in loads:
        load.start()
    arrived, sent = set(), set()

    def need(n):
        if n not in arrived:
            arrived.add(n)
            loads[n].wait()
        return held[n]

    def put(n):
        sent.add(n)
        stores[n].start()

    body(tables, need, made, put, *rest)
    for n in range(n_in):
        need(n)
    for n in range(n_out):
        if n not in sent:
            put(n)
    for store in stores:
        store.wait()


def shaped(*dims, dtype=F32):
    return jax.ShapeDtypeStruct(dims, dtype)


ANYWHERE = pl.BlockSpec(memory_space=pl.ANY)


def call(body, outs, args, flops, tables=(), raw=(), scratch=()):
    def kernel(*refs):
        t, r = len(tables), len(raw)
        operands = refs[t + r :]
        staged(
            functools.partial(body, *refs[t : t + r]), (len(args), len(outs)), refs[:t],
            *operands,
        )

    moved = sum(a.size * a.dtype.itemsize for a in args) + sum(
        o.size * jnp.dtype(o.dtype).itemsize for o in outs
    )
    return pl.pallas_call(
        kernel,
        out_shape=tuple(outs),
        in_specs=[pl.BlockSpec(memory_space=pltpu.SMEM)] * len(tables)
        + [ANYWHERE] * (len(raw) + len(args)),
        out_specs=tuple([ANYWHERE] * len(outs)),
        scratch_shapes=[pltpu.VMEM(a.shape, a.dtype) for a in args]
        + [pltpu.VMEM(o.shape, o.dtype) for o in outs]
        + [pltpu.SemaphoreType.DMA((len(args),)), pltpu.SemaphoreType.DMA((len(outs),))]
        + list(scratch),
        compiler_params=pltpu.CompilerParams(vmem_limit_bytes=60 << 20),
        cost_estimate=pl.CostEstimate(flops=flops, bytes_accessed=moved, transcendentals=0),
    )(*tables, *raw, *args)


def fold_symmetric(m):
    half = m.shape[0] // 2
    rows = lax.broadcasted_iota(jnp.int32, (half, 2 * half), 0)
    cols = lax.broadcasted_iota(jnp.int32, (half, 2 * half), 1)
    low = pltpu.roll(m[half:], half, 1)
    diagonal = jnp.sum(jnp.where(rows == cols, low, 0.0), axis=0, keepdims=True)
    mixed = jnp.where((cols > rows) & (cols < half), low, m[:half])
    return jnp.concatenate([mixed, jnp.broadcast_to(diagonal, (8, 2 * half))], axis=0)


def unfold_symmetric(f):
    half = f.shape[1] // 2
    rows = lax.broadcasted_iota(jnp.int32, (half, 2 * half), 0)
    cols = lax.broadcasted_iota(jnp.int32, (half, 2 * half), 1)
    mixed, diagonal = f[:half], f[half : half + 1]
    turned = jnp.transpose(jnp.concatenate([mixed, jnp.zeros_like(mixed)], axis=0))
    top = jnp.where((cols > rows) & (cols < half), turned[:half], mixed)
    last = jnp.where(cols > rows, mixed, jnp.where(cols < rows, turned[:half], diagonal))
    low = jnp.where(cols < half, turned[half:], pltpu.roll(last, half, 1))
    return jnp.concatenate([top, low], axis=0)


FOLDED = DK // 2 + 8
STATE = FOLDED + DK


def total_of(need, first):
    near = [need(first + n) for n in range(4)]
    state = (near[0][...] + near[1][...]) + (near[2][...] + near[3][...])
    return unfold_symmetric(state[:FOLDED]), state[FOLDED:]


def chunk(j):
    return slice(j * DK, (j + 1) * DK)


def prepare_body(tables, need, made, put):
    x, (low, high) = need(0), made
    rows = low.shape[0]
    low[...] = x[:rows].astype(F32)
    put(0)
    high[...] = x[rows:].astype(F32)


def upstream_body(tables, need, made, put):
    for h in range(HEADS):
        made[0][h] = need(0)[:, chunk(h)].astype(F32)


def project_body(slots, wk_hbm, wv_hbm, tables, need, made, put, w_buf, w_sem):
    (where,) = tables
    xb, k_out, v_out, tot = made
    cols = pl.ds(pl.multiple_of(where[len(where) - 1] * DK, DK), DK)
    weights = [
        pltpu.make_async_copy(w.at[:, cols], w_buf.at[:, chunk(n)], w_sem.at[n])
        for n, w in enumerate((wk_hbm, wv_hbm))
    ]
    for copy in weights:
        copy.start()
    for n, (slot, start) in enumerate(slots):
        piece = need(n)
        row = pl.multiple_of(where[slot] * DK + start, DK // 2)
        xb[pl.ds(row, piece.shape[0]), :] = piece[...].astype(BF16)
    put(0)
    for copy in weights:
        copy.wait()
    both = nn(xb[...], w_buf[...]).astype(BF16)
    k, v = both[:, :DK], both[:, DK:]
    k_out[...] = k
    v_out[...] = v
    put(1)
    put(2)
    rk = inv_norm(k)
    kn = k.astype(F32) * rk
    tot[:FOLDED] = fold_symmetric(fold_cols(tn(k, wide(kn * rk))))
    tot[FOLDED:] = fold_cols(tn(v, wide(kn)))


def states_body(wq_hbm, tables, need, made, put, w_buf, w_sem):
    (where,) = tables
    q_out, gram_out = made
    cols = pl.ds(pl.multiple_of(where[len(where) - 1] * DK, DK), DK)
    weight = pltpu.make_async_copy(wq_hbm.at[:, cols], w_buf, w_sem.at[0])
    weight.start()
    k_in = need(0)
    gram = jnp.zeros((DK, DK), F32)
    for j in range(CHUNKS):
        gram_out[j] = gram
        if j + 1 < CHUNKS:
            k = k_in[chunk(j), :]
            rk = inv_norm(k)
            gram = gram + fold_cols(tn(k, wide(k.astype(F32) * (rk * rk))))
    put(1)
    weight.wait()
    q_out[...] = nn(need(1)[...], w_buf[...]).astype(BF16)


def targets_body(tables, need, made, put):
    k_in, v_in, g_in = need(0), need(1), need(2)
    keep = causal(DK)
    cross = jnp.zeros((DK, DK), F32)
    for j in range(CHUNKS):
        k, v, g = k_in[chunk(j), :], v_in[chunk(j), :], g_in[j].astype(BF16)
        rk = inv_norm(k)
        scores = nt(g, v) * jnp.where(keep, across(rk), 0.0)
        made[0][j] = nn(twice_wide(g), tall(cross)) + nn(wide(scores), twice_tall(k))
        if j + 1 < CHUNKS:
            cross = cross + fold_cols(tn(v, wide(k.astype(F32) * rk)))


def solve_body(tables, need, made, put):
    (where,) = tables
    q_in, k_in, gram_in, part, g_in, damp_in = [need(n) for n in range(6)]
    gram_prior, cross_prior = total_of(need, 6)
    z_out, u_out, tot = made
    damp = damp_in[pl.ds(where[len(where) - 1], 1), :]
    keep = causal(DK)
    keys = [k_in[chunk(j), :] for j in range(CHUNKS)]
    systems = [system(k, gram_in[j] + gram_prior) for j, k in enumerate(keys)]
    cross_tall = tall(cross_prior)
    scale2, targets = [], []
    for j, k in enumerate(keys):
        rk = inv_norm(k)
        row = jnp.where(keep, across(rk * rk), 0.0)
        scale2.append(twice_tall(row))
        right = part[j] + nn(twice_wide(g_in[j].astype(BF16)), cross_tall)
        q = q_in[chunk(j), :]
        targets.append(jnp.concatenate([q.astype(F32) * inv_norm(q), right], axis=0))
    both = conjugate(targets, systems, scale2, damp)
    gram = jnp.zeros((DK, DK), F32)
    cross = jnp.zeros((DK, DK), F32)
    for j in range(CHUNKS):
        z, u = both[j][:DK], both[j][DK:]
        z_out[j] = z
        u_out[j] = u
        z_wide, u_wide = wide(z), wide(u)
        left = jnp.concatenate([u_wide, z_wide], axis=0)
        right = jnp.concatenate([z_wide, u_wide], axis=0)
        gram = gram + fold_rows(fold_cols(tn(left, right)))
        cross = cross + fold_cols(tn(g_in[j].astype(BF16), z_wide))
    tot[:FOLDED] = fold_symmetric(gram)
    tot[FOLDED:] = cross


def local_body(tables, need, made, put):
    q_in, k_in, v_in, g_in, z_in, u_in = [need(n) for n in range(6)]
    dq_out, dk_out, dv_out = made
    keep = causal(DK)
    for j in range(CHUNKS):
        q, u = q_in[chunk(j), :], u_in[j]
        rq = inv_norm(q)
        qn = q.astype(F32) * rq
        dq_out[j] = ((u - qn * rowsum(qn * u)) * rq).astype(BF16).astype(F32)
    put(0)
    gram = jnp.zeros((DK, DK), F32)
    cross = jnp.zeros((DK, DK), F32)
    for j in reversed(range(CHUNKS)):
        k, v = k_in[chunk(j), :], v_in[chunk(j), :]
        rk = inv_norm(k)
        row = jnp.where(keep, across(rk), 0.0)
        g = g_in[j].astype(BF16)
        scores = jnp.where(keep, nt(g, v), 0.0)
        u, z = u_in[j], z_in[j]
        u_wide, z_wide = wide(u), wide(z)
        kk = twice_wide(k)
        pair = nt(jnp.concatenate([u_wide, z_wide], axis=0), kk) * twice_tall(row)
        left = jnp.concatenate([scores - pair[:DK], -pair[DK:]], axis=0)
        right = jnp.concatenate([z_wide, u_wide], axis=0)
        dkn = fold_rows(fold_cols(tn(wide(left), right)))
        dkn = dkn + nn(twice_wide(v), tall(cross))
        dk_out[j] = dkn - rk * nn(kk, tall(gram))
        dv_out[j] = rk * nt(kk, wide(cross)) + tn(tall(pair[DK:]), twice_tall(g))
        if j:
            swapped = jnp.concatenate([u_wide, z_wide], axis=0)
            gram = gram + fold_rows(fold_cols(tn(swapped, right)))
            cross = cross + fold_cols(tn(g, z_wide))


def grads_body(seq, tables, need, made, put, dk_buf, dw_buf, out):
    (place,) = tables
    k_in, v_in, dk_part, dv_part, dq_in = [need(n) for n in range(5)]
    gram_after, cross_after = total_of(need, 5)
    gram_tall, cross_tall, cross_wide = tall(gram_after), tall(cross_after), wide(cross_after)
    for j in range(CHUNKS):
        k, v = k_in[chunk(j), :], v_in[chunk(j), :]
        rk = inv_norm(k)
        kn = k.astype(F32) * rk
        kk = twice_wide(k)
        dkn = dk_part[j] + nn(twice_wide(v), cross_tall) - rk * nn(kk, gram_tall)
        dk = ((dkn - kn * rowsum(kn * dkn)) * rk).astype(BF16)
        dk_buf[chunk(j), :] = dk
        out[j, :DK] = dk.astype(F32)
        dv = dv_part[j] + rk * nt(kk, cross_wide)
        out[j, DK : 2 * DK] = dv.astype(BF16).astype(F32)
        out[j, 2 * DK :] = dq_in[j]
    dw_buf[...] = jnp.transpose(tn(dk_buf[...], need(9)[...]))
    rows = made[0].shape[0]
    for step in range(seq):
        start = pl.multiple_of(lax.rem(place[0] + step, seq) * rows, rows)
        made[step][...] = dw_buf[pl.ds(start, rows), :]
        put(step)
    for step in range(CHUNKS):
        made[seq + step][...] = out[lax.rem(place[1] + step, CHUNKS)]
        put(seq + step)


def input_grad_body(tables, need, made, put, *sides):
    (place,) = tables
    for step in range(HEADS):
        piece = need(step)
        head = lax.rem(place[1] + HEADS - step, HEADS)
        cols = pl.ds(pl.multiple_of(head * DK, DK), DK)
        for n, side in enumerate(sides):
            side[:, cols] = piece[chunk(n), :].astype(BF16)
    total = nt(sides[0][...], need(HEADS)[...])
    for n in (1, 2):
        total = total + nt(sides[n][...], need(HEADS + n)[...])
    made[0][...] = total.astype(BF16)


def shift(x, axis, by, wrap):
    size = lax.axis_size(axis)
    pairs = [(i, (i + by) % size) for i in range(size) if wrap or 0 <= i + by < size]
    return lax.ppermute(x, axis, pairs)


def exclusive(total, sign):
    one, two = shift(total, "z", sign, False), shift(total, "z", 2 * sign, False)
    third = total + one + two
    return one, two, shift(third, "z", 3 * sign, False), shift(third, "z", 6 * sign, False)


def exchange(x, axis):
    return lax.all_to_all(x, axis, 0, 0)


def gather_plane(low, high):
    y, core = lax.axis_index("y"), lax.axis_index("core")
    rows = low.shape[0]
    prev_low = shift(low, "y", 1, True)
    next_high = shift(high, "y", -1, True)
    prev_high = shift(high, "y", 1, True)
    next_low = shift(low, "y", -1, True)
    far_low = shift(prev_low, "y", 1, True)
    far_high = shift(next_high, "y", -1, True)
    pieces = [(low, 0, 0), (high, 0, rows)]
    pieces += [(shift(low, "core", 1, True), 4, 0), (shift(high, "core", 1, True), 4, rows)]
    near = (
        (prev_low, 1, 0), (next_high, 2, rows), (prev_high, 1, rows), (next_low, 2, 0),
        (far_low, 3, 0), (far_high, 3, rows),
    )
    for piece, slot, start in near:
        pieces.append((piece, slot, start))
        pieces.append((shift(piece, "core", 1, True), slot + 4, start))
    ysize = lax.axis_size("y")
    places = [
        ((y + step) % ysize) * 2 + c for c in (core, 1 - core) for step in (0, -1, 1, 2)
    ] + [y * 2 + core]
    return pieces, jnp.stack(places).astype(jnp.int32)


def on_device(inputs, w_query, w_key, w_value, damping, grad_out):
    mine = inputs[0]
    tokens, width = mine.shape
    plane = CHUNKS * tokens
    blocks = shaped(CHUNKS, tokens, DK)
    brick = shaped(plane, DK, dtype=BF16)
    state = shaped(STATE, DK)
    unit = 2 * plane * DK * DK

    half = shaped(tokens // 2, width)
    low, high = call(prepare_body, [half, half], [mine], 0)
    pieces, where = gather_plane(low, high)
    slots = tuple((slot, start) for _, slot, start in pieces)
    pieces = [p for p, _, _ in pieces]
    (upstream,) = call(upstream_body, [shaped(HEADS, tokens, DK)], [grad_out[0]], 0)
    xb, k, v, first_tot = call(
        functools.partial(project_body, slots),
        [shaped(plane, width, dtype=BF16), brick, brick, state],
        pieces, unit * 28, tables=[where], raw=[w_key, w_value],
        scratch=[pltpu.VMEM((width, 2 * DK), BF16), pltpu.SemaphoreType.DMA((2,))],
    )
    prior = exclusive(first_tot, 1)
    g = exchange(upstream, PLANE)
    q, gram_pre = call(
        states_body, [brick, shaped(CHUNKS, DK, DK)], [k, xb], unit * 10,
        tables=[where], raw=[w_query],
        scratch=[pltpu.VMEM((width, DK), BF16), pltpu.SemaphoreType.DMA((1,))],
    )
    (part,) = call(targets_body, [blocks], [k, v, g], unit * 8)

    z, u, second_tot = call(
        solve_body, [blocks, blocks, state],
        [q, k, gram_pre, part, g, damping, *prior], unit * 40, tables=[where],
    )
    after = exclusive(second_tot, -1)
    dq, dk_part, dv_part = call(local_body, [blocks, blocks, blocks], [q, k, v, g, z, u], unit * 30)
    seq = lax.axis_size("seq")
    ctx = ("z", "y", "core")
    spread = lax.axis_size(ctx)
    rows = width // (seq * spread)
    place = jnp.stack(
        [lax.axis_index("seq"), lax.axis_index("y") * 2 + lax.axis_index("core")]
    ).astype(jnp.int32)
    pieces = call(
        functools.partial(grads_body, seq),
        [shaped(width // seq, DK)] * seq + [shaped(3 * tokens, DK)] * CHUNKS,
        [k, v, dk_part, dv_part, dq, *after, xb], unit * 14, tables=[place],
        scratch=[
            pltpu.VMEM((plane, DK), BF16), pltpu.VMEM((width, DK), F32),
            pltpu.VMEM((CHUNKS, 3 * tokens, DK), F32),
        ],
    )
    dw, dkv = pieces[:seq], pieces[seq:]
    dw = sum((shift(part, "seq", step, True) for step, part in enumerate(dw) if step), dw[0])
    dkv = [shift(p, PLANE, step, True) if step else p for step, p in enumerate(dkv)]
    dw = exchange(dw.reshape(spread, rows, DK), ctx)
    dw = dw.reshape(spread // HEADS, HEADS, rows, DK)
    grad_weights = jnp.sum(dw, axis=0).transpose(1, 0, 2).reshape(rows, HEADS * DK)

    (grad_inputs,) = call(
        input_grad_body, [shaped(tokens, width, dtype=BF16)],
        [*dkv, w_key, w_value, w_query], unit * 24, tables=[place],
        scratch=[pltpu.VMEM((tokens, width), BF16)] * 3,
    )
    return (grad_inputs[None], grad_weights)


def solution(mesh):
    grid = Mesh(mesh.devices.reshape(4, 8, 4, 2), ("seq", "z", "y", "core"))
    ctx = ("z", "y", "core")
    in_specs = (P("seq", ctx, None), P(), P(), P(), P(), P("seq", ctx, None))
    out_specs = (P("seq", ctx, None), P(("seq",) + ctx, None))

    return jax.shard_map(on_device, mesh=grid, in_specs=in_specs, out_specs=out_specs, check_vma=False)
```

```python
import functools

import jax
import jax.numpy as jnp
from jax import lax
from jax.experimental import pallas as pl
from jax.experimental.pallas import tpu as pltpu
from jax.sharding import Mesh, PartitionSpec as P


ITERS = 2
EPSILON = 1e-06
F32 = jnp.float32
BF16 = jnp.bfloat16
HEADS = 8
DK = 128
CHUNKS = 8
PLANE = ("y", "core")


def halves(x):
    hi = x.astype(BF16)
    return hi, (x - hi.astype(F32)).astype(BF16)


def nn(a, b):
    return lax.dot_general(a, b, (((1,), (0,)), ((), ())), preferred_element_type=F32)


def nt(a, b):
    return lax.dot_general(a, b, (((1,), (1,)), ((), ())), preferred_element_type=F32)


def tn(a, b):
    return lax.dot_general(a, b, (((0,), (0,)), ((), ())), preferred_element_type=F32)


def wide(x):
    return jnp.concatenate(halves(x), axis=1)


def tall(x):
    return jnp.concatenate(halves(x), axis=0)


def twice_wide(b):
    return jnp.concatenate([b, b], axis=1)


def twice_tall(b):
    return jnp.concatenate([b, b], axis=0)


def fold_cols(m):
    half = m.shape[1] // 2
    return m[:, :half] + m[:, half:]


def fold_rows(m):
    half = m.shape[0] // 2
    return m[:half] + m[half:]


def rowsum(x):
    return jnp.sum(x, axis=-1, keepdims=True)


def causal(size):
    rows = lax.broadcasted_iota(jnp.int32, (size, size), 0)
    cols = lax.broadcasted_iota(jnp.int32, (size, size), 1)
    return rows >= cols


def inv_norm(block):
    wide_block = block.astype(F32)
    return lax.rsqrt(rowsum(wide_block * wide_block) + EPSILON)


def across(column):
    size = column.shape[0]
    return jnp.transpose(jnp.broadcast_to(column, (size, size)))


def system(key, gram):
    turned = jnp.transpose(key)
    hi, lo = halves(gram)
    upper = jnp.concatenate([turned, hi, lo], axis=1)
    lower = jnp.concatenate([turned, hi, jnp.zeros_like(lo)], axis=1)
    return jnp.concatenate([upper, lower], axis=0), twice_tall(key)


def apply_all(vectors, systems, scale2, damp):
    firsts = [nn(wide(p), s[0]) for p, s in zip(vectors, systems)]
    inner = [wide(f[:, :DK] * m) for f, m in zip(firsts, scale2)]
    return [
        nn(i, s[1]) + (f[:, DK : 2 * DK] + f[:, 2 * DK :]) + damp * p
        for i, s, f, p in zip(inner, systems, firsts, vectors)
    ]


def conjugate(targets, systems, scale2, damp):
    residual = list(targets)
    direction = list(targets)
    norm_now = [rowsum(r * r) for r in residual]
    solution = None
    for sweep in range(ITERS):
        image = apply_all(direction, systems, scale2, damp)
        step = [n / (rowsum(p * w) + EPSILON) for n, p, w in zip(norm_now, direction, image)]
        moved = [a * p for a, p in zip(step, direction)]
        solution = moved if solution is None else [x + m for x, m in zip(solution, moved)]
        if sweep + 1 < ITERS:
            residual = [r - a * w for r, a, w in zip(residual, step, image)]
            norm_next = [rowsum(r * r) for r in residual]
            direction = [
                r + n / (o + EPSILON) * p
                for r, n, o, p in zip(residual, norm_next, norm_now, direction)
            ]
            norm_now = norm_next
    return solution


def staged(body, counts, parts, tables, *refs):
    n_in, n_out = counts
    sources, refs = refs[:n_in], refs[n_in:]
    targets, refs = refs[:n_out], refs[n_out:]
    held, refs = refs[:n_in], refs[n_in:]
    made, (in_sems, out_sems, *rest) = refs[:n_out], refs[n_out:]
    loads = [
        pltpu.make_async_copy(s.at[part] if part else s, h, in_sems.at[n])
        for n, (s, h, part) in enumerate(zip(sources, held, parts))
    ]
    stores = [
        pltpu.make_async_copy(m, t, out_sems.at[n]) for n, (m, t) in enumerate(zip(made, targets))
    ]
    for load in loads:
        load.start()
    arrived, sent = set(), set()

    def need(n):
        if n not in arrived:
            arrived.add(n)
            loads[n].wait()
        return held[n]

    def put(n):
        sent.add(n)
        stores[n].start()

    body(tables, need, made, put, *rest)
    for n in range(n_in):
        need(n)
    for n in range(n_out):
        if n not in sent:
            put(n)
    for store in stores:
        store.wait()


def shaped(*dims, dtype=F32):
    return jax.ShapeDtypeStruct(dims, dtype)


ANYWHERE = pl.BlockSpec(memory_space=pl.ANY)


def call(body, outs, args, flops, tables=(), raw=(), scratch=()):
    parts = [a[1] if isinstance(a, tuple) else None for a in args]
    args = [a[0] if isinstance(a, tuple) else a for a in args]
    held = [
        (p.stop - p.start, *a.shape[1:]) if p else a.shape for a, p in zip(args, parts)
    ]

    def kernel(*refs):
        t, r = len(tables), len(raw)
        operands = refs[t + r :]
        staged(
            functools.partial(body, *refs[t : t + r]), (len(args), len(outs)), parts, refs[:t],
            *operands,
        )

    moved = sum(a.size * a.dtype.itemsize for a in args) + sum(
        o.size * jnp.dtype(o.dtype).itemsize for o in outs
    )
    return pl.pallas_call(
        kernel,
        out_shape=tuple(outs),
        in_specs=[pl.BlockSpec(memory_space=pltpu.SMEM)] * len(tables)
        + [ANYWHERE] * (len(raw) + len(args)),
        out_specs=tuple([ANYWHERE] * len(outs)),
        scratch_shapes=[pltpu.VMEM(h, a.dtype) for h, a in zip(held, args)]
        + [pltpu.VMEM(o.shape, o.dtype) for o in outs]
        + [pltpu.SemaphoreType.DMA((len(args),)), pltpu.SemaphoreType.DMA((len(outs),))]
        + list(scratch),
        compiler_params=pltpu.CompilerParams(vmem_limit_bytes=60 << 20),
        cost_estimate=pl.CostEstimate(flops=flops, bytes_accessed=moved, transcendentals=0),
    )(*tables, *raw, *args)


def fold_symmetric(m):
    half = m.shape[0] // 2
    rows = lax.broadcasted_iota(jnp.int32, (half, 2 * half), 0)
    cols = lax.broadcasted_iota(jnp.int32, (half, 2 * half), 1)
    low = pltpu.roll(m[half:], half, 1)
    diagonal = jnp.sum(jnp.where(rows == cols, low, 0.0), axis=0, keepdims=True)
    mixed = jnp.where((cols > rows) & (cols < half), low, m[:half])
    return jnp.concatenate([mixed, jnp.broadcast_to(diagonal, (8, 2 * half))], axis=0)


def unfold_symmetric(f):
    half = f.shape[1] // 2
    rows = lax.broadcasted_iota(jnp.int32, (half, 2 * half), 0)
    cols = lax.broadcasted_iota(jnp.int32, (half, 2 * half), 1)
    mixed, diagonal = f[:half], f[half : half + 1]
    turned = jnp.transpose(jnp.concatenate([mixed, jnp.zeros_like(mixed)], axis=0))
    top = jnp.where((cols > rows) & (cols < half), turned[:half], mixed)
    last = jnp.where(cols > rows, mixed, jnp.where(cols < rows, turned[:half], diagonal))
    low = jnp.where(cols < half, turned[half:], pltpu.roll(last, half, 1))
    return jnp.concatenate([top, low], axis=0)


FOLDED = DK // 2 + 8
STATE = FOLDED + DK


def total_of(need, first):
    near = [need(first + n) for n in range(4)]
    state = (near[0][...] + near[1][...]) + (near[2][...] + near[3][...])
    return unfold_symmetric(state[:FOLDED]), state[FOLDED:]


def chunk(j):
    return slice(j * DK, (j + 1) * DK)


def prepare_body(tables, need, made, put):
    x, (low, high) = need(0), made
    rows = low.shape[0]
    low[...] = x[:rows].astype(F32)
    put(0)
    high[...] = x[rows:].astype(F32)


def upstream_body(tables, need, made, put):
    for h in range(HEADS):
        made[0][h] = need(0)[:, chunk(h)].astype(F32)


def project_body(slots, wk_hbm, wv_hbm, tables, need, made, put, w_buf, w_sem):
    (where,) = tables
    xb, k_out, v_out, tot = made
    cols = pl.ds(pl.multiple_of(where[len(where) - 1] * DK, DK), DK)
    weights = [
        pltpu.make_async_copy(w.at[:, cols], w_buf.at[:, chunk(n)], w_sem.at[n])
        for n, w in enumerate((wk_hbm, wv_hbm))
    ]
    for copy in weights:
        copy.start()
    for n, (slot, start) in enumerate(slots):
        piece = need(n)
        row = pl.multiple_of(where[slot] * DK + start, DK // 2)
        xb[pl.ds(row, piece.shape[0]), :] = piece[...].astype(BF16)
    put(0)
    for copy in weights:
        copy.wait()
    both = nn(xb[...], w_buf[...]).astype(BF16)
    k, v = both[:, :DK], both[:, DK:]
    k_out[...] = k
    v_out[...] = v
    put(1)
    put(2)
    rk = inv_norm(k)
    kn = k.astype(F32) * rk
    tot[:FOLDED] = fold_symmetric(fold_cols(tn(k, wide(kn * rk))))
    tot[FOLDED:] = fold_cols(tn(v, wide(kn)))


def states_body(wq_hbm, tables, need, made, put, w_buf, w_sem):
    (where,) = tables
    q_out, gram_out = made
    cols = pl.ds(pl.multiple_of(where[len(where) - 1] * DK, DK), DK)
    weight = pltpu.make_async_copy(wq_hbm.at[:, cols], w_buf, w_sem.at[0])
    weight.start()
    k_in = need(0)
    gram = jnp.zeros((DK, DK), F32)
    for j in range(CHUNKS):
        gram_out[j] = gram
        if j + 1 < CHUNKS:
            k = k_in[chunk(j), :]
            rk = inv_norm(k)
            gram = gram + fold_cols(tn(k, wide(k.astype(F32) * (rk * rk))))
    put(1)
    weight.wait()
    q_out[...] = nn(need(1)[...], w_buf[...]).astype(BF16)


def targets_body(tables, need, made, put):
    k_in, v_in, g_in = need(0), need(1), need(2)
    keep = causal(DK)
    cross = jnp.zeros((DK, DK), F32)
    for j in range(CHUNKS):
        k, v, g = k_in[chunk(j), :], v_in[chunk(j), :], g_in[j].astype(BF16)
        rk = inv_norm(k)
        scores = nt(g, v) * jnp.where(keep, across(rk), 0.0)
        made[0][j] = nn(twice_wide(g), tall(cross)) + nn(wide(scores), twice_tall(k))
        if j + 1 < CHUNKS:
            cross = cross + fold_cols(tn(v, wide(k.astype(F32) * rk)))


def solve_body(tables, need, made, put):
    (where,) = tables
    q_in, k_in, gram_in, part, g_in, damp_in = [need(n) for n in range(6)]
    gram_prior, cross_prior = total_of(need, 6)
    z_out, u_out, tot = made
    damp = damp_in[pl.ds(where[len(where) - 1], 1), :]
    keep = causal(DK)
    keys = [k_in[chunk(j), :] for j in range(CHUNKS)]
    systems = [system(k, gram_in[j] + gram_prior) for j, k in enumerate(keys)]
    cross_tall = tall(cross_prior)
    scale2, targets = [], []
    for j, k in enumerate(keys):
        rk = inv_norm(k)
        row = jnp.where(keep, across(rk * rk), 0.0)
        scale2.append(twice_tall(row))
        right = part[j] + nn(twice_wide(g_in[j].astype(BF16)), cross_tall)
        q = q_in[chunk(j), :]
        targets.append(jnp.concatenate([q.astype(F32) * inv_norm(q), right], axis=0))
    both = conjugate(targets, systems, scale2, damp)
    gram = jnp.zeros((DK, DK), F32)
    cross = jnp.zeros((DK, DK), F32)
    for j in range(CHUNKS):
        z, u = both[j][:DK], both[j][DK:]
        z_out[j] = z
        u_out[j] = u
        z_wide, u_wide = wide(z), wide(u)
        left = jnp.concatenate([u_wide, z_wide], axis=0)
        right = jnp.concatenate([z_wide, u_wide], axis=0)
        gram = gram + fold_rows(fold_cols(tn(left, right)))
        cross = cross + fold_cols(tn(g_in[j].astype(BF16), z_wide))
    tot[:FOLDED] = fold_symmetric(gram)
    tot[FOLDED:] = cross


def local_body(tables, need, made, put):
    q_in, k_in, v_in, g_in, z_in, u_in = [need(n) for n in range(6)]
    dq_out, dk_out, dv_out = made
    keep = causal(DK)
    for j in range(CHUNKS):
        q, u = q_in[chunk(j), :], u_in[j]
        rq = inv_norm(q)
        qn = q.astype(F32) * rq
        dq_out[j] = ((u - qn * rowsum(qn * u)) * rq).astype(BF16).astype(F32)
    put(0)
    gram = jnp.zeros((DK, DK), F32)
    cross = jnp.zeros((DK, DK), F32)
    for j in reversed(range(CHUNKS)):
        k, v = k_in[chunk(j), :], v_in[chunk(j), :]
        rk = inv_norm(k)
        row = jnp.where(keep, across(rk), 0.0)
        g = g_in[j].astype(BF16)
        scores = jnp.where(keep, nt(g, v), 0.0)
        u, z = u_in[j], z_in[j]
        u_wide, z_wide = wide(u), wide(z)
        kk = twice_wide(k)
        pair = nt(jnp.concatenate([u_wide, z_wide], axis=0), kk) * twice_tall(row)
        left = jnp.concatenate([scores - pair[:DK], -pair[DK:]], axis=0)
        right = jnp.concatenate([z_wide, u_wide], axis=0)
        dkn = fold_rows(fold_cols(tn(wide(left), right)))
        dkn = dkn + nn(twice_wide(v), tall(cross))
        dk_out[j] = dkn - rk * nn(kk, tall(gram))
        dv_out[j] = rk * nt(kk, wide(cross)) + tn(tall(pair[DK:]), twice_tall(g))
        if j:
            swapped = jnp.concatenate([u_wide, z_wide], axis=0)
            gram = gram + fold_rows(fold_cols(tn(swapped, right)))
            cross = cross + fold_cols(tn(g, z_wide))


def grads_body(seq, tables, need, made, put, dk_buf, dw_buf, out):
    (place,) = tables
    k_in, v_in, dk_part, dv_part, dq_in = [need(n) for n in range(5)]
    gram_after, cross_after = total_of(need, 5)
    gram_tall, cross_tall, cross_wide = tall(gram_after), tall(cross_after), wide(cross_after)
    for j in range(CHUNKS):
        k, v = k_in[chunk(j), :], v_in[chunk(j), :]
        rk = inv_norm(k)
        kn = k.astype(F32) * rk
        kk = twice_wide(k)
        dkn = dk_part[j] + nn(twice_wide(v), cross_tall) - rk * nn(kk, gram_tall)
        dk = ((dkn - kn * rowsum(kn * dkn)) * rk).astype(BF16)
        dk_buf[chunk(j), :] = dk
        out[j, :DK] = dk.astype(F32)
        dv = dv_part[j] + rk * nt(kk, cross_wide)
        out[j, DK : 2 * DK] = dv.astype(BF16).astype(F32)
        out[j, 2 * DK :] = dq_in[j]
    dw_buf[...] = jnp.transpose(tn(dk_buf[...], need(9)[...]))
    rows = made[0].shape[0]
    for step in range(seq):
        start = pl.multiple_of(lax.rem(place[0] + step, seq) * rows, rows)
        made[step][...] = dw_buf[pl.ds(start, rows), :]
        put(step)
    core = place[2]
    for step in range(CHUNKS // 2):
        block = lax.rem(place[1] + step, CHUNKS // 2) * 2
        made[seq + step][: 3 * DK] = out[block + core]
        made[seq + step][3 * DK :] = out[block + 1 - core]
        put(seq + step)


def input_grad_body(tables, need, made, put, *sides):
    (place,) = tables
    for step in range(HEADS):
        piece = need(step)
        chips = HEADS // 2
        core = place[2] if step < chips else 1 - place[2]
        head = lax.rem(place[1] + chips - step % chips, chips) * 2 + core
        cols = pl.ds(pl.multiple_of(head * DK, DK), DK)
        for n, side in enumerate(sides):
            side[:, cols] = piece[chunk(n), :].astype(BF16)
    total = nt(sides[0][...], need(HEADS)[...])
    for n in (1, 2):
        total = total + nt(sides[n][...], need(HEADS + n)[...])
    made[0][...] = total.astype(BF16)


def shift(x, axis, by, wrap):
    size = lax.axis_size(axis)
    pairs = [(i, (i + by) % size) for i in range(size) if wrap or 0 <= i + by < size]
    return lax.ppermute(x, axis, pairs)


def exclusive(total, sign):
    one, two = shift(total, "z", sign, False), shift(total, "z", 2 * sign, False)
    third = total + one + two
    return one, two, shift(third, "z", 3 * sign, False), shift(third, "z", 6 * sign, False)


def exchange(x, axis):
    return lax.all_to_all(x, axis, 0, 0)


def gather_plane(low, high):
    y, core = lax.axis_index("y"), lax.axis_index("core")
    rows = low.shape[0]
    prev_low = shift(low, "y", 1, True)
    next_high = shift(high, "y", -1, True)
    prev_high = shift(high, "y", 1, True)
    next_low = shift(low, "y", -1, True)
    far_low = shift(prev_low, "y", 1, True)
    far_high = shift(next_high, "y", -1, True)
    pieces = [(low, 0, 0), (high, 0, rows)]
    pieces += [(shift(low, "core", 1, True), 4, 0), (shift(high, "core", 1, True), 4, rows)]
    near = (
        (prev_low, 1, 0), (next_high, 2, rows), (prev_high, 1, rows), (next_low, 2, 0),
        (far_low, 3, 0), (far_high, 3, rows),
    )
    for piece, slot, start in near:
        pieces.append((piece, slot, start))
        pieces.append((shift(piece, "core", 1, True), slot + 4, start))
    ysize = lax.axis_size("y")
    places = [
        ((y + step) % ysize) * 2 + c for c in (core, 1 - core) for step in (0, -1, 1, 2)
    ] + [y * 2 + core]
    return pieces, jnp.stack(places).astype(jnp.int32)


def on_device(inputs, w_query, w_key, w_value, damping, grad_out):
    mine = inputs[0]
    tokens, width = mine.shape
    plane = CHUNKS * tokens
    blocks = shaped(CHUNKS, tokens, DK)
    brick = shaped(plane, DK, dtype=BF16)
    state = shaped(STATE, DK)
    unit = 2 * plane * DK * DK

    half = shaped(tokens // 2, width)
    low, high = call(prepare_body, [half, half], [mine], 0)
    pieces, where = gather_plane(low, high)
    slots = tuple((slot, start) for _, slot, start in pieces)
    pieces = [p for p, _, _ in pieces]
    (upstream,) = call(upstream_body, [shaped(HEADS, tokens, DK)], [grad_out[0]], 0)
    xb, k, v, first_tot = call(
        functools.partial(project_body, slots),
        [shaped(plane, width, dtype=BF16), brick, brick, state],
        pieces, unit * 28, tables=[where], raw=[w_key, w_value],
        scratch=[pltpu.VMEM((width, 2 * DK), BF16), pltpu.SemaphoreType.DMA((2,))],
    )
    prior = exclusive(first_tot, 1)
    g = exchange(upstream, PLANE)
    q, gram_pre = call(
        states_body, [brick, shaped(CHUNKS, DK, DK)], [k, xb], unit * 10,
        tables=[where], raw=[w_query],
        scratch=[pltpu.VMEM((width, DK), BF16), pltpu.SemaphoreType.DMA((1,))],
    )
    (part,) = call(targets_body, [blocks], [k, v, g], unit * 8)

    z, u, second_tot = call(
        solve_body, [blocks, blocks, state],
        [q, k, gram_pre, part, g, damping, *prior], unit * 40, tables=[where],
    )
    after = exclusive(second_tot, -1)
    dq, dk_part, dv_part = call(local_body, [blocks, blocks, blocks], [q, k, v, g, z, u], unit * 30)
    seq = lax.axis_size("seq")
    ctx = ("z", "y", "core")
    spread = lax.axis_size(ctx)
    rows = width // (seq * spread)
    place = jnp.stack(
        [lax.axis_index("seq"), lax.axis_index("y"), lax.axis_index("core")]
    ).astype(jnp.int32)
    pieces = call(
        functools.partial(grads_body, seq),
        [shaped(width // seq, DK)] * seq + [shaped(6 * tokens, DK)] * (CHUNKS // 2),
        [k, v, dk_part, dv_part, dq, *after, xb], unit * 14, tables=[place],
        scratch=[
            pltpu.VMEM((plane, DK), BF16), pltpu.VMEM((width, DK), F32),
            pltpu.VMEM((CHUNKS, 3 * tokens, DK), F32),
        ],
    )
    dw, dkv = pieces[:seq], pieces[seq:]
    dw = sum((shift(part, "seq", step, True) for step, part in enumerate(dw) if step), dw[0])
    dkv = [shift(p, "y", step, True) if step else p for step, p in enumerate(dkv)]
    dw = exchange(dw.reshape(spread, rows, DK), ctx)
    other = [shift(p, "core", 1, True) for p in dkv]
    dw = dw.reshape(spread // HEADS, HEADS, rows, DK)
    grad_weights = jnp.sum(dw, axis=0).transpose(1, 0, 2).reshape(rows, HEADS * DK)

    mine_of = [(p, slice(0, 3 * tokens)) for p in dkv]
    other_of = [(p, slice(3 * tokens, 6 * tokens)) for p in other]
    (grad_inputs,) = call(
        input_grad_body, [shaped(tokens, width, dtype=BF16)],
        [*mine_of, *other_of, w_key, w_value, w_query], unit * 24, tables=[place],
        scratch=[pltpu.VMEM((tokens, width), BF16)] * 3,
    )
    return (grad_inputs[None], grad_weights)


def solution(mesh):
    grid = Mesh(mesh.devices.reshape(4, 8, 4, 2), ("seq", "z", "y", "core"))
    ctx = ("z", "y", "core")
    in_specs = (P("seq", ctx, None), P(), P(), P(), P(), P("seq", ctx, None))
    out_specs = (P("seq", ctx, None), P(("seq",) + ctx, None))

    return jax.shard_map(on_device, mesh=grid, in_specs=in_specs, out_specs=out_specs, check_vma=False)
```

```python
import functools

import jax
import jax.numpy as jnp
from jax import lax
from jax.experimental import pallas as pl
from jax.experimental.pallas import tpu as pltpu
from jax.sharding import Mesh, PartitionSpec as P


ITERS = 2
EPSILON = 1e-06
F32 = jnp.float32
BF16 = jnp.bfloat16
HEADS = 8
DK = 128
CHUNKS = 8
PLANE = ("y", "core")


def halves(x):
    hi = x.astype(BF16)
    return hi, (x - hi.astype(F32)).astype(BF16)


def nn(a, b):
    return lax.dot_general(a, b, (((1,), (0,)), ((), ())), preferred_element_type=F32)


def nt(a, b):
    return lax.dot_general(a, b, (((1,), (1,)), ((), ())), preferred_element_type=F32)


def tn(a, b):
    return lax.dot_general(a, b, (((0,), (0,)), ((), ())), preferred_element_type=F32)


def wide(x):
    return jnp.concatenate(halves(x), axis=1)


def tall(x):
    return jnp.concatenate(halves(x), axis=0)


def twice_wide(b):
    return jnp.concatenate([b, b], axis=1)


def twice_tall(b):
    return jnp.concatenate([b, b], axis=0)


def fold_cols(m):
    half = m.shape[1] // 2
    return m[:, :half] + m[:, half:]


def fold_rows(m):
    half = m.shape[0] // 2
    return m[:half] + m[half:]


def rowsum(x):
    return jnp.sum(x, axis=-1, keepdims=True)


def causal(size):
    rows = lax.broadcasted_iota(jnp.int32, (size, size), 0)
    cols = lax.broadcasted_iota(jnp.int32, (size, size), 1)
    return rows >= cols


def inv_norm(block):
    wide_block = block.astype(F32)
    return lax.rsqrt(rowsum(wide_block * wide_block) + EPSILON)


def across(column):
    size = column.shape[0]
    return jnp.transpose(jnp.broadcast_to(column, (size, size)))


def system(key, gram):
    turned = jnp.transpose(key)
    hi, lo = halves(gram)
    upper = jnp.concatenate([turned, hi, lo], axis=1)
    lower = jnp.concatenate([turned, hi, jnp.zeros_like(lo)], axis=1)
    return jnp.concatenate([upper, lower], axis=0), twice_tall(key)


def apply_all(vectors, systems, scale2, damp):
    firsts = [nn(wide(p), s[0]) for p, s in zip(vectors, systems)]
    inner = [wide(f[:, :DK] * m) for f, m in zip(firsts, scale2)]
    return [
        nn(i, s[1]) + (f[:, DK : 2 * DK] + f[:, 2 * DK :]) + damp * p
        for i, s, f, p in zip(inner, systems, firsts, vectors)
    ]


def conjugate(targets, systems, scale2, damp):
    residual = list(targets)
    direction = list(targets)
    norm_now = [rowsum(r * r) for r in residual]
    solution = None
    for sweep in range(ITERS):
        image = apply_all(direction, systems, scale2, damp)
        step = [n / (rowsum(p * w) + EPSILON) for n, p, w in zip(norm_now, direction, image)]
        moved = [a * p for a, p in zip(step, direction)]
        solution = moved if solution is None else [x + m for x, m in zip(solution, moved)]
        if sweep + 1 < ITERS:
            residual = [r - a * w for r, a, w in zip(residual, step, image)]
            norm_next = [rowsum(r * r) for r in residual]
            direction = [
                r + n / (o + EPSILON) * p
                for r, n, o, p in zip(residual, norm_next, norm_now, direction)
            ]
            norm_now = norm_next
    return solution


def staged(body, counts, parts, tables, *refs):
    n_in, n_out = counts
    sources, refs = refs[:n_in], refs[n_in:]
    targets, refs = refs[:n_out], refs[n_out:]
    held, refs = refs[:n_in], refs[n_in:]
    made, (in_sems, out_sems, *rest) = refs[:n_out], refs[n_out:]
    loads = [
        pltpu.make_async_copy(s.at[part] if part else s, h, in_sems.at[n])
        for n, (s, h, part) in enumerate(zip(sources, held, parts))
    ]
    stores = [
        pltpu.make_async_copy(m, t, out_sems.at[n]) for n, (m, t) in enumerate(zip(made, targets))
    ]
    for load in loads:
        load.start()
    arrived, sent = set(), set()

    def need(n):
        if n not in arrived:
            arrived.add(n)
            loads[n].wait()
        return held[n]

    def put(n):
        sent.add(n)
        stores[n].start()

    body(tables, need, made, put, *rest)
    for n in range(n_in):
        need(n)
    for n in range(n_out):
        if n not in sent:
            put(n)
    for store in stores:
        store.wait()


def shaped(*dims, dtype=F32):
    return jax.ShapeDtypeStruct(dims, dtype)


ANYWHERE = pl.BlockSpec(memory_space=pl.ANY)


def call(body, outs, args, flops, tables=(), raw=(), scratch=()):
    parts = [a[1] if isinstance(a, tuple) else None for a in args]
    args = [a[0] if isinstance(a, tuple) else a for a in args]
    held = [
        (p.stop - p.start, *a.shape[1:]) if p else a.shape for a, p in zip(args, parts)
    ]

    def kernel(*refs):
        t, r = len(tables), len(raw)
        operands = refs[t + r :]
        staged(
            functools.partial(body, *refs[t : t + r]), (len(args), len(outs)), parts, refs[:t],
            *operands,
        )

    moved = sum(a.size * a.dtype.itemsize for a in args) + sum(
        o.size * jnp.dtype(o.dtype).itemsize for o in outs
    )
    return pl.pallas_call(
        kernel,
        out_shape=tuple(outs),
        in_specs=[pl.BlockSpec(memory_space=pltpu.SMEM)] * len(tables)
        + [ANYWHERE] * (len(raw) + len(args)),
        out_specs=tuple([ANYWHERE] * len(outs)),
        scratch_shapes=[pltpu.VMEM(h, a.dtype) for h, a in zip(held, args)]
        + [pltpu.VMEM(o.shape, o.dtype) for o in outs]
        + [pltpu.SemaphoreType.DMA((len(args),)), pltpu.SemaphoreType.DMA((len(outs),))]
        + list(scratch),
        compiler_params=pltpu.CompilerParams(vmem_limit_bytes=60 << 20),
        cost_estimate=pl.CostEstimate(flops=flops, bytes_accessed=moved, transcendentals=0),
    )(*tables, *raw, *args)


def fold_symmetric(m):
    half = m.shape[0] // 2
    rows = lax.broadcasted_iota(jnp.int32, (half, 2 * half), 0)
    cols = lax.broadcasted_iota(jnp.int32, (half, 2 * half), 1)
    low = pltpu.roll(m[half:], half, 1)
    diagonal = jnp.sum(jnp.where(rows == cols, low, 0.0), axis=0, keepdims=True)
    mixed = jnp.where((cols > rows) & (cols < half), low, m[:half])
    return jnp.concatenate([mixed, jnp.broadcast_to(diagonal, (8, 2 * half))], axis=0)


def unfold_symmetric(f):
    half = f.shape[1] // 2
    rows = lax.broadcasted_iota(jnp.int32, (half, 2 * half), 0)
    cols = lax.broadcasted_iota(jnp.int32, (half, 2 * half), 1)
    mixed, diagonal = f[:half], f[half : half + 1]
    turned = jnp.transpose(jnp.concatenate([mixed, jnp.zeros_like(mixed)], axis=0))
    top = jnp.where((cols > rows) & (cols < half), turned[:half], mixed)
    last = jnp.where(cols > rows, mixed, jnp.where(cols < rows, turned[:half], diagonal))
    low = jnp.where(cols < half, turned[half:], pltpu.roll(last, half, 1))
    return jnp.concatenate([top, low], axis=0)


FOLDED = DK // 2 + 8
STATE = FOLDED + DK


def total_of(need, first):
    near = [need(first + n) for n in range(4)]
    state = (near[0][...] + near[1][...]) + (near[2][...] + near[3][...])
    return unfold_symmetric(state[:FOLDED]), state[FOLDED:]


def chunk(j):
    return slice(j * DK, (j + 1) * DK)


def prepare_body(tables, need, made, put):
    x, (low, high) = need(0), made
    rows = low.shape[0]
    low[...] = x[:rows].astype(F32)
    put(0)
    high[...] = x[rows:].astype(F32)


def upstream_body(tables, need, made, put):
    for h in range(HEADS):
        made[0][h] = need(0)[:, chunk(h)].astype(F32)


def project_body(slots, wk_hbm, wv_hbm, tables, need, made, put, w_buf, w_sem):
    (where,) = tables
    xb, k_out, v_out, tot = made
    cols = pl.ds(pl.multiple_of(where[len(where) - 1] * DK, DK), DK)
    weights = [
        pltpu.make_async_copy(w.at[:, cols], w_buf.at[:, chunk(n)], w_sem.at[n])
        for n, w in enumerate((wk_hbm, wv_hbm))
    ]
    for copy in weights:
        copy.start()
    for n, (slot, start) in enumerate(slots):
        piece = need(n)
        row = pl.multiple_of(where[slot] * DK + start, DK // 2)
        xb[pl.ds(row, piece.shape[0]), :] = piece[...].astype(BF16)
    put(0)
    for copy in weights:
        copy.wait()
    both = nn(xb[...], w_buf[...]).astype(BF16)
    k, v = both[:, :DK], both[:, DK:]
    k_out[...] = k
    v_out[...] = v
    put(1)
    put(2)
    rk = inv_norm(k)
    kn = k.astype(F32) * rk
    tot[:FOLDED] = fold_symmetric(fold_cols(tn(k, wide(kn * rk))))
    tot[FOLDED:] = fold_cols(tn(v, wide(kn)))


def states_body(wq_hbm, tables, need, made, put, w_buf, w_sem):
    (where,) = tables
    q_out, gram_out = made
    cols = pl.ds(pl.multiple_of(where[len(where) - 1] * DK, DK), DK)
    weight = pltpu.make_async_copy(wq_hbm.at[:, cols], w_buf, w_sem.at[0])
    weight.start()
    k_in = need(0)
    gram = jnp.zeros((DK, DK), F32)
    for j in range(CHUNKS):
        gram_out[j] = gram
        if j + 1 < CHUNKS:
            k = k_in[chunk(j), :]
            rk = inv_norm(k)
            gram = gram + fold_cols(tn(k, wide(k.astype(F32) * (rk * rk))))
    put(1)
    weight.wait()
    q_out[...] = nn(need(1)[...], w_buf[...]).astype(BF16)


def targets_body(tables, need, made, put):
    k_in, v_in, g_in = need(0), need(1), need(2)
    keep = causal(DK)
    cross = jnp.zeros((DK, DK), F32)
    for j in range(CHUNKS):
        k, v, g = k_in[chunk(j), :], v_in[chunk(j), :], g_in[j].astype(BF16)
        rk = inv_norm(k)
        scores = nt(g, v) * jnp.where(keep, across(rk), 0.0)
        made[0][j] = nn(twice_wide(g), tall(cross)) + nn(wide(scores), twice_tall(k))
        if j + 1 < CHUNKS:
            cross = cross + fold_cols(tn(v, wide(k.astype(F32) * rk)))


def solve_body(tables, need, made, put):
    (where,) = tables
    q_in, k_in, gram_in, part, g_in, damp_in = [need(n) for n in range(6)]
    gram_prior, cross_prior = total_of(need, 6)
    z_out, u_out, tot = made
    damp = damp_in[pl.ds(where[len(where) - 1], 1), :]
    keep = causal(DK)
    keys = [k_in[chunk(j), :] for j in range(CHUNKS)]
    systems = [system(k, gram_in[j] + gram_prior) for j, k in enumerate(keys)]
    cross_tall = tall(cross_prior)
    scale2, targets = [], []
    for j, k in enumerate(keys):
        rk = inv_norm(k)
        row = jnp.where(keep, across(rk * rk), 0.0)
        scale2.append(twice_tall(row))
        right = part[j] + nn(twice_wide(g_in[j].astype(BF16)), cross_tall)
        q = q_in[chunk(j), :]
        targets.append(jnp.concatenate([q.astype(F32) * inv_norm(q), right], axis=0))
    both = conjugate(targets, systems, scale2, damp)
    gram = jnp.zeros((DK, DK), F32)
    cross = jnp.zeros((DK, DK), F32)
    for j in range(CHUNKS):
        z, u = both[j][:DK], both[j][DK:]
        z_out[j] = z
        u_out[j] = u
        z_wide, u_wide = wide(z), wide(u)
        left = jnp.concatenate([u_wide, z_wide], axis=0)
        right = jnp.concatenate([z_wide, u_wide], axis=0)
        gram = gram + fold_rows(fold_cols(tn(left, right)))
        cross = cross + fold_cols(tn(g_in[j].astype(BF16), z_wide))
    tot[:FOLDED] = fold_symmetric(gram)
    tot[FOLDED:] = cross


def local_body(tables, need, made, put):
    q_in, k_in, v_in, g_in, z_in, u_in = [need(n) for n in range(6)]
    dq_out, dk_out = made
    keep = causal(DK)
    for j in range(CHUNKS):
        q, u = q_in[chunk(j), :], u_in[j]
        rq = inv_norm(q)
        qn = q.astype(F32) * rq
        dq_out[j] = ((u - qn * rowsum(qn * u)) * rq).astype(BF16).astype(F32)
    put(0)
    gram = jnp.zeros((DK, DK), F32)
    cross = jnp.zeros((DK, DK), F32)
    for j in reversed(range(CHUNKS)):
        k, v = k_in[chunk(j), :], v_in[chunk(j), :]
        rk = inv_norm(k)
        row = jnp.where(keep, across(rk), 0.0)
        g = g_in[j].astype(BF16)
        scores = jnp.where(keep, nt(g, v), 0.0)
        u, z = u_in[j], z_in[j]
        u_wide, z_wide = wide(u), wide(z)
        kk = twice_wide(k)
        pair = nt(jnp.concatenate([u_wide, z_wide], axis=0), kk) * twice_tall(row)
        left = jnp.concatenate([scores - pair[:DK], -pair[DK:]], axis=0)
        right = jnp.concatenate([z_wide, u_wide], axis=0)
        dkn = fold_rows(fold_cols(tn(wide(left), right)))
        dkn = dkn + nn(twice_wide(v), tall(cross))
        dk_out[j] = dkn - rk * nn(kk, tall(gram))
        if j:
            swapped = jnp.concatenate([u_wide, z_wide], axis=0)
            gram = gram + fold_rows(fold_cols(tn(swapped, right)))
            cross = cross + fold_cols(tn(g, z_wide))


def value_terms_body(tables, need, made, put):
    k_in, g_in, z_in = [need(n) for n in range(3)]
    keep = causal(DK)
    cross = jnp.zeros((DK, DK), F32)
    for j in reversed(range(CHUNKS)):
        k, g = k_in[chunk(j), :], g_in[j].astype(BF16)
        rk = inv_norm(k)
        kk = twice_wide(k)
        z_wide = wide(z_in[j])
        scores = nt(z_wide, kk) * jnp.where(keep, across(rk), 0.0)
        made[0][j] = rk * nt(kk, wide(cross)) + tn(tall(scores), twice_tall(g))
        if j:
            cross = cross + fold_cols(tn(g, z_wide))


def grads_body(seq, tables, need, made, put, dk_buf, dw_buf, out):
    (place,) = tables
    k_in, v_in, dk_part, dv_part = [need(n) for n in range(4)]
    gram_after, cross_after = total_of(need, 4)
    gram_tall, cross_tall, cross_wide = tall(gram_after), tall(cross_after), wide(cross_after)
    for j in range(CHUNKS):
        k, v = k_in[chunk(j), :], v_in[chunk(j), :]
        rk = inv_norm(k)
        kn = k.astype(F32) * rk
        kk = twice_wide(k)
        dkn = dk_part[j] + nn(twice_wide(v), cross_tall) - rk * nn(kk, gram_tall)
        dk = ((dkn - kn * rowsum(kn * dkn)) * rk).astype(BF16)
        dk_buf[chunk(j), :] = dk
        out[j, :DK] = dk.astype(F32)
        dv = dv_part[j] + rk * nt(kk, cross_wide)
        out[j, DK:] = dv.astype(BF16).astype(F32)
    dw_buf[...] = jnp.transpose(tn(dk_buf[...], need(8)[...]))
    rows = made[0].shape[0]
    for step in range(seq):
        start = pl.multiple_of(lax.rem(place[0] + step, seq) * rows, rows)
        made[step][...] = dw_buf[pl.ds(start, rows), :]
        put(step)
    core = place[2]
    for step in range(CHUNKS // 2):
        block = lax.rem(place[1] + step, CHUNKS // 2) * 2
        made[seq + step][: 2 * DK] = out[block + core]
        made[seq + step][2 * DK :] = out[block + 1 - core]
        put(seq + step)


def query_part_body(tables, need, made, put):
    cat = jnp.concatenate([need(0)[h].astype(BF16) for h in range(HEADS)], axis=1)
    made[0][...] = nt(cat, need(1)[...])


def input_grad_body(tables, need, made, put, *sides):
    (place,) = tables
    for step in range(HEADS):
        piece = need(step)
        chips = HEADS // 2
        core = place[2] if step < chips else 1 - place[2]
        head = lax.rem(place[1] + chips - step % chips, chips) * 2 + core
        cols = pl.ds(pl.multiple_of(head * DK, DK), DK)
        for n, side in enumerate(sides):
            side[:, cols] = piece[chunk(n), :].astype(BF16)
    total = need(HEADS)[...]
    for n, side in enumerate(sides):
        total = total + nt(side[...], need(HEADS + 1 + n)[...])
    made[0][...] = total.astype(BF16)


def shift(x, axis, by, wrap):
    size = lax.axis_size(axis)
    pairs = [(i, (i + by) % size) for i in range(size) if wrap or 0 <= i + by < size]
    return lax.ppermute(x, axis, pairs)


def exclusive(total, sign):
    one, two = shift(total, "z", sign, False), shift(total, "z", 2 * sign, False)
    third = total + one + two
    six = shift(third, "z", 6 * sign, False)
    three = shift(third, "z", 3 * sign, False)
    return one, two, three, six


def exchange(x, axis):
    return lax.all_to_all(x, axis, 0, 0)


def gather_plane(low, high):
    y, core = lax.axis_index("y"), lax.axis_index("core")
    rows = low.shape[0]
    prev_low = shift(low, "y", 1, True)
    next_high = shift(high, "y", -1, True)
    prev_high = shift(high, "y", 1, True)
    next_low = shift(low, "y", -1, True)
    far_low = shift(prev_low, "y", 1, True)
    far_high = shift(next_high, "y", -1, True)
    pieces = [(low, 0, 0), (high, 0, rows)]
    pieces += [(shift(low, "core", 1, True), 4, 0), (shift(high, "core", 1, True), 4, rows)]
    near = (
        (prev_low, 1, 0), (next_high, 2, rows), (prev_high, 1, rows), (next_low, 2, 0),
        (far_low, 3, 0), (far_high, 3, rows),
    )
    for piece, slot, start in near:
        pieces.append((piece, slot, start))
        pieces.append((shift(piece, "core", 1, True), slot + 4, start))
    ysize = lax.axis_size("y")
    places = [
        ((y + step) % ysize) * 2 + c for c in (core, 1 - core) for step in (0, -1, 1, 2)
    ] + [y * 2 + core]
    return pieces, jnp.stack(places).astype(jnp.int32)


def on_device(inputs, w_query, w_key, w_value, damping, grad_out):
    mine = inputs[0]
    tokens, width = mine.shape
    plane = CHUNKS * tokens
    blocks = shaped(CHUNKS, tokens, DK)
    brick = shaped(plane, DK, dtype=BF16)
    state = shaped(STATE, DK)
    unit = 2 * plane * DK * DK

    half = shaped(tokens // 2, width)
    low, high = call(prepare_body, [half, half], [mine], 0)
    pieces, where = gather_plane(low, high)
    slots = tuple((slot, start) for _, slot, start in pieces)
    pieces = [p for p, _, _ in pieces]
    (upstream,) = call(upstream_body, [shaped(HEADS, tokens, DK)], [grad_out[0]], 0)
    xb, k, v, first_tot = call(
        functools.partial(project_body, slots),
        [shaped(plane, width, dtype=BF16), brick, brick, state],
        pieces, unit * 28, tables=[where], raw=[w_key, w_value],
        scratch=[pltpu.VMEM((width, 2 * DK), BF16), pltpu.SemaphoreType.DMA((2,))],
    )
    prior = exclusive(first_tot, 1)
    g = exchange(upstream, PLANE)
    q, gram_pre = call(
        states_body, [brick, shaped(CHUNKS, DK, DK)], [k, xb], unit * 10,
        tables=[where], raw=[w_query],
        scratch=[pltpu.VMEM((width, DK), BF16), pltpu.SemaphoreType.DMA((1,))],
    )
    (part,) = call(targets_body, [blocks], [k, v, g], unit * 8)

    z, u, second_tot = call(
        solve_body, [blocks, blocks, state],
        [q, k, gram_pre, part, g, damping, *prior], unit * 40, tables=[where],
    )
    after = exclusive(second_tot, -1)
    dq, dk_part = call(local_body, [blocks, blocks], [q, k, v, g, z, u], unit * 26)
    (dv_part,) = call(value_terms_body, [blocks], [k, g, z], unit * 8)
    dq_all = exchange(dq, PLANE)
    (partial,) = call(query_part_body, [shaped(tokens, width)], [dq_all, w_query], unit * 8)

    seq = lax.axis_size("seq")
    ctx = ("z", "y", "core")
    spread = lax.axis_size(ctx)
    rows = width // (seq * spread)
    place = jnp.stack(
        [lax.axis_index("seq"), lax.axis_index("y"), lax.axis_index("core")]
    ).astype(jnp.int32)
    pieces = call(
        functools.partial(grads_body, seq),
        [shaped(width // seq, DK)] * seq + [shaped(4 * tokens, DK)] * (CHUNKS // 2),
        [k, v, dk_part, dv_part, *after, xb], unit * 14, tables=[place],
        scratch=[
            pltpu.VMEM((plane, DK), BF16), pltpu.VMEM((width, DK), F32),
            pltpu.VMEM((CHUNKS, 2 * tokens, DK), F32),
        ],
    )
    dw, dkv = pieces[:seq], pieces[seq:]
    dw = sum((shift(part, "seq", step, True) for step, part in enumerate(dw) if step), dw[0])
    dkv = [shift(p, "y", step, True) if step else p for step, p in enumerate(dkv)]
    dw = exchange(dw.reshape(spread, rows, DK), ctx)
    other = [shift(p, "core", 1, True) for p in dkv]
    dw = dw.reshape(spread // HEADS, HEADS, rows, DK)
    grad_weights = jnp.sum(dw, axis=0).transpose(1, 0, 2).reshape(rows, HEADS * DK)

    mine_of = [(p, slice(0, 2 * tokens)) for p in dkv]
    other_of = [(p, slice(2 * tokens, 4 * tokens)) for p in other]
    (grad_inputs,) = call(
        input_grad_body, [shaped(tokens, width, dtype=BF16)],
        [*mine_of, *other_of, partial, w_key, w_value], unit * 16, tables=[place],
        scratch=[pltpu.VMEM((tokens, width), BF16)] * 2,
    )
    return (grad_inputs[None], grad_weights)


def solution(mesh):
    grid = Mesh(mesh.devices.reshape(4, 8, 4, 2), ("seq", "z", "y", "core"))
    ctx = ("z", "y", "core")
    in_specs = (P("seq", ctx, None), P(), P(), P(), P(), P("seq", ctx, None))
    out_specs = (P("seq", ctx, None), P(("seq",) + ctx, None))

    return jax.shard_map(on_device, mesh=grid, in_specs=in_specs, out_specs=out_specs, check_vma=False)
```

```python
import functools

import jax
import jax.numpy as jnp
from jax import lax
from jax.experimental import pallas as pl
from jax.experimental.pallas import tpu as pltpu
from jax.sharding import Mesh, PartitionSpec as P


ITERS = 2
EPSILON = 1e-06
F32 = jnp.float32
BF16 = jnp.bfloat16
HEADS = 8
DK = 128
CHUNKS = 8
PLANE = ("y", "core")


def halves(x):
    hi = x.astype(BF16)
    return hi, (x - hi.astype(F32)).astype(BF16)


def nn(a, b):
    return lax.dot_general(a, b, (((1,), (0,)), ((), ())), preferred_element_type=F32)


def nt(a, b):
    return lax.dot_general(a, b, (((1,), (1,)), ((), ())), preferred_element_type=F32)


def tn(a, b):
    return lax.dot_general(a, b, (((0,), (0,)), ((), ())), preferred_element_type=F32)


def wide(x):
    return jnp.concatenate(halves(x), axis=1)


def tall(x):
    return jnp.concatenate(halves(x), axis=0)


def twice_wide(b):
    return jnp.concatenate([b, b], axis=1)


def twice_tall(b):
    return jnp.concatenate([b, b], axis=0)


def fold_cols(m):
    half = m.shape[1] // 2
    return m[:, :half] + m[:, half:]


def fold_rows(m):
    half = m.shape[0] // 2
    return m[:half] + m[half:]


def rowsum(x):
    return jnp.sum(x, axis=-1, keepdims=True)


def causal(size):
    rows = lax.broadcasted_iota(jnp.int32, (size, size), 0)
    cols = lax.broadcasted_iota(jnp.int32, (size, size), 1)
    return rows >= cols


def inv_norm(block):
    wide_block = block.astype(F32)
    return lax.rsqrt(rowsum(wide_block * wide_block) + EPSILON)


def across(column):
    size = column.shape[0]
    return jnp.transpose(jnp.broadcast_to(column, (size, size)))


def system(key, gram):
    turned = jnp.transpose(key)
    hi, lo = halves(gram)
    upper = jnp.concatenate([turned, hi, lo], axis=1)
    lower = jnp.concatenate([turned, hi, jnp.zeros_like(lo)], axis=1)
    return jnp.concatenate([upper, lower], axis=0), twice_tall(key)


def apply_all(vectors, systems, scale2, damp):
    firsts = [nn(wide(p), s[0]) for p, s in zip(vectors, systems)]
    inner = [wide(f[:, :DK] * m) for f, m in zip(firsts, scale2)]
    return [
        nn(i, s[1]) + (f[:, DK : 2 * DK] + f[:, 2 * DK :]) + damp * p
        for i, s, f, p in zip(inner, systems, firsts, vectors)
    ]


def conjugate(targets, systems, scale2, damp):
    residual = list(targets)
    direction = list(targets)
    norm_now = [rowsum(r * r) for r in residual]
    solution = None
    for sweep in range(ITERS):
        image = apply_all(direction, systems, scale2, damp)
        step = [n / (rowsum(p * w) + EPSILON) for n, p, w in zip(norm_now, direction, image)]
        moved = [a * p for a, p in zip(step, direction)]
        solution = moved if solution is None else [x + m for x, m in zip(solution, moved)]
        if sweep + 1 < ITERS:
            residual = [r - a * w for r, a, w in zip(residual, step, image)]
            norm_next = [rowsum(r * r) for r in residual]
            direction = [
                r + n / (o + EPSILON) * p
                for r, n, o, p in zip(residual, norm_next, norm_now, direction)
            ]
            norm_now = norm_next
    return solution


def staged(body, counts, parts, tables, *refs):
    n_in, n_out = counts
    sources, refs = refs[:n_in], refs[n_in:]
    targets, refs = refs[:n_out], refs[n_out:]
    held, refs = refs[:n_in], refs[n_in:]
    made, (in_sems, out_sems, *rest) = refs[:n_out], refs[n_out:]
    loads = [
        pltpu.make_async_copy(s.at[part] if part else s, h, in_sems.at[n])
        for n, (s, h, part) in enumerate(zip(sources, held, parts))
    ]
    stores = [
        pltpu.make_async_copy(m, t, out_sems.at[n]) for n, (m, t) in enumerate(zip(made, targets))
    ]
    for load in loads:
        load.start()
    arrived, sent = set(), set()

    def need(n):
        if n not in arrived:
            arrived.add(n)
            loads[n].wait()
        return held[n]

    def put(n):
        sent.add(n)
        stores[n].start()

    body(tables, need, made, put, *rest)
    for n in range(n_in):
        need(n)
    for n in range(n_out):
        if n not in sent:
            put(n)
    for store in stores:
        store.wait()


def shaped(*dims, dtype=F32):
    return jax.ShapeDtypeStruct(dims, dtype)


ANYWHERE = pl.BlockSpec(memory_space=pl.ANY)


def call(body, outs, args, flops, tables=(), raw=(), scratch=()):
    parts = [a[1] if isinstance(a, tuple) else None for a in args]
    args = [a[0] if isinstance(a, tuple) else a for a in args]
    held = [
        (p.stop - p.start, *a.shape[1:]) if p else a.shape for a, p in zip(args, parts)
    ]

    def kernel(*refs):
        t, r = len(tables), len(raw)
        operands = refs[t + r :]
        staged(
            functools.partial(body, *refs[t : t + r]), (len(args), len(outs)), parts, refs[:t],
            *operands,
        )

    moved = sum(a.size * a.dtype.itemsize for a in args) + sum(
        o.size * jnp.dtype(o.dtype).itemsize for o in outs
    )
    return pl.pallas_call(
        kernel,
        out_shape=tuple(outs),
        in_specs=[pl.BlockSpec(memory_space=pltpu.SMEM)] * len(tables)
        + [ANYWHERE] * (len(raw) + len(args)),
        out_specs=tuple([ANYWHERE] * len(outs)),
        scratch_shapes=[pltpu.VMEM(h, a.dtype) for h, a in zip(held, args)]
        + [pltpu.VMEM(o.shape, o.dtype) for o in outs]
        + [pltpu.SemaphoreType.DMA((len(args),)), pltpu.SemaphoreType.DMA((len(outs),))]
        + list(scratch),
        compiler_params=pltpu.CompilerParams(vmem_limit_bytes=60 << 20),
        cost_estimate=pl.CostEstimate(flops=flops, bytes_accessed=moved, transcendentals=0),
    )(*tables, *raw, *args)


def fold_symmetric(m):
    half = m.shape[0] // 2
    rows = lax.broadcasted_iota(jnp.int32, (half, 2 * half), 0)
    cols = lax.broadcasted_iota(jnp.int32, (half, 2 * half), 1)
    low = pltpu.roll(m[half:], half, 1)
    diagonal = jnp.sum(jnp.where(rows == cols, low, 0.0), axis=0, keepdims=True)
    mixed = jnp.where((cols > rows) & (cols < half), low, m[:half])
    return jnp.concatenate([mixed, jnp.broadcast_to(diagonal, (8, 2 * half))], axis=0)


def unfold_symmetric(f):
    half = f.shape[1] // 2
    rows = lax.broadcasted_iota(jnp.int32, (half, 2 * half), 0)
    cols = lax.broadcasted_iota(jnp.int32, (half, 2 * half), 1)
    mixed, diagonal = f[:half], f[half : half + 1]
    turned = jnp.transpose(jnp.concatenate([mixed, jnp.zeros_like(mixed)], axis=0))
    top = jnp.where((cols > rows) & (cols < half), turned[:half], mixed)
    last = jnp.where(cols > rows, mixed, jnp.where(cols < rows, turned[:half], diagonal))
    low = jnp.where(cols < half, turned[half:], pltpu.roll(last, half, 1))
    return jnp.concatenate([top, low], axis=0)


FOLDED = DK // 2 + 8
STATE = FOLDED + DK


def total_of(need, first):
    near = [need(first + n) for n in range(4)]
    state = (near[0][...] + near[1][...]) + (near[2][...] + near[3][...])
    return unfold_symmetric(state[:FOLDED]), state[FOLDED:]


def chunk(j):
    return slice(j * DK, (j + 1) * DK)


def prepare_body(tables, need, made, put):
    x, (low, high) = need(0), made
    rows = low.shape[0]
    low[...] = x[:rows].astype(F32)
    put(0)
    high[...] = x[rows:].astype(F32)


def upstream_body(tables, need, made, put):
    for h in range(HEADS):
        made[0][h] = need(0)[:, chunk(h)].astype(F32)


def project_body(slots, wk_hbm, wv_hbm, tables, need, made, put, w_buf, w_sem):
    (where,) = tables
    xb, k_out, v_out, tot = made
    cols = pl.ds(pl.multiple_of(where[len(where) - 1] * DK, DK), DK)
    weights = [
        pltpu.make_async_copy(w.at[:, cols], w_buf.at[:, chunk(n)], w_sem.at[n])
        for n, w in enumerate((wk_hbm, wv_hbm))
    ]
    for copy in weights:
        copy.start()
    for n, (slot, start) in enumerate(slots):
        piece = need(n)
        row = pl.multiple_of(where[slot] * DK + start, DK // 2)
        xb[pl.ds(row, piece.shape[0]), :] = piece[...].astype(BF16)
    put(0)
    for copy in weights:
        copy.wait()
    both = nn(xb[...], w_buf[...]).astype(BF16)
    k, v = both[:, :DK], both[:, DK:]
    k_out[...] = k
    v_out[...] = v
    put(1)
    put(2)
    rk = inv_norm(k)
    kn = k.astype(F32) * rk
    tot[:FOLDED] = fold_symmetric(fold_cols(tn(k, wide(kn * rk))))
    tot[FOLDED:] = fold_cols(tn(v, wide(kn)))


def states_body(wq_hbm, tables, need, made, put, w_buf, w_sem):
    (where,) = tables
    q_out, gram_out = made
    cols = pl.ds(pl.multiple_of(where[len(where) - 1] * DK, DK), DK)
    weight = pltpu.make_async_copy(wq_hbm.at[:, cols], w_buf, w_sem.at[0])
    weight.start()
    k_in = need(0)
    gram = jnp.zeros((DK, DK), F32)
    for j in range(CHUNKS):
        gram_out[j] = gram
        if j + 1 < CHUNKS:
            k = k_in[chunk(j), :]
            rk = inv_norm(k)
            gram = gram + fold_cols(tn(k, wide(k.astype(F32) * (rk * rk))))
    put(1)
    weight.wait()
    q_out[...] = nn(need(1)[...], w_buf[...]).astype(BF16)


def targets_body(tables, need, made, put):
    k_in, v_in, g_in = need(0), need(1), need(2)
    keep = causal(DK)
    cross = jnp.zeros((DK, DK), F32)
    for j in range(CHUNKS):
        k, v, g = k_in[chunk(j), :], v_in[chunk(j), :], g_in[j].astype(BF16)
        rk = inv_norm(k)
        scores = nt(g, v) * jnp.where(keep, across(rk), 0.0)
        made[0][j] = nn(twice_wide(g), tall(cross)) + nn(wide(scores), twice_tall(k))
        if j + 1 < CHUNKS:
            cross = cross + fold_cols(tn(v, wide(k.astype(F32) * rk)))


def solve_body(tables, need, made, put):
    (where,) = tables
    q_in, k_in, gram_in, part, g_in, damp_in = [need(n) for n in range(6)]
    gram_prior, cross_prior = total_of(need, 6)
    z_out, u_out, tot = made
    damp = damp_in[pl.ds(where[len(where) - 1], 1), :]
    keep = causal(DK)
    keys = [k_in[chunk(j), :] for j in range(CHUNKS)]
    systems = [system(k, gram_in[j] + gram_prior) for j, k in enumerate(keys)]
    cross_tall = tall(cross_prior)
    scale2, targets = [], []
    for j, k in enumerate(keys):
        rk = inv_norm(k)
        row = jnp.where(keep, across(rk * rk), 0.0)
        scale2.append(twice_tall(row))
        right = part[j] + nn(twice_wide(g_in[j].astype(BF16)), cross_tall)
        q = q_in[chunk(j), :]
        targets.append(jnp.concatenate([q.astype(F32) * inv_norm(q), right], axis=0))
    both = conjugate(targets, systems, scale2, damp)
    gram = jnp.zeros((DK, DK), F32)
    cross = jnp.zeros((DK, DK), F32)
    for j in range(CHUNKS):
        z, u = both[j][:DK], both[j][DK:]
        z_out[j] = z
        u_out[j] = u
        z_wide, u_wide = wide(z), wide(u)
        left = jnp.concatenate([u_wide, z_wide], axis=0)
        right = jnp.concatenate([z_wide, u_wide], axis=0)
        gram = gram + fold_rows(fold_cols(tn(left, right)))
        cross = cross + fold_cols(tn(g_in[j].astype(BF16), z_wide))
    tot[:FOLDED] = fold_symmetric(gram)
    tot[FOLDED:] = cross


def local_body(tables, need, made, put):
    q_in, k_in, v_in, g_in, z_in, u_in = [need(n) for n in range(6)]
    dq_out, dk_out, dv_out = made
    keep = causal(DK)
    for j in range(CHUNKS):
        q, u = q_in[chunk(j), :], u_in[j]
        rq = inv_norm(q)
        qn = q.astype(F32) * rq
        dq_out[j] = ((u - qn * rowsum(qn * u)) * rq).astype(BF16).astype(F32)
    put(0)
    gram = jnp.zeros((DK, DK), F32)
    cross = jnp.zeros((DK, DK), F32)
    for j in reversed(range(CHUNKS)):
        k, v = k_in[chunk(j), :], v_in[chunk(j), :]
        rk = inv_norm(k)
        row = jnp.where(keep, across(rk), 0.0)
        g = g_in[j].astype(BF16)
        scores = jnp.where(keep, nt(g, v), 0.0)
        u, z = u_in[j], z_in[j]
        u_wide, z_wide = wide(u), wide(z)
        kk = twice_wide(k)
        pair = nt(jnp.concatenate([u_wide, z_wide], axis=0), kk) * twice_tall(row)
        left = jnp.concatenate([scores - pair[:DK], -pair[DK:]], axis=0)
        right = jnp.concatenate([z_wide, u_wide], axis=0)
        dkn = fold_rows(fold_cols(tn(wide(left), right)))
        dkn = dkn + nn(twice_wide(v), tall(cross))
        dk_out[j] = dkn - rk * nn(kk, tall(gram))
        dv_out[j] = rk * nt(kk, wide(cross)) + tn(tall(pair[DK:]), twice_tall(g))
        if j:
            swapped = jnp.concatenate([u_wide, z_wide], axis=0)
            gram = gram + fold_rows(fold_cols(tn(swapped, right)))
            cross = cross + fold_cols(tn(g, z_wide))


def grads_body(seq, tables, need, made, put, dk_buf, dw_buf, out):
    (place,) = tables
    k_in, v_in, dk_part, dv_part = [need(n) for n in range(4)]
    gram_after, cross_after = total_of(need, 4)
    gram_tall, cross_tall, cross_wide = tall(gram_after), tall(cross_after), wide(cross_after)
    for j in range(CHUNKS):
        k, v = k_in[chunk(j), :], v_in[chunk(j), :]
        rk = inv_norm(k)
        kn = k.astype(F32) * rk
        kk = twice_wide(k)
        dkn = dk_part[j] + nn(twice_wide(v), cross_tall) - rk * nn(kk, gram_tall)
        dk = ((dkn - kn * rowsum(kn * dkn)) * rk).astype(BF16)
        dk_buf[chunk(j), :] = dk
        out[j, :DK] = dk.astype(F32)
        dv = dv_part[j] + rk * nt(kk, cross_wide)
        out[j, DK:] = dv.astype(BF16).astype(F32)
    dw_buf[...] = jnp.transpose(tn(dk_buf[...], need(8)[...]))
    rows = made[0].shape[0]
    for step in range(seq):
        start = pl.multiple_of(lax.rem(place[0] + step, seq) * rows, rows)
        made[step][...] = dw_buf[pl.ds(start, rows), :]
        put(step)
    core = place[2]
    for step in range(CHUNKS // 2):
        block = lax.rem(place[1] + step, CHUNKS // 2) * 2
        made[seq + step][: 2 * DK] = out[block + core]
        made[seq + step][2 * DK :] = out[block + 1 - core]
        put(seq + step)


def query_part_body(tables, need, made, put):
    cat = jnp.concatenate([need(0)[h].astype(BF16) for h in range(HEADS)], axis=1)
    made[0][...] = nt(cat, need(1)[...])


def input_grad_body(tables, need, made, put, *sides):
    (place,) = tables
    for step in range(HEADS):
        piece = need(step)
        chips = HEADS // 2
        core = place[2] if step < chips else 1 - place[2]
        head = lax.rem(place[1] + chips - step % chips, chips) * 2 + core
        cols = pl.ds(pl.multiple_of(head * DK, DK), DK)
        for n, side in enumerate(sides):
            side[:, cols] = piece[chunk(n), :].astype(BF16)
    total = need(HEADS)[...]
    for n, side in enumerate(sides):
        total = total + nt(side[...], need(HEADS + 1 + n)[...])
    made[0][...] = total.astype(BF16)


def shift(x, axis, by, wrap):
    size = lax.axis_size(axis)
    pairs = [(i, (i + by) % size) for i in range(size) if wrap or 0 <= i + by < size]
    return lax.ppermute(x, axis, pairs)


def exclusive(total, sign):
    one, two = shift(total, "z", sign, False), shift(total, "z", 2 * sign, False)
    third = total + one + two
    six = shift(third, "z", 6 * sign, False)
    three = shift(third, "z", 3 * sign, False)
    return one, two, three, six


def exchange(x, axis):
    return lax.all_to_all(x, axis, 0, 0)


def gather_plane(low, high):
    y, core = lax.axis_index("y"), lax.axis_index("core")
    rows = low.shape[0]
    prev_low = shift(low, "y", 1, True)
    next_high = shift(high, "y", -1, True)
    prev_high = shift(high, "y", 1, True)
    next_low = shift(low, "y", -1, True)
    far_low = shift(prev_low, "y", 1, True)
    far_high = shift(next_high, "y", -1, True)
    pieces = [(low, 0, 0), (high, 0, rows)]
    pieces += [(shift(low, "core", 1, True), 4, 0), (shift(high, "core", 1, True), 4, rows)]
    near = (
        (prev_low, 1, 0), (next_high, 2, rows), (prev_high, 1, rows), (next_low, 2, 0),
        (far_low, 3, 0), (far_high, 3, rows),
    )
    for piece, slot, start in near:
        pieces.append((piece, slot, start))
        pieces.append((shift(piece, "core", 1, True), slot + 4, start))
    ysize = lax.axis_size("y")
    places = [
        ((y + step) % ysize) * 2 + c for c in (core, 1 - core) for step in (0, -1, 1, 2)
    ] + [y * 2 + core]
    return pieces, jnp.stack(places).astype(jnp.int32)


def on_device(inputs, w_query, w_key, w_value, damping, grad_out):
    mine = inputs[0]
    tokens, width = mine.shape
    plane = CHUNKS * tokens
    blocks = shaped(CHUNKS, tokens, DK)
    brick = shaped(plane, DK, dtype=BF16)
    state = shaped(STATE, DK)
    unit = 2 * plane * DK * DK

    half = shaped(tokens // 2, width)
    low, high = call(prepare_body, [half, half], [mine], 0)
    pieces, where = gather_plane(low, high)
    slots = tuple((slot, start) for _, slot, start in pieces)
    pieces = [p for p, _, _ in pieces]
    (upstream,) = call(upstream_body, [shaped(HEADS, tokens, DK)], [grad_out[0]], 0)
    xb, k, v, first_tot = call(
        functools.partial(project_body, slots),
        [shaped(plane, width, dtype=BF16), brick, brick, state],
        pieces, unit * 28, tables=[where], raw=[w_key, w_value],
        scratch=[pltpu.VMEM((width, 2 * DK), BF16), pltpu.SemaphoreType.DMA((2,))],
    )
    prior = exclusive(first_tot, 1)
    g = exchange(upstream, PLANE)
    q, gram_pre = call(
        states_body, [brick, shaped(CHUNKS, DK, DK)], [k, xb], unit * 10,
        tables=[where], raw=[w_query],
        scratch=[pltpu.VMEM((width, DK), BF16), pltpu.SemaphoreType.DMA((1,))],
    )
    (part,) = call(targets_body, [blocks], [k, v, g], unit * 8)

    z, u, second_tot = call(
        solve_body, [blocks, blocks, state],
        [q, k, gram_pre, part, g, damping, *prior], unit * 40, tables=[where],
    )
    after = exclusive(second_tot, -1)
    dq, dk_part, dv_part = call(local_body, [blocks, blocks, blocks], [q, k, v, g, z, u], unit * 30)
    dq_all = exchange(dq, PLANE)
    (partial,) = call(query_part_body, [shaped(tokens, width)], [dq_all, w_query], unit * 8)

    seq = lax.axis_size("seq")
    ctx = ("z", "y", "core")
    spread = lax.axis_size(ctx)
    rows = width // (seq * spread)
    place = jnp.stack(
        [lax.axis_index("seq"), lax.axis_index("y"), lax.axis_index("core")]
    ).astype(jnp.int32)
    pieces = call(
        functools.partial(grads_body, seq),
        [shaped(width // seq, DK)] * seq + [shaped(4 * tokens, DK)] * (CHUNKS // 2),
        [k, v, dk_part, dv_part, *after, xb], unit * 14, tables=[place],
        scratch=[
            pltpu.VMEM((plane, DK), BF16), pltpu.VMEM((width, DK), F32),
            pltpu.VMEM((CHUNKS, 2 * tokens, DK), F32),
        ],
    )
    dw, dkv = pieces[:seq], pieces[seq:]
    dw = sum((shift(part, "seq", step, True) for step, part in enumerate(dw) if step), dw[0])
    dkv = [shift(p, "y", step, True) if step else p for step, p in enumerate(dkv)]
    dw = exchange(dw.reshape(spread, rows, DK), ctx)
    other = [shift(p, "core", 1, True) for p in dkv]
    dw = dw.reshape(spread // HEADS, HEADS, rows, DK)
    grad_weights = jnp.sum(dw, axis=0).transpose(1, 0, 2).reshape(rows, HEADS * DK)

    mine_of = [(p, slice(0, 2 * tokens)) for p in dkv]
    other_of = [(p, slice(2 * tokens, 4 * tokens)) for p in other]
    (grad_inputs,) = call(
        input_grad_body, [shaped(tokens, width, dtype=BF16)],
        [*mine_of, *other_of, partial, w_key, w_value], unit * 16, tables=[place],
        scratch=[pltpu.VMEM((tokens, width), BF16)] * 2,
    )
    return (grad_inputs[None], grad_weights)


def solution(mesh):
    grid = Mesh(mesh.devices.reshape(4, 8, 4, 2), ("seq", "z", "y", "core"))
    ctx = ("z", "y", "core")
    in_specs = (P("seq", ctx, None), P(), P(), P(), P(), P("seq", ctx, None))
    out_specs = (P("seq", ctx, None), P(("seq",) + ctx, None))

    return jax.shard_map(on_device, mesh=grid, in_specs=in_specs, out_specs=out_specs, check_vma=False)
```

```python
import functools

import jax
import jax.numpy as jnp
from jax import lax
from jax.experimental import pallas as pl
from jax.experimental.pallas import tpu as pltpu
from jax.sharding import Mesh, PartitionSpec as P


ITERS = 2
EPSILON = 1e-06
F32 = jnp.float32
BF16 = jnp.bfloat16
HEADS = 8
DK = 128
CHUNKS = 8
PLANE = ("y", "core")


def halves(x):
    hi = x.astype(BF16)
    return hi, (x - hi.astype(F32)).astype(BF16)


def nn(a, b):
    return lax.dot_general(a, b, (((1,), (0,)), ((), ())), preferred_element_type=F32)


def nt(a, b):
    return lax.dot_general(a, b, (((1,), (1,)), ((), ())), preferred_element_type=F32)


def tn(a, b):
    return lax.dot_general(a, b, (((0,), (0,)), ((), ())), preferred_element_type=F32)


def wide(x):
    return jnp.concatenate(halves(x), axis=1)


def tall(x):
    return jnp.concatenate(halves(x), axis=0)


def twice_wide(b):
    return jnp.concatenate([b, b], axis=1)


def twice_tall(b):
    return jnp.concatenate([b, b], axis=0)


def fold_cols(m):
    half = m.shape[1] // 2
    return m[:, :half] + m[:, half:]


def fold_rows(m):
    half = m.shape[0] // 2
    return m[:half] + m[half:]


def rowsum(x):
    return jnp.sum(x, axis=-1, keepdims=True)


def causal(size):
    rows = lax.broadcasted_iota(jnp.int32, (size, size), 0)
    cols = lax.broadcasted_iota(jnp.int32, (size, size), 1)
    return rows >= cols


def inv_norm(block):
    wide_block = block.astype(F32)
    return lax.rsqrt(rowsum(wide_block * wide_block) + EPSILON)


def across(column):
    size = column.shape[0]
    return jnp.transpose(jnp.broadcast_to(column, (size, size)))


def system(key, gram):
    turned = jnp.transpose(key)
    hi, lo = halves(gram)
    upper = jnp.concatenate([turned, hi, lo], axis=1)
    lower = jnp.concatenate([turned, hi, jnp.zeros_like(lo)], axis=1)
    return jnp.concatenate([upper, lower], axis=0), twice_tall(key)


def apply_all(vectors, systems, scale2, damp):
    firsts = [nn(wide(p), s[0]) for p, s in zip(vectors, systems)]
    inner = [wide(f[:, :DK] * m) for f, m in zip(firsts, scale2)]
    return [
        nn(i, s[1]) + (f[:, DK : 2 * DK] + f[:, 2 * DK :]) + damp * p
        for i, s, f, p in zip(inner, systems, firsts, vectors)
    ]


def conjugate(targets, systems, scale2, damp):
    residual = list(targets)
    direction = list(targets)
    norm_now = [rowsum(r * r) for r in residual]
    solution = None
    for sweep in range(ITERS):
        image = apply_all(direction, systems, scale2, damp)
        step = [n / (rowsum(p * w) + EPSILON) for n, p, w in zip(norm_now, direction, image)]
        moved = [a * p for a, p in zip(step, direction)]
        solution = moved if solution is None else [x + m for x, m in zip(solution, moved)]
        if sweep + 1 < ITERS:
            residual = [r - a * w for r, a, w in zip(residual, step, image)]
            norm_next = [rowsum(r * r) for r in residual]
            direction = [
                r + n / (o + EPSILON) * p
                for r, n, o, p in zip(residual, norm_next, norm_now, direction)
            ]
            norm_now = norm_next
    return solution


def staged(body, counts, parts, tables, *refs):
    n_in, n_out = counts
    sources, refs = refs[:n_in], refs[n_in:]
    targets, refs = refs[:n_out], refs[n_out:]
    held, refs = refs[:n_in], refs[n_in:]
    made, (in_sems, out_sems, *rest) = refs[:n_out], refs[n_out:]
    loads = [
        pltpu.make_async_copy(s.at[part] if part else s, h, in_sems.at[n])
        for n, (s, h, part) in enumerate(zip(sources, held, parts))
    ]
    stores = [
        pltpu.make_async_copy(m, t, out_sems.at[n]) for n, (m, t) in enumerate(zip(made, targets))
    ]
    for load in loads:
        load.start()
    arrived, sent = set(), set()

    def need(n):
        if n not in arrived:
            arrived.add(n)
            loads[n].wait()
        return held[n]

    def put(n):
        sent.add(n)
        stores[n].start()

    body(tables, need, made, put, *rest)
    for n in range(n_in):
        need(n)
    for n in range(n_out):
        if n not in sent:
            put(n)
    for store in stores:
        store.wait()


def shaped(*dims, dtype=F32):
    return jax.ShapeDtypeStruct(dims, dtype)


ANYWHERE = pl.BlockSpec(memory_space=pl.ANY)


def call(body, outs, args, flops, tables=(), raw=(), scratch=()):
    parts = [a[1] if isinstance(a, tuple) else None for a in args]
    args = [a[0] if isinstance(a, tuple) else a for a in args]
    held = [
        (p.stop - p.start, *a.shape[1:]) if p else a.shape for a, p in zip(args, parts)
    ]

    def kernel(*refs):
        t, r = len(tables), len(raw)
        operands = refs[t + r :]
        staged(
            functools.partial(body, *refs[t : t + r]), (len(args), len(outs)), parts, refs[:t],
            *operands,
        )

    moved = sum(a.size * a.dtype.itemsize for a in args) + sum(
        o.size * jnp.dtype(o.dtype).itemsize for o in outs
    )
    return pl.pallas_call(
        kernel,
        out_shape=tuple(outs),
        in_specs=[pl.BlockSpec(memory_space=pltpu.SMEM)] * len(tables)
        + [ANYWHERE] * (len(raw) + len(args)),
        out_specs=tuple([ANYWHERE] * len(outs)),
        scratch_shapes=[pltpu.VMEM(h, a.dtype) for h, a in zip(held, args)]
        + [pltpu.VMEM(o.shape, o.dtype) for o in outs]
        + [pltpu.SemaphoreType.DMA((len(args),)), pltpu.SemaphoreType.DMA((len(outs),))]
        + list(scratch),
        compiler_params=pltpu.CompilerParams(vmem_limit_bytes=60 << 20),
        cost_estimate=pl.CostEstimate(flops=flops, bytes_accessed=moved, transcendentals=0),
    )(*tables, *raw, *args)


def fold_symmetric(m):
    half = m.shape[0] // 2
    rows = lax.broadcasted_iota(jnp.int32, (half, 2 * half), 0)
    cols = lax.broadcasted_iota(jnp.int32, (half, 2 * half), 1)
    low = pltpu.roll(m[half:], half, 1)
    diagonal = jnp.sum(jnp.where(rows == cols, low, 0.0), axis=0, keepdims=True)
    mixed = jnp.where((cols > rows) & (cols < half), low, m[:half])
    return jnp.concatenate([mixed, jnp.broadcast_to(diagonal, (8, 2 * half))], axis=0)


def unfold_symmetric(f):
    half = f.shape[1] // 2
    rows = lax.broadcasted_iota(jnp.int32, (half, 2 * half), 0)
    cols = lax.broadcasted_iota(jnp.int32, (half, 2 * half), 1)
    mixed, diagonal = f[:half], f[half : half + 1]
    turned = jnp.transpose(jnp.concatenate([mixed, jnp.zeros_like(mixed)], axis=0))
    top = jnp.where((cols > rows) & (cols < half), turned[:half], mixed)
    last = jnp.where(cols > rows, mixed, jnp.where(cols < rows, turned[:half], diagonal))
    low = jnp.where(cols < half, turned[half:], pltpu.roll(last, half, 1))
    return jnp.concatenate([top, low], axis=0)


FOLDED = DK // 2 + 8
STATE = FOLDED + DK


def total_of(need, first):
    near = [need(first + n) for n in range(4)]
    state = (near[0][...] + near[1][...]) + (near[2][...] + near[3][...])
    return unfold_symmetric(state[:FOLDED]), state[FOLDED:]


def chunk(j):
    return slice(j * DK, (j + 1) * DK)


def upstream_body(tables, need, made, put):
    for h in range(HEADS):
        made[0][h] = need(0)[:, chunk(h)].astype(F32)


def project_body(slots, wk_hbm, wv_hbm, tables, need, made, put, w_buf, w_sem):
    (where,) = tables
    xb, k_out, v_out, tot = made
    cols = pl.ds(pl.multiple_of(where[len(where) - 1] * DK, DK), DK)
    weights = [
        pltpu.make_async_copy(w.at[:, cols], w_buf.at[:, chunk(n)], w_sem.at[n])
        for n, w in enumerate((wk_hbm, wv_hbm))
    ]
    for copy in weights:
        copy.start()
    for n, (slot, start) in enumerate(slots):
        piece = need(n)
        row = pl.multiple_of(where[slot] * DK + start, DK // 2)
        xb[pl.ds(row, piece.shape[0]), :] = piece[...].astype(BF16)
    put(0)
    for copy in weights:
        copy.wait()
    both = nn(xb[...], w_buf[...]).astype(BF16)
    k, v = both[:, :DK], both[:, DK:]
    k_out[...] = k
    v_out[...] = v
    put(1)
    put(2)
    rk = inv_norm(k)
    kn = k.astype(F32) * rk
    tot[:FOLDED] = fold_symmetric(fold_cols(tn(k, wide(kn * rk))))
    tot[FOLDED:] = fold_cols(tn(v, wide(kn)))


def states_body(wq_hbm, tables, need, made, put, w_buf, w_sem):
    (where,) = tables
    q_out, gram_out = made
    cols = pl.ds(pl.multiple_of(where[len(where) - 1] * DK, DK), DK)
    weight = pltpu.make_async_copy(wq_hbm.at[:, cols], w_buf, w_sem.at[0])
    weight.start()
    k_in = need(0)
    gram = jnp.zeros((DK, DK), F32)
    for j in range(CHUNKS):
        gram_out[j] = gram
        if j + 1 < CHUNKS:
            k = k_in[chunk(j), :]
            rk = inv_norm(k)
            gram = gram + fold_cols(tn(k, wide(k.astype(F32) * (rk * rk))))
    put(1)
    weight.wait()
    q_out[...] = nn(need(1)[...], w_buf[...]).astype(BF16)


def targets_body(tables, need, made, put):
    k_in, v_in, g_in = need(0), need(1), need(2)
    keep = causal(DK)
    cross = jnp.zeros((DK, DK), F32)
    for j in range(CHUNKS):
        k, v, g = k_in[chunk(j), :], v_in[chunk(j), :], g_in[j].astype(BF16)
        rk = inv_norm(k)
        scores = nt(g, v) * jnp.where(keep, across(rk), 0.0)
        made[0][j] = nn(twice_wide(g), tall(cross)) + nn(wide(scores), twice_tall(k))
        if j + 1 < CHUNKS:
            cross = cross + fold_cols(tn(v, wide(k.astype(F32) * rk)))


def solve_body(tables, need, made, put):
    (where,) = tables
    q_in, k_in, gram_in, part, g_in, damp_in = [need(n) for n in range(6)]
    gram_prior, cross_prior = total_of(need, 6)
    z_out, u_out, tot = made
    damp = damp_in[pl.ds(where[len(where) - 1], 1), :]
    keep = causal(DK)
    keys = [k_in[chunk(j), :] for j in range(CHUNKS)]
    systems = [system(k, gram_in[j] + gram_prior) for j, k in enumerate(keys)]
    cross_tall = tall(cross_prior)
    scale2, targets = [], []
    for j, k in enumerate(keys):
        rk = inv_norm(k)
        row = jnp.where(keep, across(rk * rk), 0.0)
        scale2.append(twice_tall(row))
        right = part[j] + nn(twice_wide(g_in[j].astype(BF16)), cross_tall)
        q = q_in[chunk(j), :]
        targets.append(jnp.concatenate([q.astype(F32) * inv_norm(q), right], axis=0))
    both = conjugate(targets, systems, scale2, damp)
    gram = jnp.zeros((DK, DK), F32)
    cross = jnp.zeros((DK, DK), F32)
    for j in range(CHUNKS):
        z, u = both[j][:DK], both[j][DK:]
        z_out[j] = z
        u_out[j] = u
        z_wide, u_wide = wide(z), wide(u)
        left = jnp.concatenate([u_wide, z_wide], axis=0)
        right = jnp.concatenate([z_wide, u_wide], axis=0)
        gram = gram + fold_rows(fold_cols(tn(left, right)))
        cross = cross + fold_cols(tn(g_in[j].astype(BF16), z_wide))
    tot[:FOLDED] = fold_symmetric(gram)
    tot[FOLDED:] = cross


def local_body(tables, need, made, put):
    q_in, k_in, v_in, g_in, z_in, u_in = [need(n) for n in range(6)]
    dq_out, dk_out, dv_out = made
    keep = causal(DK)
    for j in range(CHUNKS):
        q, u = q_in[chunk(j), :], u_in[j]
        rq = inv_norm(q)
        qn = q.astype(F32) * rq
        dq_out[j] = ((u - qn * rowsum(qn * u)) * rq).astype(BF16).astype(F32)
    put(0)
    gram = jnp.zeros((DK, DK), F32)
    cross = jnp.zeros((DK, DK), F32)
    for j in reversed(range(CHUNKS)):
        k, v = k_in[chunk(j), :], v_in[chunk(j), :]
        rk = inv_norm(k)
        row = jnp.where(keep, across(rk), 0.0)
        g = g_in[j].astype(BF16)
        scores = jnp.where(keep, nt(g, v), 0.0)
        u, z = u_in[j], z_in[j]
        u_wide, z_wide = wide(u), wide(z)
        kk = twice_wide(k)
        pair = nt(jnp.concatenate([u_wide, z_wide], axis=0), kk) * twice_tall(row)
        left = jnp.concatenate([scores - pair[:DK], -pair[DK:]], axis=0)
        right = jnp.concatenate([z_wide, u_wide], axis=0)
        dkn = fold_rows(fold_cols(tn(wide(left), right)))
        dkn = dkn + nn(twice_wide(v), tall(cross))
        dk_out[j] = dkn - rk * nn(kk, tall(gram))
        dv_out[j] = rk * nt(kk, wide(cross)) + tn(tall(pair[DK:]), twice_tall(g))
        if j:
            swapped = jnp.concatenate([u_wide, z_wide], axis=0)
            gram = gram + fold_rows(fold_cols(tn(swapped, right)))
            cross = cross + fold_cols(tn(g, z_wide))


def grads_body(seq, tables, need, made, put, dk_buf, dw_buf, out):
    (place,) = tables
    k_in, v_in, dk_part, dv_part = [need(n) for n in range(4)]
    gram_after, cross_after = total_of(need, 4)
    gram_tall, cross_tall, cross_wide = tall(gram_after), tall(cross_after), wide(cross_after)
    for j in range(CHUNKS):
        k, v = k_in[chunk(j), :], v_in[chunk(j), :]
        rk = inv_norm(k)
        kn = k.astype(F32) * rk
        kk = twice_wide(k)
        dkn = dk_part[j] + nn(twice_wide(v), cross_tall) - rk * nn(kk, gram_tall)
        dk = ((dkn - kn * rowsum(kn * dkn)) * rk).astype(BF16)
        dk_buf[chunk(j), :] = dk
        out[j, :DK] = dk.astype(F32)
        dv = dv_part[j] + rk * nt(kk, cross_wide)
        out[j, DK:] = dv.astype(BF16).astype(F32)
    dw_buf[...] = jnp.transpose(tn(dk_buf[...], need(8)[...]))
    rows = made[0].shape[0]
    for step in range(seq):
        start = pl.multiple_of(lax.rem(place[0] + step, seq) * rows, rows)
        made[step][...] = dw_buf[pl.ds(start, rows), :]
        put(step)
    core = place[2]
    for step in range(CHUNKS // 2):
        block = lax.rem(place[1] + step, CHUNKS // 2) * 2
        made[seq + step][: 2 * DK] = out[block + core]
        made[seq + step][2 * DK :] = out[block + 1 - core]
        put(seq + step)


def query_part_body(tables, need, made, put):
    cat = jnp.concatenate([need(0)[h].astype(BF16) for h in range(HEADS)], axis=1)
    made[0][...] = nt(cat, need(1)[...])


def input_grad_body(tables, need, made, put, *sides):
    (place,) = tables
    for step in range(HEADS):
        piece = need(step)
        chips = HEADS // 2
        core = place[2] if step < chips else 1 - place[2]
        head = lax.rem(place[1] + chips - step % chips, chips) * 2 + core
        cols = pl.ds(pl.multiple_of(head * DK, DK), DK)
        for n, side in enumerate(sides):
            side[:, cols] = piece[chunk(n), :].astype(BF16)
    total = need(HEADS)[...]
    for n, side in enumerate(sides):
        total = total + nt(side[...], need(HEADS + 1 + n)[...])
    made[0][...] = total.astype(BF16)


def shift(x, axis, by, wrap):
    size = lax.axis_size(axis)
    pairs = [(i, (i + by) % size) for i in range(size) if wrap or 0 <= i + by < size]
    return lax.ppermute(x, axis, pairs)


def exclusive(total, sign):
    one, two = shift(total, "z", sign, False), shift(total, "z", 2 * sign, False)
    third = total + one + two
    six = shift(third, "z", 6 * sign, False)
    three = shift(third, "z", 3 * sign, False)
    return one, two, three, six


def exchange(x, axis):
    return lax.all_to_all(x, axis, 0, 0)


def gather_plane(low, high):
    y, core = lax.axis_index("y"), lax.axis_index("core")
    rows = low.shape[0]
    prev_low = shift(low, "y", 1, True)
    next_high = shift(high, "y", -1, True)
    prev_high = shift(high, "y", 1, True)
    next_low = shift(low, "y", -1, True)
    far_low = shift(prev_low, "y", 1, True)
    far_high = shift(next_high, "y", -1, True)
    pieces = [(low, 0, 0), (high, 0, rows)]
    pieces += [(shift(low, "core", 1, True), 4, 0), (shift(high, "core", 1, True), 4, rows)]
    near = (
        (prev_low, 1, 0), (next_high, 2, rows), (prev_high, 1, rows), (next_low, 2, 0),
        (far_low, 3, 0), (far_high, 3, rows),
    )
    for piece, slot, start in near:
        pieces.append((piece, slot, start))
        pieces.append((shift(piece, "core", 1, True), slot + 4, start))
    ysize = lax.axis_size("y")
    places = [
        ((y + step) % ysize) * 2 + c for c in (core, 1 - core) for step in (0, -1, 1, 2)
    ] + [y * 2 + core]
    return pieces, jnp.stack(places).astype(jnp.int32)


def on_device(inputs, w_query, w_key, w_value, damping, grad_out):
    mine = inputs[0]
    tokens, width = mine.shape
    plane = CHUNKS * tokens
    blocks = shaped(CHUNKS, tokens, DK)
    brick = shaped(plane, DK, dtype=BF16)
    state = shaped(STATE, DK)
    unit = 2 * plane * DK * DK

    low, high = mine[: tokens // 2].astype(F32), mine[tokens // 2 :].astype(F32)
    pieces, where = gather_plane(low, high)
    slots = tuple((slot, start) for _, slot, start in pieces)
    pieces = [p for p, _, _ in pieces]
    (upstream,) = call(upstream_body, [shaped(HEADS, tokens, DK)], [grad_out[0]], 0)
    xb, k, v, first_tot = call(
        functools.partial(project_body, slots),
        [shaped(plane, width, dtype=BF16), brick, brick, state],
        pieces, unit * 28, tables=[where], raw=[w_key, w_value],
        scratch=[pltpu.VMEM((width, 2 * DK), BF16), pltpu.SemaphoreType.DMA((2,))],
    )
    prior = exclusive(first_tot, 1)
    g = exchange(upstream, PLANE)
    q, gram_pre = call(
        states_body, [brick, shaped(CHUNKS, DK, DK)], [k, xb], unit * 10,
        tables=[where], raw=[w_query],
        scratch=[pltpu.VMEM((width, DK), BF16), pltpu.SemaphoreType.DMA((1,))],
    )
    (part,) = call(targets_body, [blocks], [k, v, g], unit * 8)

    z, u, second_tot = call(
        solve_body, [blocks, blocks, state],
        [q, k, gram_pre, part, g, damping, *prior], unit * 40, tables=[where],
    )
    after = exclusive(second_tot, -1)
    dq, dk_part, dv_part = call(local_body, [blocks, blocks, blocks], [q, k, v, g, z, u], unit * 30)
    dq_all = exchange(dq, PLANE)
    (partial,) = call(query_part_body, [shaped(tokens, width)], [dq_all, w_query], unit * 8)

    seq = lax.axis_size("seq")
    ctx = ("z", "y", "core")
    spread = lax.axis_size(ctx)
    rows = width // (seq * spread)
    place = jnp.stack(
        [lax.axis_index("seq"), lax.axis_index("y"), lax.axis_index("core")]
    ).astype(jnp.int32)
    pieces = call(
        functools.partial(grads_body, seq),
        [shaped(width // seq, DK)] * seq + [shaped(4 * tokens, DK)] * (CHUNKS // 2),
        [k, v, dk_part, dv_part, *after, xb], unit * 14, tables=[place],
        scratch=[
            pltpu.VMEM((plane, DK), BF16), pltpu.VMEM((width, DK), F32),
            pltpu.VMEM((CHUNKS, 2 * tokens, DK), F32),
        ],
    )
    dw, dkv = pieces[:seq], pieces[seq:]
    dw = sum((shift(part, "seq", step, True) for step, part in enumerate(dw) if step), dw[0])
    dkv = [shift(p, "y", step, True) if step else p for step, p in enumerate(dkv)]
    dw = exchange(dw.reshape(spread, rows, DK), ctx)
    other = [shift(p, "core", 1, True) for p in dkv]
    dw = dw.reshape(spread // HEADS, HEADS, rows, DK)
    grad_weights = jnp.sum(dw, axis=0).transpose(1, 0, 2).reshape(rows, HEADS * DK)

    mine_of = [(p, slice(0, 2 * tokens)) for p in dkv]
    other_of = [(p, slice(2 * tokens, 4 * tokens)) for p in other]
    (grad_inputs,) = call(
        input_grad_body, [shaped(tokens, width, dtype=BF16)],
        [*mine_of, *other_of, partial, w_key, w_value], unit * 16, tables=[place],
        scratch=[pltpu.VMEM((tokens, width), BF16)] * 2,
    )
    return (grad_inputs[None], grad_weights)


def solution(mesh):
    grid = Mesh(mesh.devices.reshape(4, 8, 4, 2), ("seq", "z", "y", "core"))
    ctx = ("z", "y", "core")
    in_specs = (P("seq", ctx, None), P(), P(), P(), P(), P("seq", ctx, None))
    out_specs = (P("seq", ctx, None), P(("seq",) + ctx, None))

    return jax.shard_map(on_device, mesh=grid, in_specs=in_specs, out_specs=out_specs, check_vma=False)
```
